512 devices in a mesh: gx: 32 (over x, z), gy: 16 (over y, core).
Axes of the slice: x: 4, y: 8, z: 8, core: 2. Of those that a mesh axis runs over, the one named last changes fastest.
Arguments:
- labels: int32 [192, 128, 256], P('gx', 'gy'), may hold values from 0 to 7
- permittivity_real: float32 [8], replicated, may hold values from 1 to 2.5
- permittivity_imag: float32 [8], replicated, may hold values from 0 to 0.5
- angles: float32 [360], replicated, may hold values from -3.140625 to 3.140625
- angle_pick: int32 [4], replicated, may hold values from 0 to 359
Outputs:
- scattered_field: float32 [2, 4, 192, 128, 256], P(None, None, 'gx', 'gy')
The draws below stay inside these ranges and needn't reach their ends.
All inputs are finite; a program needn't handle non-finite values.
Results may differ from the reference program's by a relative error of at most 0.000054.
Values sent between devices are 32-bit elements; how exact they have to be, the bound alone decides.
No kernel may reach another device: no remote copies, remote signals or barrier semaphores. Data moves between devices by JAX's collectives and lax.ppermute only.
A program may use at most 64 MiB of HBM per device.

```python
import jax
import jax.numpy as jnp
from jax import lax

NZ = 256
COLS = 4
NANG = 360
MAT = 8
FINE_SWEEPS = 2
COARSE_SWEEPS = 4
NX = 192
NY = 128


def set_ends(result, stream_key, least, top_value):
    shape = result.shape
    spot = [jax.random.randint(jax.random.fold_in(stream_key, axis), (), 0, shape[axis]) for axis in range(len(shape))]
    result = result.at[tuple(spot)].set(least)
    longest = shape.index(max(shape))
    spot[longest] = (spot[longest] + 1) % shape[longest]
    return result.at[tuple(spot)].set(top_value)


def setup_inputs(seed: int = 0) -> dict:
    keys = jax.random.split(jax.random.key(seed), 6)
    return {
        "labels": set_ends(jax.random.randint(keys[0], (NX, NY, NZ), 0, MAT), jax.random.fold_in(keys[0], 1), 0, MAT - 1).astype(jnp.int32),
        "permittivity_real": jnp.clip(jax.random.uniform(keys[1], (MAT,), jnp.float32, 1.0, 2.5), 1.0, 2.5),
        "permittivity_imag": jnp.clip(jax.random.uniform(keys[2], (MAT,), jnp.float32, 0.0, 0.5), 0.0, 0.5),
        "angles": jnp.clip(jax.random.uniform(keys[3], (NANG,), jnp.float32, -3.140625, 3.140625), -3.140625, 3.140625),
        "angle_pick": set_ends(jax.random.randint(keys[4], (COLS,), 0, NANG), jax.random.fold_in(keys[4], 1), 0, NANG - 1).astype(jnp.int32),
    }


WEIGHTS = (128.0, -14.0, -3.0, -1.0)
DAMPING = 0.8
WAVE_SQUARED = 0.1
SHIFT_IMAG = 0.5
SOURCE_GAIN = 4.0

def stencil(padded):
    extent_x = padded.shape[-3] - 2
    extent_y = padded.shape[-2] - 2
    extent_z = padded.shape[-1] - 2
    summed = jnp.zeros(padded.shape[:-3] + (extent_x, extent_y, extent_z), padded.dtype)
    for offset_x in (0, 1, 2):
        for offset_y in (0, 1, 2):
            for offset_z in (0, 1, 2):
                weight = WEIGHTS[abs(offset_x - 1) + abs(offset_y - 1) + abs(offset_z - 1)]
                summed = summed + weight * padded[..., offset_x:offset_x + extent_x, offset_y:offset_y + extent_y, offset_z:offset_z + extent_z]
    return summed / 30.0

def complex_product(coefs, values):
    real_out = coefs[0] * values[0] - coefs[1] * values[1]
    imag_out = coefs[0] * values[1] + coefs[1] * values[0]
    return jnp.stack([real_out, imag_out])

def apply_operator(iterate, padded, medium, factor):
    laplace = stencil(padded) * factor
    return laplace - complex_product(medium, iterate)

def inverse_diagonal(medium, centre_weight):
    diag_real = centre_weight - medium[0]
    diag_imag = -medium[1]
    modulus = diag_real * diag_real + diag_imag * diag_imag
    return jnp.stack([diag_real / modulus, -diag_imag / modulus])

def pad_all(values):
    return jnp.pad(values, ((0, 0), (0, 0), (1, 1), (1, 1), (1, 1)))

def restrict_axis(values, along):
    planes = (values.shape[along] - 1) // 2
    low_side = lax.slice_in_dim(values, 0, 2 * planes, 2, along)
    centre = lax.slice_in_dim(values, 1, 2 * planes, 2, along)
    high_side = lax.slice_in_dim(values, 2, 2 * planes + 1, 2, along)
    return (low_side + 2.0 * centre + high_side) * 0.25

def prolong_axis(values, along):
    planes = values.shape[along] - 1
    lower_part = lax.slice_in_dim(values, 0, planes, 1, along)
    upper_part = lax.slice_in_dim(values, 1, planes + 1, 1, along)
    even_rows = (lower_part + upper_part) * 0.5
    stacked = jnp.stack([even_rows, upper_part], axis=along + 1)
    new_shape = list(values.shape)
    new_shape[along] = 2 * planes
    return stacked.reshape(new_shape)

def reference(labels, permittivity_real, permittivity_imag, angles, angle_pick):
    eps_real = permittivity_real[labels]
    eps_imag = permittivity_imag[labels]
    medium = WAVE_SQUARED * jnp.stack([eps_real + SHIFT_IMAG * eps_imag, eps_imag - SHIFT_IMAG * eps_real])
    incidence = angles[angle_pick]
    wavenumber = jnp.sqrt(WAVE_SQUARED)
    pos_x = jnp.arange(NX).astype(jnp.float32)
    pos_y = jnp.arange(NY).astype(jnp.float32)
    phases = wavenumber * (jnp.cos(incidence)[:, None, None] * pos_x[None, :, None] + jnp.sin(incidence)[:, None, None] * pos_y[None, None, :])
    phases = phases[..., None]
    contrast = eps_real - 1.0
    source = SOURCE_GAIN * jnp.stack([contrast * jnp.cos(phases) - eps_imag * jnp.sin(phases), contrast * jnp.sin(phases) + eps_imag * jnp.cos(phases)])
    inverse = inverse_diagonal(medium, 128.0 / 30.0)
    iterate = DAMPING * complex_product(inverse, source)
    for sweep_index in range(FINE_SWEEPS - 1):
        residual = source - apply_operator(iterate, pad_all(iterate), medium, 1.0)
        iterate = iterate + DAMPING * complex_product(inverse, residual)
    residual = source - apply_operator(iterate, pad_all(iterate), medium, 1.0)
    extended = jnp.pad(residual, ((0, 0), (0, 0), (0, 1), (0, 1), (0, 1)))
    coarse_rhs = restrict_axis(restrict_axis(restrict_axis(extended, 2), 3), 4)
    coarse_medium = medium[:, 1::2, 1::2, 1::2]
    coarse_inverse = inverse_diagonal(coarse_medium, 128.0 / 120.0)
    correction = DAMPING * complex_product(coarse_inverse, coarse_rhs)
    for sweep_index in range(COARSE_SWEEPS - 1):
        coarse_res = coarse_rhs - apply_operator(correction, pad_all(correction), coarse_medium, 0.25)
        correction = correction + DAMPING * complex_product(coarse_inverse, coarse_res)
    extended = jnp.pad(correction, ((0, 0), (0, 0), (1, 0), (1, 0), (1, 0)))
    fine_correction = prolong_axis(prolong_axis(prolong_axis(extended, 2), 3), 4)
    return iterate + fine_correction
```

```python
import jax
import jax.numpy as jnp
from jax import lax
from jax.experimental import pallas as pl
from jax.experimental.pallas import tpu as pltpu
from jax.sharding import PartitionSpec as P

NANG = 360
MAT = 8
DAMPING = 0.8
WAVE_SQUARED = 0.1
SHIFT_IMAG = 0.5
SOURCE_GAIN = 4.0

OWN_X = 6
OWN_Y = 8
PX = 16
PY = 35
LOW = 10
CX, CY = 5, 15
NI, NJ = 10, 11
LANES = 128
F32 = jnp.float32
OUTSIDE = 8


def lane_iota():
    return lax.broadcasted_iota(jnp.int32, (8, LANES), 1)


def sign_rows():
    rows = lax.broadcasted_iota(jnp.int32, (8, LANES), 0)
    return jnp.where(rows < 4, -1.0, 1.0).astype(F32)


def up(values, first):
    return jnp.where(first, 0.0, pltpu.roll(values, 1, 1))


def down(values, last):
    return jnp.where(last, 0.0, pltpu.roll(values, LANES - 1, 1))


def turned(values):
    return pltpu.roll(values, 4, 0)


def row_of(ref, y, x):
    return jnp.broadcast_to(ref[y, pl.ds(x, 1), :], (8, LANES))


def edge_face(values, near):
    edge = 3.0 * values + near
    face = 3.0 * edge + 5.0 * values
    return edge, face


def region_kernel(
    sc, mid, low, high, tab, ex, ey,
    c1_out, ck_out, send_out, it2_out, inv_out,
    ge_r, go_r, ge_i, go_i, ie_r, io_r, ie_i, io_i, sa_r, sa_i, kr_t, ki_t,
    it1, pp, qq, va, vb, sy,
):
    core = sc[0]
    x0 = sc[1]
    y0 = sc[2]
    nx = sc[3]
    ny = sc[4]
    lanes = lane_iota()
    first = lanes == 0
    last = lanes == LANES - 1
    sgn = sign_rows()

    rows = lax.broadcasted_iota(jnp.int32, (2 * LANES, 2 * LANES), 0)
    cols = lax.broadcasted_iota(jnp.int32, (2 * LANES, 2 * LANES), 1)
    source_row = jnp.where(cols < LANES, 2 * cols, 2 * (cols - LANES) + 1)
    perm = jnp.where(rows == source_row, 1.0, 0.0).astype(jnp.bfloat16)

    def tables(labels, first_row, count):
        flat = labels[...].reshape(count * PX, 2 * LANES).astype(F32).astype(jnp.bfloat16)
        apart = jnp.dot(flat, perm, preferred_element_type=F32)
        for k in range(count):
            y = first_row + k
            y_in = jnp.logical_and(y0 + y >= 0, y0 + y < ny)
            for h in range(2):
                xs = x0 + 8 * h + lax.broadcasted_iota(jnp.int32, (8, LANES), 0)
                valid = jnp.logical_and(jnp.logical_and(xs >= 0, xs < nx), y_in)
                part = apart[k * PX + 8 * h : k * PX + 8 * h + 8]
                even = jnp.where(valid, part[:, :LANES].astype(jnp.int32), OUTSIDE)
                odd = jnp.where(valid, part[:, LANES:].astype(jnp.int32), OUTSIDE)

                def pick(row, index):
                    table = jnp.broadcast_to(tab[row : row + 1, :], (8, LANES))
                    return jnp.take_along_axis(
                        table, index, axis=1, mode="promise_in_bounds"
                    )

                at = (y, pl.ds(8 * h, 8), slice(None))
                ge_r[at] = pick(0, even)
                go_r[at] = pick(0, odd)
                ge_i[at] = pick(1, even)
                go_i[at] = pick(1, odd)
                ie_r[at] = pick(2, even)
                io_r[at] = pick(2, odd)
                ie_i[at] = pick(3, even)
                io_i[at] = pick(3, odd)
                for row, out in ((4, sa_r), (5, sa_i)):
                    se = pick(row, even)
                    so = pick(row, odd)
                    out[at] = se + down(se, last) + 2.0 * so
                kr_t[at] = pick(6, odd)
                ki_t[at] = pick(7, odd)

    tables(low, 0, LOW)
    tables(mid, LOW, 16)
    tables(high, LOW + 16, PY - LOW - 16)

    def first_stage(y, carry):
        wave = ey[y, 0]
        wave_t = ey[y, 1]
        edges, faces, centres = [[], []], [[], []], [[], []]
        for x in range(PX):
            c = ex[x, 0]
            s = ex[x, 1]
            e = c * wave + s * wave_t
            e_t = c * wave_t - s * wave
            even = row_of(ge_r, y, x) * e + row_of(ge_i, y, x) * e_t
            odd = row_of(go_r, y, x) * e + row_of(go_i, y, x) * e_t
            sy[y * PX + x] = row_of(sa_r, y, x) * e + row_of(sa_i, y, x) * e_t
            at = (y * PX + x) * 2
            it1[at] = even
            it1[at + 1] = odd
            near_e = odd + up(odd, first)
            near_o = even + down(even, last)
            for h, (v, near) in enumerate(((even, near_e), (odd, near_o))):
                edge, face = edge_face(v, near)
                edges[h].append(edge)
                faces[h].append(face)
                centres[h].append(14.0 * near)
        for x in range(PX):
            at = (y * PX + x) * 2
            for h in range(2):
                p = centres[h][x]
                q = faces[h][x]
                if x > 0 and x < PX - 1:
                    p = p + (faces[h][x - 1] + faces[h][x + 1])
                    q = q + (edges[h][x - 1] + edges[h][x + 1])
                elif x > 0:
                    p = p + faces[h][x - 1]
                    q = q + edges[h][x - 1]
                else:
                    p = p + faces[h][x + 1]
                    q = q + edges[h][x + 1]
                pp[at + h] = p
                qq[at + h] = q
        return carry

    lax.fori_loop(0, PY, first_stage, 0)

    def update(y, x, h, ir, ii):
        at = (y * PX + x) * 2 + h
        row = PX * 2
        n = pp[at] + (qq[at - row] + qq[at + row])
        return row_of(ir, y, x) * n + (row_of(ii, y, x) * sgn) * turned(n)

    def second_stage(y, carry):
        for x in range(1, 14):
            at = (y * PX + x) * 2
            we = 0.4 * it1[at] + update(y, x, 0, ie_r, ie_i)
            wo = 0.4 * it1[at + 1] + update(y, x, 1, io_r, io_i)
            p = we + down(we, last)
            after = jnp.where(last, -wo, pltpu.roll(wo, LANES - 1, 1))
            va[y * PX + x] = p + 2.0 * wo
            vb[y * PX + x] = (up(wo, first) + after) + 2.0 * (p + wo)
        return carry

    lax.fori_loop(1, PY - 1, second_stage, 0)

    def third_stage(j, carry):
        my = jnp.where(y0 + 4 + 2 * j == ny, 1.0, 2.0).astype(F32)
        base = (2 + 2 * j) * PX
        gs, hs = {}, {}
        for x in range(1, 14):

            def combos(ref):
                vm, v0, v1, v2, v3 = (ref[base + (d - 1) * PX + x] for d in range(5))
                p = v0 + v2
                return p + 2.0 * v1, (vm + v3) + 2.0 * p + my * v1

            aa, ba = combos(va)
            ab, bb = combos(vb)
            u = ba + ab
            g = 14.0 * u + 3.0 * bb
            if 2 <= x <= 12:
                g = g + (
                    (sy[base + x] + sy[base + 2 * PX + x]) + 2.0 * sy[base + PX + x]
                )
            gs[x] = g
            hs[x] = 14.0 * aa + 3.0 * u + bb
        for i in range(CX):
            b = 2 + 2 * i
            mx = jnp.where(x0 + b + 2 == nx, 1.0, 2.0).astype(F32)
            raw = (
                (gs[b] + gs[b + 2])
                + 2.0 * gs[b + 1]
                + (hs[b - 1] + hs[b + 3])
                + 2.0 * (hs[b] + hs[b + 2])
                + mx * hs[b + 1]
            ) * (1.0 / 1920.0)
            kr = row_of(kr_t, 3 + 2 * j, b + 1)
            ki = row_of(ki_t, 3 + 2 * j, b + 1)
            c1_out[i, j] = kr * raw + (ki * sgn) * turned(raw)
            ck_out[0, i, pl.ds(j, 1), :] = kr_t[3 + 2 * j, b + 1 : b + 2, :]
            ck_out[1, i, pl.ds(j, 1), :] = ki_t[3 + 2 * j, b + 1 : b + 2, :]
        return carry

    for k in range(2):
        for i in range(CX):
            ck_out[k, i, 8:16, :] = jnp.zeros((8, LANES), F32)
    lax.fori_loop(0, CY, third_stage, 0)

    xb = core * LOW
    yb = LOW + core * OWN_Y

    def own_stage(k, carry):
        y = yb + k
        for xx in range(OWN_X):
            x = xb + xx
            at = (y * PX + x) * 2
            it2_out[xx * OWN_Y + k, 0] = 1.2 * it1[at] + update(y, x, 0, ie_r, ie_i)
            it2_out[xx * OWN_Y + k, 1] = 1.2 * it1[at + 1] + update(y, x, 1, io_r, io_i)
        xe = core * (PX - 1)
        for n, ref in enumerate((ie_r, io_r, ie_i, io_i)):
            inv_out[n, pl.ds(k, 1), :] = ref[y, pl.ds(xe, 1), :]
        return carry

    lax.fori_loop(0, OWN_Y, own_stage, 0)

    j0 = 4 - 4 * core
    for i in range(CX):
        for j in range(NJ):
            send_out[i * NJ + j] = c1_out[i, j0 + j]
        for k in range(2):
            send_out[CX * NJ + (k * CX + i) * 2] = ck_out[k, i, 0:8, :]
            send_out[CX * NJ + (k * CX + i) * 2 + 1] = ck_out[k, i, 8:16, :]
    plane = 6 + 3 * core
    ys = LOW + OWN_Y - core * OWN_Y
    edges, faces = [], []
    for k in range(OWN_Y + 2):
        at = ((ys - 1 + k) * PX + plane) * 2
        even = it1[at]
        odd = it1[at + 1]
        ee, fe = edge_face(even, odd + up(odd, first))
        eo, fo = edge_face(odd, even + down(even, last))
        edges.append((ee, eo))
        faces.append((fe, fo))
    for k in range(OWN_Y):
        for h in range(2):
            send_out[CX * NJ + 4 * CX + 2 * k + h] = faces[k + 1][h] + (
                edges[k][h] + edges[k + 2][h]
            )


SEND = CX * NJ + 4 * CX + 2 * OWN_Y


def cycle_kernel(sc, c1_own, ck_own, recv, it2, inv, out, c1, ckr, cki, cc, pp, qq, vv, oo):
    core = sc[0]
    lanes = lane_iota()
    first = lanes == 0
    last = lanes == LANES - 1
    sgn = sign_rows()
    own_i = CX - core * CX
    other_i = core * CX
    own_j = 4 * core
    other_j = 4 - 4 * core

    for i in range(CX):
        for j in range(NJ):
            at = (own_i + i) * NJ + j
            c1[at] = c1_own[i, own_j + j]
            ckr[at] = jnp.broadcast_to(ck_own[0, i, pl.ds(own_j + j, 1), :], (8, LANES))
            cki[at] = (
                jnp.broadcast_to(ck_own[1, i, pl.ds(own_j + j, 1), :], (8, LANES)) * sgn
            )
            at = (other_i + i) * NJ + j
            c1[at] = recv[i * NJ + j]
            for k, ref in ((0, ckr), (1, cki)):
                row = (CX * NJ + (k * CX + i) * 2) * 8 + own_j + j
                value = recv[row // 8, pl.ds(row % 8, 1), :]
                value = jnp.broadcast_to(value, (8, LANES))
                ref[at] = value * sgn if k else value

    for sweep in range(3):
        ref = c1 if sweep == 0 else cc

        def sums(i, carry, ref=ref, sweep=sweep):
            edges, faces, centres = {}, {}, {}
            for j in range(sweep, NJ - sweep):
                v = ref[i * NJ + j]
                near = up(v, first) + down(v, last)
                edges[j], faces[j] = edge_face(v, near)
                centres[j] = 14.0 * near
            for j in range(sweep + 1, NJ - sweep - 1):
                pp[i * NJ + j] = centres[j] + (faces[j - 1] + faces[j + 1])
                qq[i * NJ + j] = faces[j] + (edges[j - 1] + edges[j + 1])
            return carry

        lax.fori_loop(sweep, NI - sweep, sums, 0)

        def relax(i, carry, ref=ref, sweep=sweep):
            for j in range(sweep + 1, NJ - sweep - 1):
                at = i * NJ + j
                n = (pp[at] + (qq[at - NJ] + qq[at + NJ])) * (1.0 / 120.0)
                cc[at] = (0.2 * ref[at] + c1[at]) + (ckr[at] * n + cki[at] * turned(n))
            return carry

        lax.fori_loop(sweep + 1, NI - sweep - 1, relax, 0)

    def put(x, y, value):
        col = x * OWN_Y + y
        even = 0.5 * (value + up(value, first))
        vv[col * 8 : col * 8 + 8, :LANES] = it2[col, 0] + even
        vv[col * 8 : col * 8 + 8, LANES:] = it2[col, 1] + value

    for i in range(OWN_X // 2):
        for j in range(OWN_Y // 2):
            at = (i + 4) * NJ + j + 4
            here = cc[at]
            left = cc[at - NJ]
            mix = 0.5 * (left + here)
            below = cc[at - 1]
            mix_below = 0.5 * (cc[at - NJ - 1] + below)
            put(2 * i + 1, 2 * j + 1, here)
            put(2 * i, 2 * j + 1, mix)
            put(2 * i + 1, 2 * j, 0.5 * (below + here))
            put(2 * i, 2 * j, 0.5 * (mix_below + mix))

    for k in range(OWN_Y):
        at = pl.multiple_of((core * (OWN_X - 1) * OWN_Y + k) * 8, 8)
        for h in range(2):
            n = recv[CX * NJ + 4 * CX + 2 * k + h]
            ir = jnp.broadcast_to(inv[h, k : k + 1, :], (8, LANES))
            ii = jnp.broadcast_to(inv[2 + h, k : k + 1, :], (8, LANES))
            where = (pl.ds(at, 8), slice(h * LANES, (h + 1) * LANES))
            vv[where] = vv[where] + (ir * n + (ii * sgn) * turned(n))

    rows = lax.broadcasted_iota(jnp.int32, (2 * LANES, 2 * LANES), 0)
    cols = lax.broadcasted_iota(jnp.int32, (2 * LANES, 2 * LANES), 1)
    target = jnp.where(rows < LANES, 2 * rows, 2 * (rows - LANES) + 1)
    perm = jnp.where(cols == target, 1.0, 0.0).astype(jnp.bfloat16)
    value = vv[...]
    top = value.astype(jnp.bfloat16)
    rest = value - top.astype(F32)
    middle = rest.astype(jnp.bfloat16)
    bottom = (rest - middle.astype(F32)).astype(jnp.bfloat16)
    oo[...] = (
        jnp.dot(bottom, perm, preferred_element_type=F32)
        + jnp.dot(middle, perm, preferred_element_type=F32)
    ) + jnp.dot(top, perm, preferred_element_type=F32)
    count = OWN_X * OWN_Y
    for col in range(count):
        block = oo[col * 8 : col * 8 + 8, :]
        for f in range(8):
            out[f * count + col : f * count + col + 1, :] = block[f : f + 1, :]


def vmem(*shape):
    return pltpu.VMEM(shape, F32)


def region_call(*args):
    spec = pl.BlockSpec(memory_space=pltpu.VMEM)
    cells = PY * PX
    return pl.pallas_call(
        region_kernel,
        out_shape=(
            jax.ShapeDtypeStruct((CX, CY, 8, LANES), F32),
            jax.ShapeDtypeStruct((2, CX, 16, LANES), F32),
            jax.ShapeDtypeStruct((SEND, 8, LANES), F32),
            jax.ShapeDtypeStruct((OWN_X * OWN_Y, 2, 8, LANES), F32),
            jax.ShapeDtypeStruct((4, 8, LANES), F32),
        ),
        in_specs=[pl.BlockSpec(memory_space=pltpu.SMEM)] + [spec] * 6,
        out_specs=(spec,) * 5,
        scratch_shapes=[vmem(PY, PX, LANES)] * 12
        + [vmem(cells * 2, 8, LANES)] * 3
        + [vmem(cells, 8, LANES)] * 3,
    )(*args)


def cycle_call(*args):
    spec = pl.BlockSpec(memory_space=pltpu.VMEM)
    points = NI * NJ
    rows = OWN_X * OWN_Y * 8
    return pl.pallas_call(
        cycle_kernel,
        out_shape=jax.ShapeDtypeStruct((rows, 2 * LANES), F32),
        in_specs=[pl.BlockSpec(memory_space=pltpu.SMEM)] + [spec] * 5,
        out_specs=spec,
        scratch_shapes=[vmem(points, 8, LANES)] * 6 + [vmem(rows, 2 * LANES)] * 2,
    )(*args)


def complex_inverse(real, imag):
    modulus = real * real + imag * imag
    return real / modulus, -imag / modulus


def material_tables(er, ei):
    med_r = WAVE_SQUARED * (er + SHIFT_IMAG * ei)
    med_i = WAVE_SQUARED * (ei - SHIFT_IMAG * er)
    inv_r, inv_i = complex_inverse(128.0 / 30.0 - med_r, -med_i)
    src_r = SOURCE_GAIN * (er - 1.0)
    src_i = SOURCE_GAIN * ei
    g_r = DAMPING * (inv_r * src_r - inv_i * src_i)
    g_i = DAMPING * (inv_r * src_i + inv_i * src_r)
    ci_r, ci_i = complex_inverse(128.0 / 120.0 - med_r, -med_i)
    scale = DAMPING / 30.0
    rows = jnp.stack(
        [g_r, g_i, scale * inv_r, scale * inv_i, 1.2 * src_r, 1.2 * src_i,
         DAMPING * ci_r, DAMPING * ci_i]
    )
    return jnp.pad(rows, ((0, 0), (0, LANES - MAT)))


def local(labels, permittivity_real, permittivity_imag, angles, angle_pick):
    gx_n = lax.axis_size("gx")
    gy_n = lax.axis_size("gy")
    gx = lax.axis_index("gx")
    gy = lax.axis_index("gy")
    core = gy % 2
    x0 = OWN_X * gx - LOW * core
    y0 = 2 * OWN_Y * (gy // 2) - LOW
    is_low = core == 0

    def along_x(values, by):
        pairs = []
        for j in range(gy_n):
            step = by if j % 2 == 0 else -by
            for i in range(gx_n):
                if 0 <= i + step < gx_n:
                    pairs.append(((i + step) * gy_n + j, i * gy_n + j))
        return lax.ppermute(values, ("gx", "gy"), pairs)

    def along_y(values, by):
        pairs = [(j, j + by) for j in range(gy_n) if 0 <= j + by < gy_n]
        return lax.ppermute(values, "gy", pairs)

    def core_swap(values):
        return lax.ppermute(values, "gy", [(j, j ^ 1) for j in range(gy_n)])

    other = core_swap(labels)
    both = jnp.where(
        is_low,
        jnp.concatenate([labels, other], axis=1),
        jnp.concatenate([other, labels], axis=1),
    )
    far = along_x(jnp.where(is_low, both[:4], both[2:]), 2)
    near = along_x(both, 1)
    region = jnp.where(
        is_low,
        jnp.concatenate([both, near, far], axis=0),
        jnp.concatenate([far, near, both], axis=0),
    )
    region = jnp.transpose(region, (1, 0, 2))
    low = along_y(region[2 * OWN_Y - LOW :], 2)
    high = along_y(region[: PY - LOW - 2 * OWN_Y], -2)

    table = material_tables(permittivity_real, permittivity_imag)
    pick = (angle_pick[:, None] == jnp.arange(NANG, dtype=jnp.int32)[None, :]).astype(F32)
    incidence = jnp.sum(pick * angles[None, :], axis=1)
    wavenumber = jnp.sqrt(WAVE_SQUARED)
    pos_x = (x0 + jnp.arange(PX, dtype=jnp.int32)).astype(F32)
    pos_y = (y0 + jnp.arange(PY, dtype=jnp.int32)).astype(F32)
    phase_x = wavenumber * (jnp.cos(incidence)[None, :] * pos_x[:, None])
    phase_y = wavenumber * (jnp.sin(incidence)[None, :] * pos_y[:, None])
    phases = jnp.concatenate([phase_x, phase_y], axis=0)
    cosine, sine = lax.optimization_barrier((jnp.cos(phases), jnp.sin(phases)))
    cx, sx, cy, sny = cosine[:PX], sine[:PX], cosine[PX:], sine[PX:]
    ex = jnp.stack(
        [jnp.concatenate([cx, cx], axis=1), jnp.concatenate([sx, sx], axis=1)], axis=1
    )
    ey = jnp.stack(
        [jnp.concatenate([cy, sny], axis=1), jnp.concatenate([-sny, cy], axis=1)], axis=1
    )
    ex = jnp.broadcast_to(ex[..., None], (PX, 2, 8, LANES))
    ey = jnp.broadcast_to(ey[..., None], (PY, 2, 8, LANES))
    scalars = jnp.stack(
        [core, x0, y0, jnp.int32(OWN_X * gx_n), jnp.int32(OWN_Y * gy_n)]
    ).astype(jnp.int32)
    c1, ck, send, it2, inv = region_call(scalars, region, low, high, table, ex, ey)
    recv = core_swap(send)
    out = cycle_call(scalars, c1, ck, recv, it2, inv)
    return out.reshape(2, 4, OWN_X, OWN_Y, 2 * LANES)


def solution(mesh):
    return jax.shard_map(
        local,
        mesh=mesh,
        in_specs=(P("gx", "gy", None), P(), P(), P(), P()),
        out_specs=P(None, None, "gx", "gy", None),
        check_vma=False,
    )
```

```python
import jax
import jax.numpy as jnp
from jax import lax
from jax.experimental import pallas as pl
from jax.experimental.pallas import tpu as pltpu
from jax.sharding import PartitionSpec as P

NANG = 360
MAT = 8
DAMPING = 0.8
WAVE_SQUARED = 0.1
SHIFT_IMAG = 0.5
SOURCE_GAIN = 4.0

OWN_X = 6
OWN_Y = 8
PX = 16
PY = 35
LOW = 10
CX, CY = 5, 15
NI, NJ = 10, 11
LANES = 128
F32 = jnp.float32
OUTSIDE = 8


def lane_iota():
    return lax.broadcasted_iota(jnp.int32, (8, LANES), 1)


def sign_rows():
    rows = lax.broadcasted_iota(jnp.int32, (8, LANES), 0)
    return jnp.where(rows < 4, -1.0, 1.0).astype(F32)


def up(values, first):
    return jnp.where(first, 0.0, pltpu.roll(values, 1, 1))


def down(values, last):
    return jnp.where(last, 0.0, pltpu.roll(values, LANES - 1, 1))


def turned(values):
    return pltpu.roll(values, 4, 0)


def row_of(ref, y, x):
    return jnp.broadcast_to(ref[y, pl.ds(x, 1), :], (8, LANES))


def edge_face(values, near):
    edge = (3.0 / 14.0) * (values + (1.0 / 3.0) * near)
    face = values + (3.0 / 14.0) * near
    return edge, face


def where_am_i():
    gx = lax.axis_index("gx")
    gy = lax.axis_index("gy")
    core = lax.rem(gy, 2)
    x0 = OWN_X * gx - LOW * core
    y0 = OWN_Y * (gy - core) - LOW
    return core, x0, y0


def wave_kernel(ex, ey, wave):
    def rows(y, carry):
        w = ey[y, 0]
        w_t = ey[y, 1]
        for x in range(PX):
            c = ex[x, 0]
            s = ex[x, 1]
            wave[(y * PX + x) * 2] = c * w + s * w_t
            wave[(y * PX + x) * 2 + 1] = c * w_t - s * w
        return carry

    lax.fori_loop(0, PY, rows, 0)


def row_loop(first, count, step, body):
    def some(n, carry):
        for k in range(step):
            body(first + n * step + k)
        return carry

    lax.fori_loop(0, count // step, some, 0)


class Region:
    def __init__(self, sizes, tab, wave, shared, scratch):
        self.nx, self.ny = sizes
        self.core, self.x0, self.y0 = where_am_i()
        self.tab = tab
        self.wave = wave
        (self.ie_r, self.io_r, self.ie_i, self.io_i, self.kr, self.ki,
         self.it1, self.pp, self.qq, self.va, self.vb, self.sy) = shared
        (self.ge_r, self.go_r, self.ge_i, self.go_i, self.sa_r, self.sa_i,
         self.apart) = scratch
        lanes = lane_iota()
        self.first = lanes == 0
        self.last = lanes == LANES - 1
        self.sgn = sign_rows()
        rows = lax.broadcasted_iota(jnp.int32, (2 * LANES, 2 * LANES), 0)
        cols = lax.broadcasted_iota(jnp.int32, (2 * LANES, 2 * LANES), 1)
        source = jnp.where(cols < LANES, 2 * cols, 2 * (cols - LANES) + 1)
        self.perm = jnp.where(rows == source, 1.0, 0.0).astype(jnp.bfloat16)

    def pick(self, row, index):
        table = jnp.broadcast_to(self.tab[row : row + 1, :], (8, LANES))
        return jnp.take_along_axis(table, index, axis=1, mode="promise_in_bounds")

    def tables(self, labels, first_row, count, step):
        flat = labels[...].reshape(count * PX, 2 * LANES).astype(F32).astype(jnp.bfloat16)
        self.apart[0 : count * PX, :] = jnp.dot(
            flat, self.perm, preferred_element_type=F32
        )
        rows = lax.broadcasted_iota(jnp.int32, (8, LANES), 0)
        inside = []
        for h in range(2):
            xs = self.x0 + 8 * h + rows
            inside.append(jnp.logical_and(xs >= 0, xs < self.nx))

        def some(n, carry):
            for k in range(step):
                y = first_row + n * step + k
                y_in = jnp.logical_and(self.y0 + y >= 0, self.y0 + y < self.ny)
                beyond = jnp.where(y_in, 0, OUTSIDE)
                for h in range(2):
                    start = pl.multiple_of((n * step + k) * PX + 8 * h, 8)
                    part = self.apart[pl.ds(start, 8), :]
                    at = (y, pl.ds(8 * h, 8), slice(None))
                    halves = []
                    for odd, (inv_r, inv_i, g_r, g_i) in enumerate(
                        (
                            (self.ie_r, self.ie_i, self.ge_r, self.ge_i),
                            (self.io_r, self.io_i, self.go_r, self.go_i),
                        )
                    ):
                        label = part[:, odd * LANES : (odd + 1) * LANES].astype(jnp.int32)
                        index = jnp.where(inside[h], label, OUTSIDE) + beyond
                        ir = self.pick(0, index)
                        ii = self.pick(1, index)
                        sr = self.pick(2, index)
                        si = self.pick(3, index)
                        inv_r[at] = ir
                        inv_i[at] = ii
                        g_r[at] = (25.0 / 14.0) * (ir * sr - ii * si)
                        g_i[at] = (25.0 / 14.0) * (ir * si + ii * sr)
                        halves.append((sr, si))
                        if odd and (first_row + k) % 2 == 1:
                            self.kr[at] = self.pick(4, index)
                            self.ki[at] = self.pick(5, index)
                    for c, out in ((0, self.sa_r), (1, self.sa_i)):
                        se = halves[0][c]
                        out[at] = se + down(se, self.last) + 2.0 * halves[1][c]
            return carry

        lax.fori_loop(0, count // step, some, 0)

    def first_stage(self, y):
        edges, faces, centres = [[], []], [[], []], [[], []]
        for x in range(PX):
            at = (y * PX + x) * 2
            e = self.wave[at]
            e_t = self.wave[at + 1]
            even = row_of(self.ge_r, y, x) * e + row_of(self.ge_i, y, x) * e_t
            odd = row_of(self.go_r, y, x) * e + row_of(self.go_i, y, x) * e_t
            if 2 <= x <= 12:
                self.sy[y * PX + x] = (
                    row_of(self.sa_r, y, x) * e + row_of(self.sa_i, y, x) * e_t
                )
            self.it1[at] = even
            self.it1[at + 1] = odd
            near_e = odd + up(odd, self.first)
            near_o = even + down(even, self.last)
            for h, (v, near) in enumerate(((even, near_e), (odd, near_o))):
                edge, face = edge_face(v, near)
                edges[h].append(edge)
                faces[h].append(face)
                centres[h].append(near)
        for x in range(PX):
            at = (y * PX + x) * 2
            for h in range(2):
                p = centres[h][x]
                q = faces[h][x]
                if 0 < x < PX - 1:
                    p = p + (faces[h][x - 1] + faces[h][x + 1])
                    q = q + (edges[h][x - 1] + edges[h][x + 1])
                else:
                    beside = x - 1 if x else x + 1
                    p = p + faces[h][beside]
                    q = q + edges[h][beside]
                self.pp[at + h] = p
                self.qq[at + h] = q

    def update(self, y, x, h):
        at = (y * PX + x) * 2 + h
        row = PX * 2
        ir, ii = ((self.ie_r, self.ie_i), (self.io_r, self.io_i))[h]
        n = self.pp[at] + (self.qq[at - row] + self.qq[at + row])
        return row_of(ir, y, x) * n + row_of(ii, y, x) * (self.sgn * turned(n))

    def second_stage(self, y):
        for x in range(1, 14):
            at = (y * PX + x) * 2
            we = 0.4 * self.it1[at] + self.update(y, x, 0)
            wo = 0.4 * self.it1[at + 1] + self.update(y, x, 1)
            p = we + down(we, self.last)
            half = p + wo
            after = jnp.where(self.last, -wo, pltpu.roll(wo, LANES - 1, 1))
            self.va[y * PX + x] = half + wo
            self.vb[y * PX + x] = (up(wo, self.first) + after) + 2.0 * half

    def third_stage(self, j, c1_out, ck_out):
        base = (2 + 2 * j) * PX
        gs, hs = {}, {}
        for x in range(1, 14):

            def combos(ref):
                vm, v0, v1, v2, v3 = (ref[base + (d - 1) * PX + x] for d in range(5))
                half = (v0 + v2) + v1
                return half + v1, (vm + v3) + 2.0 * half

            aa, ba = combos(self.va)
            ab, bb = combos(self.vb)
            u = ba + ab
            if 2 <= x <= 12:
                at = base + x
                gs[x] = (14.0 * u + 3.0 * bb) + (
                    (self.sy[at] + self.sy[at + 2 * PX]) + 2.0 * self.sy[at + PX]
                )
            hs[x] = 14.0 * aa + (3.0 * u + bb)
        for i in range(CX):
            b = 2 + 2 * i
            mx = jnp.where(self.x0 + b + 2 == self.nx, 1.0, 2.0).astype(F32)
            raw = (
                (gs[b] + gs[b + 2])
                + 2.0 * (gs[b + 1] + (hs[b] + hs[b + 2]))
                + (hs[b - 1] + hs[b + 3])
                + mx * hs[b + 1]
            ) * (1.0 / 1920.0)
            kr = row_of(self.kr, 3 + 2 * j, b + 1)
            ki = row_of(self.ki, 3 + 2 * j, b + 1)
            c1_out[i, j] = kr * raw + ki * (self.sgn * turned(raw))
            ck_out[0, i, pl.ds(j, 1), :] = self.kr[3 + 2 * j, b + 1 : b + 2, :]
            ck_out[1, i, pl.ds(j, 1), :] = self.ki[3 + 2 * j, b + 1 : b + 2, :]


def middle_kernel(sizes, labels, tab, wave, *refs):
    region = Region(sizes, tab, wave, refs[:12], refs[12:])
    region.tables(labels, LOW, 2 * OWN_Y, 8)
    row_loop(LOW, 2 * OWN_Y, 2, region.first_stage)
    row_loop(LOW + 1, 2 * OWN_Y - 2, 2, region.second_stage)


def outer_kernel(sizes, low, high, tab, wave, *refs):
    region = Region(sizes, tab, wave, refs[12:24], refs[29:])
    c1_out, ck_out, send_out, it2_out, inv_out = refs[24:29]
    core, y0, ny = region.core, region.y0, region.ny
    it1 = region.it1
    top = LOW + 2 * OWN_Y
    region.tables(low, 0, LOW, LOW)
    row_loop(0, LOW, 2, region.first_stage)
    row_loop(1, LOW, 2, region.second_stage)
    region.tables(high, top, PY - top, PY - top)
    row_loop(top, PY - top, 3, region.first_stage)
    row_loop(top - 1, PY - top, 3, region.second_stage)

    @pl.when(y0 + top == ny)
    def _():
        for x in range(1, 14):
            for ref in (region.va, region.vb):
                ref[(top + 1) * PX + x] = -ref[(top - 1) * PX + x]

    for k in range(2):
        for i in range(CX):
            ck_out[k, i, 8:16, :] = jnp.zeros((8, LANES), F32)
    row_loop(0, CY, 1, lambda j: region.third_stage(j, c1_out, ck_out))

    xb = core * LOW
    yb = LOW + core * OWN_Y
    xe = core * (PX - 1)
    tables = (region.ie_r, region.io_r, region.ie_i, region.io_i)

    def own_stage(k):
        y = yb + k
        for xx in range(OWN_X):
            x = xb + xx
            at = (y * PX + x) * 2
            for h in range(2):
                it2_out[xx * OWN_Y + k, h] = 1.2 * it1[at + h] + region.update(y, x, h)
        for n, ref in enumerate(tables):
            inv_out[n, pl.ds(k, 1), :] = ref[y, pl.ds(xe, 1), :]

    row_loop(0, OWN_Y, 2, own_stage)

    j0 = 4 - 4 * core
    for i in range(CX):
        for j in range(NJ):
            send_out[i * NJ + j] = c1_out[i, j0 + j]
        for k in range(2):
            send_out[CX * NJ + (k * CX + i) * 2] = ck_out[k, i, 0:8, :]
            send_out[CX * NJ + (k * CX + i) * 2 + 1] = ck_out[k, i, 8:16, :]
    plane = 6 + 3 * core
    ys = LOW + OWN_Y - core * OWN_Y
    edges, faces = [], []
    for k in range(OWN_Y + 2):
        at = ((ys - 1 + k) * PX + plane) * 2
        even = it1[at]
        odd = it1[at + 1]
        ee, fe = edge_face(even, odd + up(odd, region.first))
        eo, fo = edge_face(odd, even + down(even, region.last))
        edges.append((ee, eo))
        faces.append((fe, fo))
    for k in range(OWN_Y):
        for h in range(2):
            send_out[CX * NJ + 4 * CX + 2 * k + h] = faces[k + 1][h] + (
                edges[k][h] + edges[k + 2][h]
            )


SEND = CX * NJ + 4 * CX + 2 * OWN_Y


def cycle_kernel(c1_own, ck_own, recv, it2, inv, out, c1, ckr, cki, cc, pp, qq, vv, o0, o1):
    core = where_am_i()[0]
    lanes = lane_iota()
    first = lanes == 0
    last = lanes == LANES - 1
    sgn = sign_rows()

    def spread(row):
        return jnp.broadcast_to(row, (8, LANES))

    def assemble(which):
        own_i, other_i, j0 = CX - which * CX, which * CX, 4 * which
        for i in range(CX):
            for j in range(NJ):
                at = (own_i + i) * NJ + j
                row = j0 + j
                c1[at] = c1_own[i, row]
                ckr[at] = spread(ck_own[0, i, row : row + 1, :])
                cki[at] = spread(ck_own[1, i, row : row + 1, :]) * sgn
                at = (other_i + i) * NJ + j
                c1[at] = recv[i * NJ + j]
                for k, ref in ((0, ckr), (1, cki)):
                    tile = CX * NJ + (k * CX + i) * 2 + row // 8
                    value = spread(recv[tile, row % 8 : row % 8 + 1, :])
                    ref[at] = value * sgn if k else value

    @pl.when(core == 0)
    def _():
        assemble(0)

    @pl.when(core == 1)
    def _():
        assemble(1)

    for sweep in range(3):
        ref = c1 if sweep == 0 else cc

        def sums(i, ref=ref, sweep=sweep):
            edges, faces, centres = {}, {}, {}
            for j in range(sweep, NJ - sweep):
                v = ref[i * NJ + j]
                near = up(v, first) + down(v, last)
                edges[j], faces[j] = edge_face(v, near)
                centres[j] = near
            for j in range(sweep + 1, NJ - sweep - 1):
                pp[i * NJ + j] = centres[j] + (faces[j - 1] + faces[j + 1])
                qq[i * NJ + j] = faces[j] + (edges[j - 1] + edges[j + 1])

        row_loop(sweep, NI - 2 * sweep, 2, sums)

        def relax(i, ref=ref, sweep=sweep):
            for j in range(sweep + 1, NJ - sweep - 1):
                at = i * NJ + j
                n = (pp[at] + (qq[at - NJ] + qq[at + NJ])) * (14.0 / 120.0)
                cc[at] = (0.2 * ref[at] + c1[at]) + (ckr[at] * n + cki[at] * turned(n))

        row_loop(sweep + 1, NI - 2 * sweep - 2, 2, relax)

    def put(x, y, value):
        col = x * OWN_Y + y
        even = 0.5 * (value + up(value, first))
        vv[col * 8 : col * 8 + 8, :LANES] = it2[col, 0] + even
        vv[col * 8 : col * 8 + 8, LANES:] = it2[col, 1] + value

    for i in range(OWN_X // 2):
        for j in range(OWN_Y // 2):
            at = (i + 4) * NJ + j + 4
            here = cc[at]
            left = cc[at - NJ]
            mix = 0.5 * (left + here)
            below = cc[at - 1]
            mix_below = 0.5 * (cc[at - NJ - 1] + below)
            put(2 * i + 1, 2 * j + 1, here)
            put(2 * i, 2 * j + 1, mix)
            put(2 * i + 1, 2 * j, 0.5 * (below + here))
            put(2 * i, 2 * j, 0.5 * (mix_below + mix))

    for k in range(OWN_Y):
        at = pl.multiple_of((core * (OWN_X - 1) * OWN_Y + k) * 8, 8)
        for h in range(2):
            n = recv[CX * NJ + 4 * CX + 2 * k + h]
            ir = spread(inv[h, k : k + 1, :])
            ii = spread(inv[2 + h, k : k + 1, :])
            where = (pl.ds(at, 8), slice(h * LANES, (h + 1) * LANES))
            vv[where] = vv[where] + (ir * n + (ii * sgn) * turned(n))

    rows = lax.broadcasted_iota(jnp.int32, (2 * LANES, 2 * LANES), 0)
    cols = lax.broadcasted_iota(jnp.int32, (2 * LANES, 2 * LANES), 1)
    target = jnp.where(rows < LANES, 2 * rows, 2 * (rows - LANES) + 1)
    perm = jnp.where(cols == target, 1.0, 0.0).astype(jnp.bfloat16)
    count = OWN_X * OWN_Y
    for x in range(OWN_X):
        value = vv[x * 64 : x * 64 + 64, :]
        top = value.astype(jnp.bfloat16)
        rest = value - top.astype(F32)
        middle = rest.astype(jnp.bfloat16)
        bottom = (rest - middle.astype(F32)).astype(jnp.bfloat16)
        mixed = (
            jnp.dot(bottom, perm, preferred_element_type=F32)
            + jnp.dot(middle, perm, preferred_element_type=F32)
        ) + jnp.dot(top, perm, preferred_element_type=F32)
        for y in range(OWN_Y):
            block = mixed[y * 8 : y * 8 + 8]
            o0[pl.ds(x * OWN_Y + y, 8, stride=count), :] = block[:, :LANES]
            o1[pl.ds(x * OWN_Y + y, 8, stride=count), :] = block[:, LANES:]
    out[:, :LANES] = o0[...]
    out[:, LANES:] = o1[...]


def vmem(*shape):
    return pltpu.VMEM(shape, F32)


SPEC = pl.BlockSpec(memory_space=pltpu.VMEM)
CELLS = PY * PX
SHARED = (vmem(PY, PX, LANES),) * 6 + (vmem(CELLS * 2, 8, LANES),) * 3 + (
    vmem(CELLS, 8, LANES),
) * 3
TABLES = [vmem(PY, PX, LANES)] * 6


def limit(mib):
    return pltpu.CompilerParams(vmem_limit_bytes=mib << 20)


def near_core(*arrays):
    return [pltpu.with_memory_space_constraint(a, pltpu.VMEM) for a in arrays]


def wave_call(ex, ey):
    return pl.pallas_call(
        wave_kernel,
        out_shape=vmem(CELLS * 2, 8, LANES),
        in_specs=[SPEC] * 2,
        out_specs=SPEC,
        compiler_params=limit(2),
    )(*near_core(ex, ey))


def middle_call(sizes, labels, tab, wave):
    def kernel(*refs):
        middle_kernel(sizes, *refs)

    return pl.pallas_call(
        kernel,
        out_shape=SHARED,
        in_specs=[SPEC] * 3,
        out_specs=(SPEC,) * 12,
        scratch_shapes=TABLES + [vmem(2 * OWN_Y * PX, 2 * LANES)],
        compiler_params=limit(6),
    )(*near_core(labels, tab, wave))


def outer_call(sizes, low, high, tab, wave, shared):
    def kernel(*refs):
        outer_kernel(sizes, *refs)

    results = pl.pallas_call(
        kernel,
        out_shape=SHARED
        + (
            vmem(CX, CY, 8, LANES),
            vmem(2, CX, 16, LANES),
            vmem(SEND, 8, LANES),
            vmem(OWN_X * OWN_Y, 2, 8, LANES),
            vmem(4, 8, LANES),
        ),
        in_specs=[SPEC] * 16,
        out_specs=(SPEC,) * 17,
        input_output_aliases={4 + n: n for n in range(12)},
        scratch_shapes=TABLES + [vmem(LOW * PX, 2 * LANES)],
        compiler_params=limit(6),
    )(*near_core(low, high, tab, wave), *shared)
    return results[12:]


def cycle_call(*args):
    points = NI * NJ
    rows = OWN_X * OWN_Y * 8
    return pl.pallas_call(
        cycle_kernel,
        out_shape=jax.ShapeDtypeStruct((rows, 2 * LANES), F32),
        in_specs=[SPEC] * 5,
        out_specs=SPEC,
        scratch_shapes=[vmem(points, 8, LANES)] * 6
        + [vmem(rows, 2 * LANES)]
        + [vmem(rows, LANES)] * 2,
        compiler_params=limit(8),
    )(*near_core(*args))


def complex_inverse(real, imag):
    modulus = real * real + imag * imag
    return real / modulus, -imag / modulus


def material_tables(er, ei):
    med_r = WAVE_SQUARED * (er + SHIFT_IMAG * ei)
    med_i = WAVE_SQUARED * (ei - SHIFT_IMAG * er)
    inv_r, inv_i = complex_inverse(128.0 / 30.0 - med_r, -med_i)
    src_r = SOURCE_GAIN * (er - 1.0)
    src_i = SOURCE_GAIN * ei
    ci_r, ci_i = complex_inverse(128.0 / 120.0 - med_r, -med_i)
    scale = 14.0 * DAMPING / 30.0
    rows = jnp.stack(
        [scale * inv_r, scale * inv_i, 1.2 * src_r, 1.2 * src_i,
         DAMPING * ci_r, DAMPING * ci_i]
    )
    return jnp.pad(rows, ((0, 2), (0, LANES - MAT)))


def local(labels, permittivity_real, permittivity_imag, angles, angle_pick):
    gx_n = lax.axis_size("gx")
    gy_n = lax.axis_size("gy")
    gx = lax.axis_index("gx")
    gy = lax.axis_index("gy")
    core = gy % 2
    x0 = OWN_X * gx - LOW * core
    y0 = 2 * OWN_Y * (gy // 2) - LOW
    is_low = core == 0

    def along_x(values, by):
        pairs = []
        for j in range(gy_n):
            step = by if j % 2 == 0 else -by
            for i in range(gx_n):
                if 0 <= i + step < gx_n:
                    pairs.append(((i + step) * gy_n + j, i * gy_n + j))
        return lax.ppermute(values, ("gx", "gy"), pairs)

    def along_y(values, by):
        pairs = [(j, j + by) for j in range(gy_n) if 0 <= j + by < gy_n]
        return lax.ppermute(values, "gy", pairs)

    def core_swap(values):
        return lax.ppermute(values, "gy", [(j, j ^ 1) for j in range(gy_n)])

    other = core_swap(labels)
    both = jnp.where(
        is_low,
        jnp.concatenate([labels, other], axis=1),
        jnp.concatenate([other, labels], axis=1),
    )
    far = along_x(jnp.where(is_low, both[:4], both[2:]), 2)
    near = along_x(both, 1)
    region = jnp.where(
        is_low,
        jnp.concatenate([both, near, far], axis=0),
        jnp.concatenate([far, near, both], axis=0),
    )
    region = jnp.transpose(region, (1, 0, 2))
    low = along_y(region[2 * OWN_Y - LOW :], 2)
    high = along_y(region[: PY - LOW - 2 * OWN_Y], -2)

    table = material_tables(permittivity_real, permittivity_imag)
    pick = (angle_pick[:, None] == jnp.arange(NANG, dtype=jnp.int32)[None, :]).astype(F32)
    incidence = jnp.sum(pick * angles[None, :], axis=1)
    wavenumber = jnp.sqrt(WAVE_SQUARED)
    pos_x = (x0 + jnp.arange(PX, dtype=jnp.int32)).astype(F32)
    pos_y = (y0 + jnp.arange(PY, dtype=jnp.int32)).astype(F32)
    phase_x = wavenumber * (jnp.cos(incidence)[None, :] * pos_x[:, None])
    phase_y = wavenumber * (jnp.sin(incidence)[None, :] * pos_y[:, None])
    phases = jnp.concatenate([phase_x, phase_y], axis=0)
    cosine, sine = lax.optimization_barrier((jnp.cos(phases), jnp.sin(phases)))
    cx, sx, cy, sny = cosine[:PX], sine[:PX], cosine[PX:], sine[PX:]
    ex = jnp.stack(
        [jnp.concatenate([cx, cx], axis=1), jnp.concatenate([sx, sx], axis=1)], axis=1
    )
    ey = jnp.stack(
        [jnp.concatenate([cy, sny], axis=1), jnp.concatenate([-sny, cy], axis=1)], axis=1
    )
    ex = jnp.broadcast_to(ex[..., None], (PX, 2, 8, LANES))
    ey = jnp.broadcast_to(ey[..., None], (PY, 2, 8, LANES))
    wave = wave_call(ex, ey)
    sizes = (OWN_X * gx_n, OWN_Y * gy_n)
    shared = middle_call(sizes, region, table, wave)
    c1, ck, send, it2, inv = outer_call(sizes, low, high, table, wave, shared)
    recv = core_swap(send)
    out = cycle_call(c1, ck, recv, it2, inv)
    return out.reshape(2, 4, OWN_X, OWN_Y, 2 * LANES)


def solution(mesh):
    return jax.shard_map(
        local,
        mesh=mesh,
        in_specs=(P("gx", "gy", None), P(), P(), P(), P()),
        out_specs=P(None, None, "gx", "gy", None),
        check_vma=False,
    )
```

```python
import jax
import jax.numpy as jnp
import numpy as np
from jax import lax
from jax.experimental import pallas as pl
from jax.experimental.pallas import tpu as pltpu
from jax.experimental.layout import Layout, with_layout_constraint
from jax.sharding import PartitionSpec as P

MAT = 8
DAMPING = 0.8
WAVE_SQUARED = 0.1
SHIFT_IMAG = 0.5
SOURCE_GAIN = 4.0

OWN_X = 6
OWN_Y = 8
PX = 16
PY = 35
LOW = 10
CX, CY = 5, 15
NI, NJ = 10, 11
LANES = 128
F32 = jnp.float32
OUTSIDE = 8
WAVENUMBER = float(np.sqrt(np.float32(WAVE_SQUARED)))


def lane_iota():
    return lax.broadcasted_iota(jnp.int32, (8, LANES), 1)


def sign_rows():
    rows = lax.broadcasted_iota(jnp.int32, (8, LANES), 0)
    return jnp.where(rows < 4, -1.0, 1.0).astype(F32)


def up(values, first):
    return jnp.where(first, 0.0, pltpu.roll(values, 1, 1))


def down(values, last):
    return jnp.where(last, 0.0, pltpu.roll(values, LANES - 1, 1))


def turned(values):
    return pltpu.roll(values, 4, 0)


def row_of(ref, y, x):
    return jnp.broadcast_to(ref[y, pl.ds(x, 1), :], (8, LANES))


def edge_face(values, near):
    edge = (3.0 / 14.0) * (values + (1.0 / 3.0) * near)
    face = values + (3.0 / 14.0) * near
    return edge, face


def where_am_i():
    gx = lax.axis_index("gx")
    gy = lax.axis_index("gy")
    core = lax.rem(gy, 2)
    x0 = OWN_X * gx - LOW * core
    y0 = OWN_Y * (gy - core) - LOW
    return core, x0, y0


def splat(value):
    return jnp.full((8, LANES), value, F32)


def wave_kernel(
    real_in, imag_in, angles_in, picks_in, after, wave, tab, real, imag, angles, picks, sems
):
    del after
    copies = [
        pltpu.make_async_copy(src, dst, sems.at[n])
        for n, (src, dst) in enumerate(
            (
                (real_in, real),
                (imag_in, imag),
                (angles_in, angles),
                (picks_in, picks),
            )
        )
    ]
    for copy in copies:
        copy.start()
    for copy in copies:
        copy.wait()
    _, x0, y0 = where_am_i()
    lanes = lane_iota()
    rows = lax.broadcasted_iota(jnp.int32, (8, LANES), 0)

    er = jnp.zeros((8, LANES), F32)
    ei = jnp.zeros((8, LANES), F32)
    for m in range(MAT):
        er = jnp.where(lanes == m, splat(real[m]), er)
        ei = jnp.where(lanes == m, splat(imag[m]), ei)
    for n, table in enumerate(material_tables(er, ei)):
        tab[n : n + 1, :] = jnp.where(lanes < MAT, table, 0.0)[0:1]

    incidence = jnp.zeros((8, LANES), F32)
    for c in range(4):
        mine = jnp.bitwise_and(rows, 3) == c
        incidence = jnp.where(mine, splat(angles[picks[c]]), incidence)
    in_x = lanes < PX
    place = jnp.where(in_x, x0 + lanes, y0 + (lanes - PX)).astype(F32)
    slope = jnp.where(in_x, jnp.cos(incidence), jnp.sin(incidence))
    phases = WAVENUMBER * (slope * place)
    cosine = jnp.cos(phases)
    sine = jnp.sin(phases)
    upper = rows < 4
    front = jnp.where(upper, cosine, sine)
    turn = jnp.where(upper, -sine, cosine)

    def along(values, n):
        return jnp.broadcast_to(values[:, n : n + 1], (8, LANES))

    for x in range(PX):
        wave[x * 2] = along(cosine, x)
        wave[x * 2 + 1] = along(sine, x)
    for y in reversed(range(PY)):
        w = along(front, PX + y)
        w_t = along(turn, PX + y)
        for x in range(PX):
            c = wave[x * 2]
            s = wave[x * 2 + 1]
            wave[(y * PX + x) * 2] = c * w + s * w_t
            wave[(y * PX + x) * 2 + 1] = c * w_t - s * w


def row_loop(first, count, step, body):
    def some(n, carry):
        for k in range(step):
            body(first + n * step + k)
        return carry

    lax.fori_loop(0, count // step, some, 0)


class Region:
    def __init__(self, sizes, tab, wave, shared, scratch):
        self.nx, self.ny = sizes
        self.core, self.x0, self.y0 = where_am_i()
        self.tab = tab
        self.wave = wave
        (self.ie_r, self.io_r, self.ie_i, self.io_i, self.kr, self.ki,
         self.it1, self.pp, self.qq, self.va, self.vb, self.sy) = shared
        (self.ge_r, self.go_r, self.ge_i, self.go_i, self.sa_r, self.sa_i,
         self.apart) = scratch
        lanes = lane_iota()
        self.first = lanes == 0
        self.last = lanes == LANES - 1
        self.sgn = sign_rows()
        rows = lax.broadcasted_iota(jnp.int32, (2 * LANES, 2 * LANES), 0)
        cols = lax.broadcasted_iota(jnp.int32, (2 * LANES, 2 * LANES), 1)
        source = jnp.where(cols < LANES, 2 * cols, 2 * (cols - LANES) + 1)
        self.perm = jnp.where(rows == source, 1.0, 0.0).astype(jnp.bfloat16)

    def pick(self, row, index):
        table = jnp.broadcast_to(self.tab[row : row + 1, :], (8, LANES))
        return jnp.take_along_axis(table, index, axis=1, mode="promise_in_bounds")

    def tables(self, labels, first_row, count, step):
        flat = labels[...].reshape(count * PX, 2 * LANES).astype(F32).astype(jnp.bfloat16)
        self.apart[0 : count * PX, :] = jnp.dot(
            flat, self.perm, preferred_element_type=F32
        )
        rows = lax.broadcasted_iota(jnp.int32, (8, LANES), 0)
        inside = []
        for h in range(2):
            xs = self.x0 + 8 * h + rows
            inside.append(jnp.logical_and(xs >= 0, xs < self.nx))

        def some(n, carry):
            for k in range(step):
                y = first_row + n * step + k
                y_in = jnp.logical_and(self.y0 + y >= 0, self.y0 + y < self.ny)
                beyond = jnp.where(y_in, 0, OUTSIDE)
                for h in range(2):
                    start = pl.multiple_of((n * step + k) * PX + 8 * h, 8)
                    part = self.apart[pl.ds(start, 8), :]
                    at = (y, pl.ds(8 * h, 8), slice(None))
                    halves = []
                    for odd, (inv_r, inv_i, g_r, g_i) in enumerate(
                        (
                            (self.ie_r, self.ie_i, self.ge_r, self.ge_i),
                            (self.io_r, self.io_i, self.go_r, self.go_i),
                        )
                    ):
                        label = part[:, odd * LANES : (odd + 1) * LANES].astype(jnp.int32)
                        index = jnp.where(inside[h], label, OUTSIDE) + beyond
                        ir = self.pick(0, index)
                        ii = self.pick(1, index)
                        sr = self.pick(2, index)
                        si = self.pick(3, index)
                        inv_r[at] = ir
                        inv_i[at] = ii
                        g_r[at] = (25.0 / 14.0) * (ir * sr - ii * si)
                        g_i[at] = (25.0 / 14.0) * (ir * si + ii * sr)
                        halves.append((sr, si))
                        if odd and (first_row + k) % 2 == 1:
                            self.kr[at] = self.pick(4, index)
                            self.ki[at] = self.pick(5, index)
                    for c, out in ((0, self.sa_r), (1, self.sa_i)):
                        se = halves[0][c]
                        out[at] = se + down(se, self.last) + 2.0 * halves[1][c]
            return carry

        lax.fori_loop(0, count // step, some, 0)

    def first_stage(self, y):
        edges, faces, centres = [[], []], [[], []], [[], []]
        for x in range(PX):
            at = (y * PX + x) * 2
            e = self.wave[at]
            e_t = self.wave[at + 1]
            even = row_of(self.ge_r, y, x) * e + row_of(self.ge_i, y, x) * e_t
            odd = row_of(self.go_r, y, x) * e + row_of(self.go_i, y, x) * e_t
            if 2 <= x <= 12:
                self.sy[y * PX + x] = (
                    row_of(self.sa_r, y, x) * e + row_of(self.sa_i, y, x) * e_t
                )
            self.it1[at] = even
            self.it1[at + 1] = odd
            near_e = odd + up(odd, self.first)
            near_o = even + down(even, self.last)
            for h, (v, near) in enumerate(((even, near_e), (odd, near_o))):
                edge, face = edge_face(v, near)
                edges[h].append(edge)
                faces[h].append(face)
                centres[h].append(near)
        for x in range(PX):
            at = (y * PX + x) * 2
            for h in range(2):
                p = centres[h][x]
                q = faces[h][x]
                if 0 < x < PX - 1:
                    p = p + (faces[h][x - 1] + faces[h][x + 1])
                    q = q + (edges[h][x - 1] + edges[h][x + 1])
                else:
                    beside = x - 1 if x else x + 1
                    p = p + faces[h][beside]
                    q = q + edges[h][beside]
                self.pp[at + h] = p
                self.qq[at + h] = q

    def update(self, y, x, h):
        at = (y * PX + x) * 2 + h
        row = PX * 2
        ir, ii = ((self.ie_r, self.ie_i), (self.io_r, self.io_i))[h]
        n = self.pp[at] + (self.qq[at - row] + self.qq[at + row])
        return row_of(ir, y, x) * n + row_of(ii, y, x) * (self.sgn * turned(n))

    def second_stage(self, y):
        for x in range(1, 14):
            at = (y * PX + x) * 2
            we = 0.4 * self.it1[at] + self.update(y, x, 0)
            wo = 0.4 * self.it1[at + 1] + self.update(y, x, 1)
            p = we + down(we, self.last)
            half = p + wo
            after = jnp.where(self.last, -wo, pltpu.roll(wo, LANES - 1, 1))
            self.va[y * PX + x] = half + wo
            self.vb[y * PX + x] = (up(wo, self.first) + after) + 2.0 * half

    def third_stage(self, j, c1_out, ck_out):
        base = (2 + 2 * j) * PX
        gs, hs = {}, {}
        for x in range(1, 14):

            def combos(ref):
                vm, v0, v1, v2, v3 = (ref[base + (d - 1) * PX + x] for d in range(5))
                half = (v0 + v2) + v1
                return half + v1, (vm + v3) + 2.0 * half

            aa, ba = combos(self.va)
            ab, bb = combos(self.vb)
            u = ba + ab
            if 2 <= x <= 12:
                at = base + x
                gs[x] = (14.0 * u + 3.0 * bb) + (
                    (self.sy[at] + self.sy[at + 2 * PX]) + 2.0 * self.sy[at + PX]
                )
            hs[x] = 14.0 * aa + (3.0 * u + bb)
        for i in range(CX):
            b = 2 + 2 * i
            mx = jnp.where(self.x0 + b + 2 == self.nx, 1.0, 2.0).astype(F32)
            raw = (
                (gs[b] + gs[b + 2])
                + 2.0 * (gs[b + 1] + (hs[b] + hs[b + 2]))
                + (hs[b - 1] + hs[b + 3])
                + mx * hs[b + 1]
            ) * (1.0 / 1920.0)
            kr = row_of(self.kr, 3 + 2 * j, b + 1)
            ki = row_of(self.ki, 3 + 2 * j, b + 1)
            c1_out[i, j] = kr * raw + ki * (self.sgn * turned(raw))
            ck_out[0, i, pl.ds(j, 1), :] = self.kr[3 + 2 * j, b + 1 : b + 2, :]
            ck_out[1, i, pl.ds(j, 1), :] = self.ki[3 + 2 * j, b + 1 : b + 2, :]


def middle_kernel(sizes, labels, tab, wave, *refs):
    region = Region(sizes, tab, wave, refs[:12], refs[12:])
    region.tables(labels, LOW, 2 * OWN_Y, 8)
    row_loop(LOW, 2 * OWN_Y, 4, region.first_stage)
    row_loop(LOW + 1, 2 * OWN_Y - 2, 7, region.second_stage)


def outer_kernel(sizes, low, high, tab, wave, *refs):
    region = Region(sizes, tab, wave, refs[12:24], refs[29:])
    c1_out, ck_out, send_out, it2_out, inv_out = refs[24:29]
    core, y0, ny = region.core, region.y0, region.ny
    it1 = region.it1
    top = LOW + 2 * OWN_Y
    region.tables(low, 0, LOW, LOW)
    row_loop(0, LOW, 5, region.first_stage)
    row_loop(1, LOW, 5, region.second_stage)
    region.tables(high, top, PY - top, PY - top)
    row_loop(top, PY - top, 3, region.first_stage)
    row_loop(top - 1, PY - top, 3, region.second_stage)

    @pl.when(y0 + top == ny)
    def _():
        for x in range(1, 14):
            for ref in (region.va, region.vb):
                ref[(top + 1) * PX + x] = -ref[(top - 1) * PX + x]

    for k in range(2):
        for i in range(CX):
            ck_out[k, i, 8:16, :] = jnp.zeros((8, LANES), F32)
    row_loop(0, CY, 1, lambda j: region.third_stage(j, c1_out, ck_out))

    xb = core * LOW
    yb = LOW + core * OWN_Y
    xe = core * (PX - 1)
    tables = (region.ie_r, region.io_r, region.ie_i, region.io_i)

    def own_stage(k):
        y = yb + k
        for xx in range(OWN_X):
            x = xb + xx
            at = (y * PX + x) * 2
            for h in range(2):
                it2_out[xx * OWN_Y + k, h] = 1.2 * it1[at + h] + region.update(y, x, h)
        for n, ref in enumerate(tables):
            inv_out[n, pl.ds(k, 1), :] = ref[y, pl.ds(xe, 1), :]

    row_loop(0, OWN_Y, 2, own_stage)

    j0 = 4 - 4 * core
    for i in range(CX):
        for j in range(NJ):
            send_out[i * NJ + j] = c1_out[i, j0 + j]
        for k in range(2):
            send_out[CX * NJ + (k * CX + i) * 2] = ck_out[k, i, 0:8, :]
            send_out[CX * NJ + (k * CX + i) * 2 + 1] = ck_out[k, i, 8:16, :]
    plane = 6 + 3 * core
    ys = LOW + OWN_Y - core * OWN_Y
    edges, faces = [], []
    for k in range(OWN_Y + 2):
        at = ((ys - 1 + k) * PX + plane) * 2
        even = it1[at]
        odd = it1[at + 1]
        ee, fe = edge_face(even, odd + up(odd, region.first))
        eo, fo = edge_face(odd, even + down(even, region.last))
        edges.append((ee, eo))
        faces.append((fe, fo))
    for k in range(OWN_Y):
        for h in range(2):
            send_out[CX * NJ + 4 * CX + 2 * k + h] = faces[k + 1][h] + (
                edges[k][h] + edges[k + 2][h]
            )


SEND = CX * NJ + 4 * CX + 2 * OWN_Y


def cycle_kernel(c1_own, ck_own, recv, it2, inv, out, c1, ck, cc, pp, qq, parts, o0, o1):
    core = where_am_i()[0]
    lanes = lane_iota()
    first = lanes == 0
    last = lanes == LANES - 1
    sgn = sign_rows()
    j0 = 4 * core

    def spread(row):
        return jnp.broadcast_to(row, (8, LANES))

    def assemble(which):
        own_i, other_i = CX - which * CX, which * CX
        for i in range(CX):
            for j in range(NJ):
                c1[(own_i + i) * NJ + j] = c1_own[i, 4 * which + j]
                c1[(other_i + i) * NJ + j] = recv[i * NJ + j]
            for k in range(2):
                for h in range(2):
                    tile = slice(8 * h, 8 * h + 8)
                    ck[k, own_i + i, tile, :] = ck_own[k, i, tile, :]
                    ck[k, other_i + i, tile, :] = recv[CX * NJ + (k * CX + i) * 2 + h]

    @pl.when(core == 0)
    def _():
        assemble(0)

    @pl.when(core == 1)
    def _():
        assemble(1)

    for sweep, (sum_step, relax_step) in enumerate(((5, 4), (4, 3), (3, 4))):
        ref = c1 if sweep == 0 else cc

        def sums(i, ref=ref, sweep=sweep):
            edges, faces, centres = {}, {}, {}
            for j in range(sweep, NJ - sweep):
                v = ref[i * NJ + j]
                near = up(v, first) + down(v, last)
                edges[j], faces[j] = edge_face(v, near)
                centres[j] = near
            for j in range(sweep + 1, NJ - sweep - 1):
                pp[i * NJ + j] = centres[j] + (faces[j - 1] + faces[j + 1])
                qq[i * NJ + j] = faces[j] + (edges[j - 1] + edges[j + 1])

        row_loop(sweep, NI - 2 * sweep, sum_step, sums)

        def relax(i, ref=ref, sweep=sweep):
            for j in range(sweep + 1, NJ - sweep - 1):
                at = i * NJ + j
                n = (pp[at] + (qq[at - NJ] + qq[at + NJ])) * (14.0 / 120.0)
                kr = spread(ck[0, i, pl.ds(j0 + j, 1), :])
                ki = spread(ck[1, i, pl.ds(j0 + j, 1), :])
                cc[at] = (0.2 * ref[at] + c1[at]) + (kr * n + ki * (sgn * turned(n)))

        row_loop(sweep + 1, NI - 2 * sweep - 2, relax_step, relax)

    flags = {0: jnp.where(core == 0, 1.0, 0.0), OWN_X - 1: jnp.where(core == 1, 1.0, 0.0)}
    added = []
    for k in range(OWN_Y):
        pair = []
        for h in range(2):
            n = recv[CX * NJ + 4 * CX + 2 * k + h]
            ir = spread(inv[h, k : k + 1, :])
            ii = spread(inv[2 + h, k : k + 1, :])
            pair.append(ir * n + ii * (sgn * turned(n)))
        added.append(pair)

    rows = lax.broadcasted_iota(jnp.int32, (2 * LANES, 2 * LANES), 0)
    cols = lax.broadcasted_iota(jnp.int32, (2 * LANES, 2 * LANES), 1)
    target = jnp.where(rows < LANES, 2 * rows, 2 * (rows - LANES) + 1)
    perm = jnp.where(cols == target, 1.0, 0.0).astype(jnp.bfloat16)
    count = OWN_X * OWN_Y

    def fine(x, y, value):
        col = x * OWN_Y + y
        even = it2[col, 0] + 0.5 * (value + up(value, first))
        odd = it2[col, 1] + value
        if x in flags:
            even = even + flags[x] * added[y][0]
            odd = odd + flags[x] * added[y][1]
        return even, odd

    size = 2 * OWN_Y * 8
    for i in range(OWN_X // 2):
        for j in range(OWN_Y // 2):
            at = (i + 4) * NJ + j + 4
            here = cc[at]
            left = cc[at - NJ]
            mix = 0.5 * (left + here)
            below = cc[at - 1]
            mix_below = 0.5 * (cc[at - NJ - 1] + below)
            for x in range(2):
                lower, upper = (
                    (0.5 * (mix_below + mix), mix),
                    (0.5 * (below + here), here),
                )[x]
                a = fine(2 * i + x, 2 * j, lower)
                b = fine(2 * i + x, 2 * j + 1, upper)
                for h in range(2):
                    value = jnp.concatenate([a[h], b[h]], axis=0)
                    top = value.astype(jnp.bfloat16)
                    rest = (value - top.astype(F32)).astype(jnp.bfloat16)
                    start = i * 2 * size + (x * OWN_Y + 2 * j) * 8
                    half = slice(h * LANES, h * LANES + LANES)
                    parts[start : start + 16, half] = top
                    parts[start + size : start + size + 16, half] = rest
        mixed = jnp.dot(
            parts[i * 2 * size : (i + 1) * 2 * size, :], perm, preferred_element_type=F32
        )
        for n in range(2 * OWN_Y):
            block = mixed[n * 8 : n * 8 + 8] + mixed[size + n * 8 : size + n * 8 + 8]
            col = i * 2 * OWN_Y + n
            o0[pl.ds(col, 8, stride=count), :] = block[:, :LANES]
            o1[pl.ds(col, 8, stride=count), :] = block[:, LANES:]
    out[:, :LANES] = o0[...]
    out[:, LANES:] = o1[...]


def vmem(*shape):
    return pltpu.VMEM(shape, F32)


SPEC = pl.BlockSpec(memory_space=pltpu.VMEM)
CELLS = PY * PX
SHARED = (vmem(PY, PX, LANES),) * 6 + (vmem(CELLS * 2, 8, LANES),) * 3 + (
    vmem(CELLS, 8, LANES),
) * 3
TABLES = [vmem(PY, PX, LANES)] * 6


def limit(mib):
    return pltpu.CompilerParams(vmem_limit_bytes=mib << 20)


def near_core(*arrays):
    return [pltpu.with_memory_space_constraint(a, pltpu.VMEM) for a in arrays]


def wave_call(real, imag, angles, picks, after):
    small = pl.BlockSpec(memory_space=pltpu.HBM)
    return pl.pallas_call(
        wave_kernel,
        out_shape=(vmem(CELLS * 2, 8, LANES), vmem(8, LANES)),
        in_specs=[small] * 4 + [SPEC],
        out_specs=(SPEC,) * 2,
        scratch_shapes=[
            pltpu.SMEM(a.shape, a.dtype) for a in (real, imag, angles, picks)
        ]
        + [pltpu.SemaphoreType.DMA((4,))],
        compiler_params=limit(6),
    )(
        *(pltpu.with_memory_space_constraint(a, pltpu.HBM) for a in (real, imag, angles, picks)),
        *near_core(after),
    )


def middle_call(sizes, labels, tab, wave):
    def kernel(*refs):
        middle_kernel(sizes, *refs)

    return pl.pallas_call(
        kernel,
        out_shape=SHARED,
        in_specs=[SPEC] * 3,
        out_specs=(SPEC,) * 12,
        scratch_shapes=TABLES + [vmem(2 * OWN_Y * PX, 2 * LANES)],
        compiler_params=limit(6),
    )(*near_core(labels, tab, wave))


def outer_call(sizes, low, high, tab, wave, shared):
    def kernel(*refs):
        outer_kernel(sizes, *refs)

    results = pl.pallas_call(
        kernel,
        out_shape=SHARED
        + (
            vmem(CX, CY, 8, LANES),
            vmem(2, CX, 16, LANES),
            vmem(SEND, 8, LANES),
            vmem(OWN_X * OWN_Y, 2, 8, LANES),
            vmem(4, 8, LANES),
        ),
        in_specs=[SPEC] * 16,
        out_specs=(SPEC,) * 17,
        input_output_aliases={4 + n: n for n in range(12)},
        scratch_shapes=TABLES + [vmem(LOW * PX, 2 * LANES)],
        compiler_params=limit(6),
    )(*near_core(low, high, tab, wave), *shared)
    return results[12:]


def cycle_call(*args):
    points = NI * NJ
    rows = OWN_X * OWN_Y * 8
    return pl.pallas_call(
        cycle_kernel,
        out_shape=jax.ShapeDtypeStruct((rows, 2 * LANES), F32),
        in_specs=[SPEC] * 5,
        out_specs=SPEC,
        scratch_shapes=[vmem(points, 8, LANES), vmem(2, NI, 16, LANES)]
        + [vmem(points, 8, LANES)] * 3
        + [pltpu.VMEM((2 * rows, 2 * LANES), jnp.bfloat16)]
        + [vmem(rows, LANES)] * 2,
        compiler_params=limit(8),
    )(*near_core(*args))


def complex_inverse(real, imag):
    modulus = real * real + imag * imag
    return real / modulus, -imag / modulus


def material_tables(er, ei):
    med_r = WAVE_SQUARED * (er + SHIFT_IMAG * ei)
    med_i = WAVE_SQUARED * (ei - SHIFT_IMAG * er)
    inv_r, inv_i = complex_inverse(128.0 / 30.0 - med_r, -med_i)
    src_r = SOURCE_GAIN * (er - 1.0)
    src_i = SOURCE_GAIN * ei
    ci_r, ci_i = complex_inverse(128.0 / 120.0 - med_r, -med_i)
    scale = 14.0 * DAMPING / 30.0
    return (
        scale * inv_r, scale * inv_i, 1.2 * src_r, 1.2 * src_i,
        DAMPING * ci_r, DAMPING * ci_i,
    )


def body(labels, permittivity_real, permittivity_imag, angles, angle_pick):
    gx_n = lax.axis_size("gx")
    gy_n = lax.axis_size("gy")
    core = lax.axis_index("gy") % 2
    is_low = core == 0

    def along_x(values, by):
        pairs = []
        for j in range(gy_n):
            step = by if j % 2 == 0 else -by
            for i in range(gx_n):
                if 0 <= i + step < gx_n:
                    pairs.append(((i + step) * gy_n + j, i * gy_n + j))
        return lax.ppermute(values, ("gx", "gy"), pairs)

    def along_y(values, by):
        pairs = [(j, j + by) for j in range(gy_n) if 0 <= j + by < gy_n]
        return lax.ppermute(values, "gy", pairs)

    def core_swap(values):
        return lax.ppermute(values, "gy", [(j, j ^ 1) for j in range(gy_n)])

    other = core_swap(labels)
    both = jnp.where(
        is_low,
        jnp.concatenate([labels, other], axis=1),
        jnp.concatenate([other, labels], axis=1),
    )
    both = with_layout_constraint(both, Layout((0, 1, 2)))
    far = along_x(jnp.where(is_low, both[:4], both[2:]), 2)
    near = along_x(both, 1)
    region = jnp.where(
        is_low,
        jnp.concatenate([both, near, far], axis=0),
        jnp.concatenate([far, near, both], axis=0),
    )
    region = jnp.transpose(region, (1, 0, 2))
    low = along_y(region[2 * OWN_Y - LOW :], 2)
    high = along_y(region[: PY - LOW - 2 * OWN_Y], -2)

    wave, table = wave_call(
        permittivity_real, permittivity_imag, angles, angle_pick, both
    )
    sizes = (OWN_X * gx_n, OWN_Y * gy_n)
    shared = middle_call(sizes, region, table, wave)
    c1, ck, send, it2, inv = outer_call(sizes, low, high, table, wave, shared)
    recv = core_swap(send)
    out = cycle_call(c1, ck, recv, it2, inv)
    return out.reshape(2, 4, OWN_X, OWN_Y, 2 * LANES)


def solution(mesh):
    return jax.shard_map(
        body,
        mesh=mesh,
        in_specs=(P("gx", "gy", None), P(), P(), P(), P()),
        out_specs=P(None, None, "gx", "gy", None),
        check_vma=False,
    )
```

```python
import jax
import jax.numpy as jnp
import numpy as np
from jax import lax
from jax.experimental import pallas as pl
from jax.experimental.pallas import tpu as pltpu
from jax.experimental.layout import Layout, with_layout_constraint
from jax.sharding import PartitionSpec as P

MAT = 8
DAMPING = 0.8
WAVE_SQUARED = 0.1
SHIFT_IMAG = 0.5
SOURCE_GAIN = 4.0

OWN_X = 6
OWN_Y = 8
PX = 16
PY = 35
LOW = 10
CX, CY = 5, 15
NI, NJ = 10, 11
LANES = 128
F32 = jnp.float32
OUTSIDE = 8
WAVENUMBER = float(np.sqrt(np.float32(WAVE_SQUARED)))


def lane_iota():
    return lax.broadcasted_iota(jnp.int32, (8, LANES), 1)


def sign_rows():
    rows = lax.broadcasted_iota(jnp.int32, (8, LANES), 0)
    return jnp.where(rows < 4, -1.0, 1.0).astype(F32)


def up(values, first):
    return jnp.where(first, 0.0, pltpu.roll(values, 1, 1))


def down(values, last):
    return jnp.where(last, 0.0, pltpu.roll(values, LANES - 1, 1))


def turned(values):
    return pltpu.roll(values, 4, 0)


def row_of(ref, y, x):
    return jnp.broadcast_to(ref[y, pl.ds(x, 1), :], (8, LANES))


def edge_face(values, near):
    edge = (3.0 / 14.0) * (values + (1.0 / 3.0) * near)
    face = values + (3.0 / 14.0) * near
    return edge, face


def where_am_i():
    gx = lax.axis_index("gx")
    gy = lax.axis_index("gy")
    core = lax.rem(gy, 2)
    x0 = OWN_X * gx - LOW * core
    y0 = OWN_Y * (gy - core) - LOW
    return core, x0, y0


def stay_kernel(labels, held, sem):
    copy = pltpu.make_async_copy(labels, held, sem)
    copy.start()
    copy.wait()


def splat(value):
    return jnp.full((8, LANES), value, F32)


def wave_kernel(
    real_in, imag_in, angles_in, picks_in, after, wave, tab, real, imag, angles, picks, sems
):
    del after
    copies = [
        pltpu.make_async_copy(src, dst, sems.at[n])
        for n, (src, dst) in enumerate(
            (
                (real_in, real),
                (imag_in, imag),
                (angles_in, angles),
                (picks_in, picks),
            )
        )
    ]
    for copy in copies:
        copy.start()
    for copy in copies:
        copy.wait()
    _, x0, y0 = where_am_i()
    lanes = lane_iota()
    rows = lax.broadcasted_iota(jnp.int32, (8, LANES), 0)

    er = jnp.zeros((8, LANES), F32)
    ei = jnp.zeros((8, LANES), F32)
    for m in range(MAT):
        er = jnp.where(lanes == m, splat(real[m]), er)
        ei = jnp.where(lanes == m, splat(imag[m]), ei)
    for n, table in enumerate(material_tables(er, ei)):
        tab[n : n + 1, :] = jnp.where(lanes < MAT, table, 0.0)[0:1]

    incidence = jnp.zeros((8, LANES), F32)
    for c in range(4):
        mine = jnp.bitwise_and(rows, 3) == c
        incidence = jnp.where(mine, splat(angles[picks[c]]), incidence)
    in_x = lanes < PX
    place = jnp.where(in_x, x0 + lanes, y0 + (lanes - PX)).astype(F32)
    slope = jnp.where(in_x, jnp.cos(incidence), jnp.sin(incidence))
    phases = WAVENUMBER * (slope * place)
    cosine = jnp.cos(phases)
    sine = jnp.sin(phases)
    upper = rows < 4
    front = jnp.where(upper, cosine, sine)
    turn = jnp.where(upper, -sine, cosine)

    def along(values, n):
        return jnp.broadcast_to(values[:, n : n + 1], (8, LANES))

    for x in range(PX):
        wave[x * 2] = along(cosine, x)
        wave[x * 2 + 1] = along(sine, x)
    for y in reversed(range(PY)):
        w = along(front, PX + y)
        w_t = along(turn, PX + y)
        for x in range(PX):
            c = wave[x * 2]
            s = wave[x * 2 + 1]
            wave[(y * PX + x) * 2] = c * w + s * w_t
            wave[(y * PX + x) * 2 + 1] = c * w_t - s * w


def row_loop(first, count, step, body):
    def some(n, carry):
        for k in range(step):
            body(first + n * step + k)
        return carry

    lax.fori_loop(0, count // step, some, 0)


class Region:
    def __init__(self, sizes, tab, wave, shared, scratch):
        self.nx, self.ny = sizes
        self.core, self.x0, self.y0 = where_am_i()
        self.tab = tab
        self.wave = wave
        (self.ie_r, self.io_r, self.ie_i, self.io_i, self.kr, self.ki,
         self.it1, self.pp, self.qq, self.va, self.vb, self.sy) = shared
        (self.ge_r, self.go_r, self.ge_i, self.go_i, self.sa_r, self.sa_i,
         self.apart) = scratch
        lanes = lane_iota()
        self.first = lanes == 0
        self.last = lanes == LANES - 1
        self.sgn = sign_rows()
        rows = lax.broadcasted_iota(jnp.int32, (2 * LANES, 2 * LANES), 0)
        cols = lax.broadcasted_iota(jnp.int32, (2 * LANES, 2 * LANES), 1)
        source = jnp.where(cols < LANES, 2 * cols, 2 * (cols - LANES) + 1)
        self.perm = jnp.where(rows == source, 1.0, 0.0).astype(jnp.bfloat16)

    def pick(self, row, index):
        table = jnp.broadcast_to(self.tab[row : row + 1, :], (8, LANES))
        return jnp.take_along_axis(table, index, axis=1, mode="promise_in_bounds")

    def tables(self, labels, first_row, count, step):
        flat = labels[...].reshape(count * PX, 2 * LANES).astype(F32).astype(jnp.bfloat16)
        self.apart[0 : count * PX, :] = jnp.dot(
            flat, self.perm, preferred_element_type=F32
        )
        rows = lax.broadcasted_iota(jnp.int32, (8, LANES), 0)
        inside = []
        for h in range(2):
            xs = self.x0 + 8 * h + rows
            inside.append(jnp.logical_and(xs >= 0, xs < self.nx))

        def some(n, carry):
            for k in range(step):
                y = first_row + n * step + k
                y_in = jnp.logical_and(self.y0 + y >= 0, self.y0 + y < self.ny)
                beyond = jnp.where(y_in, 0, OUTSIDE)
                for h in range(2):
                    start = pl.multiple_of((n * step + k) * PX + 8 * h, 8)
                    part = self.apart[pl.ds(start, 8), :]
                    at = (y, pl.ds(8 * h, 8), slice(None))
                    halves = []
                    for odd, (inv_r, inv_i, g_r, g_i) in enumerate(
                        (
                            (self.ie_r, self.ie_i, self.ge_r, self.ge_i),
                            (self.io_r, self.io_i, self.go_r, self.go_i),
                        )
                    ):
                        label = part[:, odd * LANES : (odd + 1) * LANES].astype(jnp.int32)
                        index = jnp.where(inside[h], label, OUTSIDE) + beyond
                        ir = self.pick(0, index)
                        ii = self.pick(1, index)
                        sr = self.pick(2, index)
                        si = self.pick(3, index)
                        inv_r[at] = ir
                        inv_i[at] = ii
                        g_r[at] = (25.0 / 14.0) * (ir * sr - ii * si)
                        g_i[at] = (25.0 / 14.0) * (ir * si + ii * sr)
                        halves.append((sr, si))
                        if odd and (first_row + k) % 2 == 1:
                            self.kr[at] = self.pick(4, index)
                            self.ki[at] = self.pick(5, index)
                    for c, out in ((0, self.sa_r), (1, self.sa_i)):
                        se = halves[0][c]
                        out[at] = se + down(se, self.last) + 2.0 * halves[1][c]
            return carry

        lax.fori_loop(0, count // step, some, 0)

    def first_stage(self, y):
        edges, faces, centres = [[], []], [[], []], [[], []]
        for x in range(PX):
            at = (y * PX + x) * 2
            e = self.wave[at]
            e_t = self.wave[at + 1]
            even = row_of(self.ge_r, y, x) * e + row_of(self.ge_i, y, x) * e_t
            odd = row_of(self.go_r, y, x) * e + row_of(self.go_i, y, x) * e_t
            if 2 <= x <= 12:
                self.sy[y * PX + x] = (
                    row_of(self.sa_r, y, x) * e + row_of(self.sa_i, y, x) * e_t
                )
            self.it1[at] = even
            self.it1[at + 1] = odd
            near_e = odd + up(odd, self.first)
            near_o = even + down(even, self.last)
            for h, (v, near) in enumerate(((even, near_e), (odd, near_o))):
                edge, face = edge_face(v, near)
                edges[h].append(edge)
                faces[h].append(face)
                centres[h].append(near)
        for x in range(PX):
            at = (y * PX + x) * 2
            for h in range(2):
                p = centres[h][x]
                q = faces[h][x]
                if 0 < x < PX - 1:
                    p = p + (faces[h][x - 1] + faces[h][x + 1])
                    q = q + (edges[h][x - 1] + edges[h][x + 1])
                else:
                    beside = x - 1 if x else x + 1
                    p = p + faces[h][beside]
                    q = q + edges[h][beside]
                self.pp[at + h] = p
                self.qq[at + h] = q

    def update(self, y, x, h):
        at = (y * PX + x) * 2 + h
        row = PX * 2
        ir, ii = ((self.ie_r, self.ie_i), (self.io_r, self.io_i))[h]
        n = self.pp[at] + (self.qq[at - row] + self.qq[at + row])
        return row_of(ir, y, x) * n + row_of(ii, y, x) * (self.sgn * turned(n))

    def second_stage(self, y):
        for x in range(1, 14):
            at = (y * PX + x) * 2
            we = 0.4 * self.it1[at] + self.update(y, x, 0)
            wo = 0.4 * self.it1[at + 1] + self.update(y, x, 1)
            p = we + down(we, self.last)
            half = p + wo
            after = jnp.where(self.last, -wo, pltpu.roll(wo, LANES - 1, 1))
            self.va[y * PX + x] = half + wo
            self.vb[y * PX + x] = (up(wo, self.first) + after) + 2.0 * half

    def third_stage(self, j, c1_out, ck_out):
        base = (2 + 2 * j) * PX
        gs, hs = {}, {}
        for x in range(1, 14):

            def combos(ref):
                vm, v0, v1, v2, v3 = (ref[base + (d - 1) * PX + x] for d in range(5))
                half = (v0 + v2) + v1
                return half + v1, (vm + v3) + 2.0 * half

            aa, ba = combos(self.va)
            ab, bb = combos(self.vb)
            u = ba + ab
            if 2 <= x <= 12:
                at = base + x
                gs[x] = (14.0 * u + 3.0 * bb) + (
                    (self.sy[at] + self.sy[at + 2 * PX]) + 2.0 * self.sy[at + PX]
                )
            hs[x] = 14.0 * aa + (3.0 * u + bb)
        for i in range(CX):
            b = 2 + 2 * i
            mx = jnp.where(self.x0 + b + 2 == self.nx, 1.0, 2.0).astype(F32)
            raw = (
                (gs[b] + gs[b + 2])
                + 2.0 * (gs[b + 1] + (hs[b] + hs[b + 2]))
                + (hs[b - 1] + hs[b + 3])
                + mx * hs[b + 1]
            ) * (1.0 / 1920.0)
            kr = row_of(self.kr, 3 + 2 * j, b + 1)
            ki = row_of(self.ki, 3 + 2 * j, b + 1)
            c1_out[i, j] = kr * raw + ki * (self.sgn * turned(raw))
            ck_out[0, i, pl.ds(j, 1), :] = self.kr[3 + 2 * j, b + 1 : b + 2, :]
            ck_out[1, i, pl.ds(j, 1), :] = self.ki[3 + 2 * j, b + 1 : b + 2, :]


def middle_kernel(sizes, labels, tab, wave, *refs):
    region = Region(sizes, tab, wave, refs[:12], refs[12:])
    region.tables(labels, LOW, 2 * OWN_Y, 8)
    row_loop(LOW, 2 * OWN_Y, 4, region.first_stage)
    row_loop(LOW + 1, 2 * OWN_Y - 2, 7, region.second_stage)


def low_kernel(sizes, labels, tab, wave, *refs):
    region = Region(sizes, tab, wave, refs[12:24], refs[24:])
    region.tables(labels, 0, LOW, LOW)
    row_loop(0, LOW, 5, region.first_stage)
    row_loop(1, LOW, 5, region.second_stage)


def high_kernel(sizes, labels, tab, wave, *refs):
    region = Region(sizes, tab, wave, refs[12:24], refs[29:])
    c1_out, ck_out, send_out, it2_out, inv_out = refs[24:29]
    core, y0, ny = region.core, region.y0, region.ny
    it1 = region.it1
    top = LOW + 2 * OWN_Y
    region.tables(labels, top, PY - top, PY - top)
    row_loop(top, PY - top, 3, region.first_stage)
    row_loop(top - 1, PY - top, 3, region.second_stage)

    @pl.when(y0 + top == ny)
    def _():
        for x in range(1, 14):
            for ref in (region.va, region.vb):
                ref[(top + 1) * PX + x] = -ref[(top - 1) * PX + x]

    for k in range(2):
        for i in range(CX):
            ck_out[k, i, 8:16, :] = jnp.zeros((8, LANES), F32)
    row_loop(0, CY, 1, lambda j: region.third_stage(j, c1_out, ck_out))

    xb = core * LOW
    yb = LOW + core * OWN_Y
    xe = core * (PX - 1)
    tables = (region.ie_r, region.io_r, region.ie_i, region.io_i)

    def own_stage(k):
        y = yb + k
        for xx in range(OWN_X):
            x = xb + xx
            at = (y * PX + x) * 2
            for h in range(2):
                it2_out[xx * OWN_Y + k, h] = 1.2 * it1[at + h] + region.update(y, x, h)
        for n, ref in enumerate(tables):
            inv_out[n, pl.ds(k, 1), :] = ref[y, pl.ds(xe, 1), :]

    row_loop(0, OWN_Y, 2, own_stage)

    j0 = 4 - 4 * core
    for i in range(CX):
        for j in range(NJ):
            send_out[i * NJ + j] = c1_out[i, j0 + j]
        for k in range(2):
            send_out[CX * NJ + (k * CX + i) * 2] = ck_out[k, i, 0:8, :]
            send_out[CX * NJ + (k * CX + i) * 2 + 1] = ck_out[k, i, 8:16, :]
    plane = 6 + 3 * core
    ys = LOW + OWN_Y - core * OWN_Y
    edges, faces = [], []
    for k in range(OWN_Y + 2):
        at = ((ys - 1 + k) * PX + plane) * 2
        even = it1[at]
        odd = it1[at + 1]
        ee, fe = edge_face(even, odd + up(odd, region.first))
        eo, fo = edge_face(odd, even + down(even, region.last))
        edges.append((ee, eo))
        faces.append((fe, fo))
    for k in range(OWN_Y):
        for h in range(2):
            send_out[CX * NJ + 4 * CX + 2 * k + h] = faces[k + 1][h] + (
                edges[k][h] + edges[k + 2][h]
            )


SEND = CX * NJ + 4 * CX + 2 * OWN_Y


def cycle_kernel(c1_own, ck_own, recv, it2, inv, out, c1, ck, cc, pp, qq, parts, o0, o1):
    core = where_am_i()[0]
    lanes = lane_iota()
    first = lanes == 0
    last = lanes == LANES - 1
    sgn = sign_rows()
    j0 = 4 * core

    def spread(row):
        return jnp.broadcast_to(row, (8, LANES))

    def assemble(which):
        own_i, other_i = CX - which * CX, which * CX
        for i in range(CX):
            for j in range(NJ):
                c1[(own_i + i) * NJ + j] = c1_own[i, 4 * which + j]
                c1[(other_i + i) * NJ + j] = recv[i * NJ + j]
            for k in range(2):
                for h in range(2):
                    tile = slice(8 * h, 8 * h + 8)
                    ck[k, own_i + i, tile, :] = ck_own[k, i, tile, :]
                    ck[k, other_i + i, tile, :] = recv[CX * NJ + (k * CX + i) * 2 + h]

    @pl.when(core == 0)
    def _():
        assemble(0)

    @pl.when(core == 1)
    def _():
        assemble(1)

    for sweep, (sum_step, relax_step) in enumerate(((5, 4), (4, 3), (3, 4))):
        ref = c1 if sweep == 0 else cc

        def sums(i, ref=ref, sweep=sweep):
            edges, faces, centres = {}, {}, {}
            for j in range(sweep, NJ - sweep):
                v = ref[i * NJ + j]
                near = up(v, first) + down(v, last)
                edges[j], faces[j] = edge_face(v, near)
                centres[j] = near
            for j in range(sweep + 1, NJ - sweep - 1):
                pp[i * NJ + j] = centres[j] + (faces[j - 1] + faces[j + 1])
                qq[i * NJ + j] = faces[j] + (edges[j - 1] + edges[j + 1])

        row_loop(sweep, NI - 2 * sweep, sum_step, sums)

        def relax(i, ref=ref, sweep=sweep):
            for j in range(sweep + 1, NJ - sweep - 1):
                at = i * NJ + j
                n = (pp[at] + (qq[at - NJ] + qq[at + NJ])) * (14.0 / 120.0)
                kr = spread(ck[0, i, pl.ds(j0 + j, 1), :])
                ki = spread(ck[1, i, pl.ds(j0 + j, 1), :])
                cc[at] = (0.2 * ref[at] + c1[at]) + (kr * n + ki * (sgn * turned(n)))

        row_loop(sweep + 1, NI - 2 * sweep - 2, relax_step, relax)

    flags = {0: jnp.where(core == 0, 1.0, 0.0), OWN_X - 1: jnp.where(core == 1, 1.0, 0.0)}
    added = []
    for k in range(OWN_Y):
        pair = []
        for h in range(2):
            n = recv[CX * NJ + 4 * CX + 2 * k + h]
            ir = spread(inv[h, k : k + 1, :])
            ii = spread(inv[2 + h, k : k + 1, :])
            pair.append(ir * n + ii * (sgn * turned(n)))
        added.append(pair)

    rows = lax.broadcasted_iota(jnp.int32, (2 * LANES, 2 * LANES), 0)
    cols = lax.broadcasted_iota(jnp.int32, (2 * LANES, 2 * LANES), 1)
    target = jnp.where(rows < LANES, 2 * rows, 2 * (rows - LANES) + 1)
    perm = jnp.where(cols == target, 1.0, 0.0).astype(jnp.bfloat16)
    count = OWN_X * OWN_Y

    def fine(x, y, value):
        col = x * OWN_Y + y
        even = it2[col, 0] + 0.5 * (value + up(value, first))
        odd = it2[col, 1] + value
        if x in flags:
            even = even + flags[x] * added[y][0]
            odd = odd + flags[x] * added[y][1]
        return even, odd

    size = 2 * OWN_Y * 8
    for i in range(OWN_X // 2):
        for j in range(OWN_Y // 2):
            at = (i + 4) * NJ + j + 4
            here = cc[at]
            left = cc[at - NJ]
            mix = 0.5 * (left + here)
            below = cc[at - 1]
            mix_below = 0.5 * (cc[at - NJ - 1] + below)
            for x in range(2):
                lower, upper = (
                    (0.5 * (mix_below + mix), mix),
                    (0.5 * (below + here), here),
                )[x]
                a = fine(2 * i + x, 2 * j, lower)
                b = fine(2 * i + x, 2 * j + 1, upper)
                for h in range(2):
                    value = jnp.concatenate([a[h], b[h]], axis=0)
                    top = value.astype(jnp.bfloat16)
                    rest = (value - top.astype(F32)).astype(jnp.bfloat16)
                    start = i * 2 * size + (x * OWN_Y + 2 * j) * 8
                    half = slice(h * LANES, h * LANES + LANES)
                    parts[start : start + 16, half] = top
                    parts[start + size : start + size + 16, half] = rest
        mixed = jnp.dot(
            parts[i * 2 * size : (i + 1) * 2 * size, :], perm, preferred_element_type=F32
        )
        for n in range(2 * OWN_Y):
            block = mixed[n * 8 : n * 8 + 8] + mixed[size + n * 8 : size + n * 8 + 8]
            col = i * 2 * OWN_Y + n
            o0[pl.ds(col, 8, stride=count), :] = block[:, :LANES]
            o1[pl.ds(col, 8, stride=count), :] = block[:, LANES:]
    out[:, :LANES] = o0[...]
    out[:, LANES:] = o1[...]


def vmem(*shape):
    return pltpu.VMEM(shape, F32)


SPEC = pl.BlockSpec(memory_space=pltpu.VMEM)
CELLS = PY * PX
SHARED = (vmem(PY, PX, LANES),) * 6 + (vmem(CELLS * 2, 8, LANES),) * 3 + (
    vmem(CELLS, 8, LANES),
) * 3
TABLES = [vmem(PY, PX, LANES)] * 6


def limit(mib):
    return pltpu.CompilerParams(vmem_limit_bytes=mib << 20)


def near_core(*arrays):
    return [pltpu.with_memory_space_constraint(a, pltpu.VMEM) for a in arrays]


def stay_call(labels):
    return pl.pallas_call(
        stay_kernel,
        out_shape=pltpu.VMEM(labels.shape, labels.dtype),
        in_specs=[pl.BlockSpec(memory_space=pltpu.HBM)],
        out_specs=SPEC,
        scratch_shapes=[pltpu.SemaphoreType.DMA(())],
        compiler_params=limit(1),
    )(pltpu.with_memory_space_constraint(labels, pltpu.HBM))


def wave_call(real, imag, angles, picks, after):
    small = pl.BlockSpec(memory_space=pltpu.HBM)
    return pl.pallas_call(
        wave_kernel,
        out_shape=(vmem(CELLS * 2, 8, LANES), vmem(8, LANES)),
        in_specs=[small] * 4 + [SPEC],
        out_specs=(SPEC,) * 2,
        scratch_shapes=[
            pltpu.SMEM(a.shape, a.dtype) for a in (real, imag, angles, picks)
        ]
        + [pltpu.SemaphoreType.DMA((4,))],
        compiler_params=limit(6),
    )(
        *(pltpu.with_memory_space_constraint(a, pltpu.HBM) for a in (real, imag, angles, picks)),
        *near_core(after),
    )


def middle_call(sizes, labels, tab, wave):
    def kernel(*refs):
        middle_kernel(sizes, *refs)

    return pl.pallas_call(
        kernel,
        out_shape=SHARED,
        in_specs=[SPEC] * 3,
        out_specs=(SPEC,) * 12,
        scratch_shapes=TABLES + [vmem(2 * OWN_Y * PX, 2 * LANES)],
        compiler_params=limit(6),
    )(*near_core(labels, tab, wave))


def low_call(sizes, labels, tab, wave, shared):
    def kernel(*refs):
        low_kernel(sizes, *refs)

    return pl.pallas_call(
        kernel,
        out_shape=SHARED,
        in_specs=[SPEC] * 15,
        out_specs=(SPEC,) * 12,
        input_output_aliases={3 + n: n for n in range(12)},
        scratch_shapes=TABLES + [vmem(LOW * PX, 2 * LANES)],
        compiler_params=limit(6),
    )(*near_core(labels, tab, wave), *shared)


def high_call(sizes, labels, tab, wave, shared):
    def kernel(*refs):
        high_kernel(sizes, *refs)

    results = pl.pallas_call(
        kernel,
        out_shape=SHARED
        + (
            vmem(CX, CY, 8, LANES),
            vmem(2, CX, 16, LANES),
            vmem(SEND, 8, LANES),
            vmem(OWN_X * OWN_Y, 2, 8, LANES),
            vmem(4, 8, LANES),
        ),
        in_specs=[SPEC] * 15,
        out_specs=(SPEC,) * 17,
        input_output_aliases={3 + n: n for n in range(12)},
        scratch_shapes=TABLES + [vmem(LOW * PX, 2 * LANES)],
        compiler_params=limit(6),
    )(*near_core(labels, tab, wave), *shared)
    return results[12:]


def cycle_call(*args):
    points = NI * NJ
    rows = OWN_X * OWN_Y * 8
    return pl.pallas_call(
        cycle_kernel,
        out_shape=jax.ShapeDtypeStruct((rows, 2 * LANES), F32),
        in_specs=[SPEC] * 5,
        out_specs=SPEC,
        scratch_shapes=[vmem(points, 8, LANES), vmem(2, NI, 16, LANES)]
        + [vmem(points, 8, LANES)] * 3
        + [pltpu.VMEM((2 * rows, 2 * LANES), jnp.bfloat16)]
        + [vmem(rows, LANES)] * 2,
        compiler_params=limit(8),
    )(*near_core(*args))


def complex_inverse(real, imag):
    modulus = real * real + imag * imag
    return real / modulus, -imag / modulus


def material_tables(er, ei):
    med_r = WAVE_SQUARED * (er + SHIFT_IMAG * ei)
    med_i = WAVE_SQUARED * (ei - SHIFT_IMAG * er)
    inv_r, inv_i = complex_inverse(128.0 / 30.0 - med_r, -med_i)
    src_r = SOURCE_GAIN * (er - 1.0)
    src_i = SOURCE_GAIN * ei
    ci_r, ci_i = complex_inverse(128.0 / 120.0 - med_r, -med_i)
    scale = 14.0 * DAMPING / 30.0
    return (
        scale * inv_r, scale * inv_i, 1.2 * src_r, 1.2 * src_i,
        DAMPING * ci_r, DAMPING * ci_i,
    )


def body(labels, permittivity_real, permittivity_imag, angles, angle_pick):
    gx_n = lax.axis_size("gx")
    gy_n = lax.axis_size("gy")
    core = lax.axis_index("gy") % 2
    is_low = core == 0

    def along_x(values, by):
        pairs = []
        for j in range(gy_n):
            step = by if j % 2 == 0 else -by
            for i in range(gx_n):
                if 0 <= i + step < gx_n:
                    pairs.append(((i + step) * gy_n + j, i * gy_n + j))
        return lax.ppermute(values, ("gx", "gy"), pairs)

    def along_y(values, by):
        pairs = [(j, j + by) for j in range(gy_n) if 0 <= j + by < gy_n]
        return lax.ppermute(values, "gy", pairs)

    def core_swap(values):
        return lax.ppermute(values, "gy", [(j, j ^ 1) for j in range(gy_n)])

    other = core_swap(labels)
    labels = stay_call(labels)
    both = jnp.where(
        is_low,
        jnp.concatenate([labels, other], axis=1),
        jnp.concatenate([other, labels], axis=1),
    )
    both = with_layout_constraint(both, Layout((0, 1, 2)))
    far = along_x(jnp.where(is_low, both[:4], both[2:]), 2)
    near = along_x(both, 1)
    near = with_layout_constraint(near, Layout((0, 1, 2)))
    far = with_layout_constraint(far, Layout((0, 1, 2)))
    region = jnp.where(
        is_low,
        jnp.concatenate([both, near, far], axis=0),
        jnp.concatenate([far, near, both], axis=0),
    )
    region = jnp.transpose(region, (1, 0, 2))
    low = along_y(region[2 * OWN_Y - LOW :], 2)
    high = along_y(region[: PY - LOW - 2 * OWN_Y], -2)

    wave, table = wave_call(
        permittivity_real, permittivity_imag, angles, angle_pick, both
    )
    sizes = (OWN_X * gx_n, OWN_Y * gy_n)
    shared = middle_call(sizes, region, table, wave)
    shared = low_call(sizes, low, table, wave, shared)
    c1, ck, send, it2, inv = high_call(sizes, high, table, wave, shared)
    recv = core_swap(send)
    out = cycle_call(c1, ck, recv, it2, inv)
    return out.reshape(2, 4, OWN_X, OWN_Y, 2 * LANES)


def solution(mesh):
    return jax.shard_map(
        body,
        mesh=mesh,
        in_specs=(P("gx", "gy", None), P(), P(), P(), P()),
        out_specs=P(None, None, "gx", "gy", None),
        check_vma=False,
    )
```

```python
import jax
import jax.numpy as jnp
import numpy as np
from jax import lax
from jax.experimental import pallas as pl
from jax.experimental.pallas import tpu as pltpu
from jax.experimental.layout import Layout, with_layout_constraint
from jax.sharding import PartitionSpec as P

MAT = 8
DAMPING = 0.8
WAVE_SQUARED = 0.1
SHIFT_IMAG = 0.5
SOURCE_GAIN = 4.0

OWN_X = 6
OWN_Y = 8
PX = 16
PY = 35
LOW = 10
CX, CY = 5, 15
NI, NJ = 10, 11
LANES = 128
F32 = jnp.float32
OUTSIDE = 8
WAVENUMBER = float(np.sqrt(np.float32(WAVE_SQUARED)))


def lane_iota():
    return lax.broadcasted_iota(jnp.int32, (8, LANES), 1)


def sign_rows():
    rows = lax.broadcasted_iota(jnp.int32, (8, LANES), 0)
    return jnp.where(rows < 4, -1.0, 1.0).astype(F32)


def up(values, first):
    return jnp.where(first, 0.0, pltpu.roll(values, 1, 1))


def down(values, last):
    return jnp.where(last, 0.0, pltpu.roll(values, LANES - 1, 1))


def turned(values):
    return pltpu.roll(values, 4, 0)


def row_of(ref, y, x):
    return jnp.broadcast_to(ref[y, pl.ds(x, 1), :], (8, LANES))


def edge_face(values, near):
    edge = (3.0 / 14.0) * (values + (1.0 / 3.0) * near)
    face = values + (3.0 / 14.0) * near
    return edge, face


def where_am_i():
    gx = lax.axis_index("gx")
    gy = lax.axis_index("gy")
    core = lax.rem(gy, 2)
    x0 = OWN_X * gx - LOW * core
    y0 = OWN_Y * (gy - core) - LOW
    return core, x0, y0


def stay_kernel(labels, held, sem):
    copy = pltpu.make_async_copy(labels, held, sem)
    copy.start()
    copy.wait()


def splat(value):
    return jnp.full((8, LANES), value, F32)


def wave_kernel(
    real_in, imag_in, angles_in, picks_in, after, wave, tab, real, imag, angles, picks, sems
):
    del after
    copies = [
        pltpu.make_async_copy(src, dst, sems.at[n])
        for n, (src, dst) in enumerate(
            (
                (real_in, real),
                (imag_in, imag),
                (angles_in, angles),
                (picks_in, picks),
            )
        )
    ]
    for copy in copies:
        copy.start()
    for copy in copies:
        copy.wait()
    _, x0, y0 = where_am_i()
    lanes = lane_iota()
    rows = lax.broadcasted_iota(jnp.int32, (8, LANES), 0)

    er = jnp.zeros((8, LANES), F32)
    ei = jnp.zeros((8, LANES), F32)
    for m in range(MAT):
        er = jnp.where(lanes == m, splat(real[m]), er)
        ei = jnp.where(lanes == m, splat(imag[m]), ei)
    for n, table in enumerate(material_tables(er, ei)):
        tab[n : n + 1, :] = jnp.where(lanes < MAT, table, 0.0)[0:1]

    incidence = jnp.zeros((8, LANES), F32)
    for c in range(4):
        mine = jnp.bitwise_and(rows, 3) == c
        incidence = jnp.where(mine, splat(angles[picks[c]]), incidence)
    in_x = lanes < PX
    place = jnp.where(in_x, x0 + lanes, y0 + (lanes - PX)).astype(F32)
    slope = jnp.where(in_x, jnp.cos(incidence), jnp.sin(incidence))
    phases = WAVENUMBER * (slope * place)
    cosine = jnp.cos(phases)
    sine = jnp.sin(phases)
    upper = rows < 4
    front = jnp.where(upper, cosine, sine)
    turn = jnp.where(upper, -sine, cosine)

    def along(values, n):
        return jnp.broadcast_to(values[:, n : n + 1], (8, LANES))

    for x in range(PX):
        wave[x * 2] = along(cosine, x)
        wave[x * 2 + 1] = along(sine, x)
    for y in reversed(range(PY)):
        w = along(front, PX + y)
        w_t = along(turn, PX + y)
        for x in range(PX):
            c = wave[x * 2]
            s = wave[x * 2 + 1]
            wave[(y * PX + x) * 2] = c * w + s * w_t
            wave[(y * PX + x) * 2 + 1] = c * w_t - s * w


def row_loop(first, count, step, body):
    def some(n, carry):
        for k in range(step):
            body(first + n * step + k)
        return carry

    lax.fori_loop(0, count // step, some, 0)


class Region:
    def __init__(self, sizes, tab, wave, shared, scratch):
        self.nx, self.ny = sizes
        self.core, self.x0, self.y0 = where_am_i()
        self.tab = tab
        self.wave = wave
        (self.ie_r, self.io_r, self.ie_i, self.io_i, self.kr, self.ki,
         self.it1, self.pp, self.qq, self.va, self.vb, self.sy) = shared
        (self.ge_r, self.go_r, self.ge_i, self.go_i, self.sa_r, self.sa_i,
         self.apart) = scratch
        lanes = lane_iota()
        self.first = lanes == 0
        self.last = lanes == LANES - 1
        self.sgn = sign_rows()
        rows = lax.broadcasted_iota(jnp.int32, (2 * LANES, 2 * LANES), 0)
        cols = lax.broadcasted_iota(jnp.int32, (2 * LANES, 2 * LANES), 1)
        source = jnp.where(cols < LANES, 2 * cols, 2 * (cols - LANES) + 1)
        self.perm = jnp.where(rows == source, 1.0, 0.0).astype(jnp.bfloat16)

    def pick(self, row, index):
        table = jnp.broadcast_to(self.tab[row : row + 1, :], (8, LANES))
        return jnp.take_along_axis(table, index, axis=1, mode="promise_in_bounds")

    def tables(self, labels, first_row, count, step):
        flat = labels[...].reshape(count * PX, 2 * LANES).astype(F32).astype(jnp.bfloat16)
        self.apart[0 : count * PX, :] = jnp.dot(
            flat, self.perm, preferred_element_type=F32
        )
        rows = lax.broadcasted_iota(jnp.int32, (8, LANES), 0)
        inside = []
        for h in range(2):
            xs = self.x0 + 8 * h + rows
            inside.append(jnp.logical_and(xs >= 0, xs < self.nx))

        def some(n, carry):
            for k in range(step):
                y = first_row + n * step + k
                y_in = jnp.logical_and(self.y0 + y >= 0, self.y0 + y < self.ny)
                beyond = jnp.where(y_in, 0, OUTSIDE)
                for h in range(2):
                    start = pl.multiple_of((n * step + k) * PX + 8 * h, 8)
                    part = self.apart[pl.ds(start, 8), :]
                    at = (y, pl.ds(8 * h, 8), slice(None))
                    halves = []
                    for odd, (inv_r, inv_i, g_r, g_i) in enumerate(
                        (
                            (self.ie_r, self.ie_i, self.ge_r, self.ge_i),
                            (self.io_r, self.io_i, self.go_r, self.go_i),
                        )
                    ):
                        label = part[:, odd * LANES : (odd + 1) * LANES].astype(jnp.int32)
                        index = jnp.where(inside[h], label, OUTSIDE) + beyond
                        ir = self.pick(0, index)
                        ii = self.pick(1, index)
                        sr = self.pick(2, index)
                        si = self.pick(3, index)
                        inv_r[at] = ir
                        inv_i[at] = ii
                        g_r[at] = (25.0 / 14.0) * (ir * sr - ii * si)
                        g_i[at] = (25.0 / 14.0) * (ir * si + ii * sr)
                        halves.append((sr, si))
                        if odd and (first_row + k) % 2 == 1:
                            self.kr[at] = self.pick(4, index)
                            self.ki[at] = self.pick(5, index)
                    for c, out in ((0, self.sa_r), (1, self.sa_i)):
                        se = halves[0][c]
                        out[at] = se + down(se, self.last) + 2.0 * halves[1][c]
            return carry

        lax.fori_loop(0, count // step, some, 0)

    def first_stage(self, y):
        edges, faces, centres = [[], []], [[], []], [[], []]
        for x in range(PX):
            at = (y * PX + x) * 2
            e = self.wave[at]
            e_t = self.wave[at + 1]
            even = row_of(self.ge_r, y, x) * e + row_of(self.ge_i, y, x) * e_t
            odd = row_of(self.go_r, y, x) * e + row_of(self.go_i, y, x) * e_t
            if 2 <= x <= 12:
                self.sy[y * PX + x] = (
                    row_of(self.sa_r, y, x) * e + row_of(self.sa_i, y, x) * e_t
                )
            self.it1[at] = even
            self.it1[at + 1] = odd
            near_e = odd + up(odd, self.first)
            near_o = even + down(even, self.last)
            for h, (v, near) in enumerate(((even, near_e), (odd, near_o))):
                edge, face = edge_face(v, near)
                edges[h].append(edge)
                faces[h].append(face)
                centres[h].append(near)
        for x in range(PX):
            at = (y * PX + x) * 2
            for h in range(2):
                p = centres[h][x]
                q = faces[h][x]
                if 0 < x < PX - 1:
                    p = p + (faces[h][x - 1] + faces[h][x + 1])
                    q = q + (edges[h][x - 1] + edges[h][x + 1])
                else:
                    beside = x - 1 if x else x + 1
                    p = p + faces[h][beside]
                    q = q + edges[h][beside]
                self.pp[at + h] = p
                self.qq[at + h] = q

    def update(self, y, x, h):
        at = (y * PX + x) * 2 + h
        row = PX * 2
        ir, ii = ((self.ie_r, self.ie_i), (self.io_r, self.io_i))[h]
        n = self.pp[at] + (self.qq[at - row] + self.qq[at + row])
        return row_of(ir, y, x) * n + row_of(ii, y, x) * (self.sgn * turned(n))

    def second_stage(self, y):
        for x in range(1, 14):
            at = (y * PX + x) * 2
            we = 0.4 * self.it1[at] + self.update(y, x, 0)
            wo = 0.4 * self.it1[at + 1] + self.update(y, x, 1)
            p = we + down(we, self.last)
            half = p + wo
            after = jnp.where(self.last, -wo, pltpu.roll(wo, LANES - 1, 1))
            self.va[y * PX + x] = half + wo
            self.vb[y * PX + x] = (up(wo, self.first) + after) + 2.0 * half

    def third_stage(self, j, c1_out, ck_out):
        base = (2 + 2 * j) * PX
        gs, hs = {}, {}
        for x in range(1, 14):

            def combos(ref):
                vm, v0, v1, v2, v3 = (ref[base + (d - 1) * PX + x] for d in range(5))
                half = (v0 + v2) + v1
                return half + v1, (vm + v3) + 2.0 * half

            aa, ba = combos(self.va)
            ab, bb = combos(self.vb)
            u = ba + ab
            if 2 <= x <= 12:
                at = base + x
                gs[x] = (14.0 * u + 3.0 * bb) + (
                    (self.sy[at] + self.sy[at + 2 * PX]) + 2.0 * self.sy[at + PX]
                )
            hs[x] = 14.0 * aa + (3.0 * u + bb)
        for i in range(CX):
            b = 2 + 2 * i
            mx = jnp.where(self.x0 + b + 2 == self.nx, 1.0, 2.0).astype(F32)
            raw = (
                (gs[b] + gs[b + 2])
                + 2.0 * (gs[b + 1] + (hs[b] + hs[b + 2]))
                + (hs[b - 1] + hs[b + 3])
                + mx * hs[b + 1]
            ) * (1.0 / 1920.0)
            kr = row_of(self.kr, 3 + 2 * j, b + 1)
            ki = row_of(self.ki, 3 + 2 * j, b + 1)
            c1_out[i, j] = kr * raw + ki * (self.sgn * turned(raw))
            ck_out[0, i, pl.ds(j, 1), :] = self.kr[3 + 2 * j, b + 1 : b + 2, :]
            ck_out[1, i, pl.ds(j, 1), :] = self.ki[3 + 2 * j, b + 1 : b + 2, :]


def middle_kernel(sizes, labels, tab, wave, *refs):
    region = Region(sizes, tab, wave, refs[:12], refs[12:])
    region.tables(labels, LOW, 2 * OWN_Y, 8)
    row_loop(LOW, 2 * OWN_Y, 4, region.first_stage)
    row_loop(LOW + 1, 2 * OWN_Y - 2, 7, region.second_stage)


def low_kernel(sizes, labels, tab, wave, *refs):
    region = Region(sizes, tab, wave, refs[12:24], refs[24:])
    region.tables(labels, 0, LOW, LOW)
    row_loop(0, LOW, 5, region.first_stage)
    row_loop(1, LOW, 5, region.second_stage)


def high_kernel(sizes, labels, tab, wave, *refs):
    region = Region(sizes, tab, wave, refs[12:24], refs[27:])
    c1_out, ck_out, send_out = refs[24:27]
    core, y0, ny = region.core, region.y0, region.ny
    it1 = region.it1
    top = LOW + 2 * OWN_Y
    region.tables(labels, top, PY - top, PY - top)
    row_loop(top, PY - top, 3, region.first_stage)
    row_loop(top - 1, PY - top, 3, region.second_stage)

    @pl.when(y0 + top == ny)
    def _():
        for x in range(1, 14):
            for ref in (region.va, region.vb):
                ref[(top + 1) * PX + x] = -ref[(top - 1) * PX + x]

    for k in range(2):
        for i in range(CX):
            ck_out[k, i, 8:16, :] = jnp.zeros((8, LANES), F32)
    row_loop(0, CY, 3, lambda j: region.third_stage(j, c1_out, ck_out))

    j0 = 4 - 4 * core
    for i in range(CX):
        for j in range(NJ):
            send_out[i * NJ + j] = c1_out[i, j0 + j]
        for k in range(2):
            send_out[CX * NJ + (k * CX + i) * 2] = ck_out[k, i, 0:8, :]
            send_out[CX * NJ + (k * CX + i) * 2 + 1] = ck_out[k, i, 8:16, :]
    plane = 6 + 3 * core
    ys = LOW + OWN_Y - core * OWN_Y
    edges, faces = [], []
    for k in range(OWN_Y + 2):
        at = ((ys - 1 + k) * PX + plane) * 2
        even = it1[at]
        odd = it1[at + 1]
        ee, fe = edge_face(even, odd + up(odd, region.first))
        eo, fo = edge_face(odd, even + down(even, region.last))
        edges.append((ee, eo))
        faces.append((fe, fo))
    for k in range(OWN_Y):
        for h in range(2):
            send_out[CX * NJ + 4 * CX + 2 * k + h] = faces[k + 1][h] + (
                edges[k][h] + edges[k + 2][h]
            )


SEND = CX * NJ + 4 * CX + 2 * OWN_Y


class Own(Region):
    def __init__(self, refs):
        (self.ie_r, self.io_r, self.ie_i, self.io_i, self.it1, self.pp, self.qq) = refs
        self.sgn = sign_rows()


def coarse_sums(ref, pp, qq, i, sweep, first, last):
    edges, faces, centres = {}, {}, {}
    for j in range(sweep, NJ - sweep):
        v = ref[i * NJ + j]
        near = up(v, first) + down(v, last)
        edges[j], faces[j] = edge_face(v, near)
        centres[j] = near
    for j in range(sweep + 1, NJ - sweep - 1):
        pp[i * NJ + j] = centres[j] + (faces[j - 1] + faces[j + 1])
        qq[i * NJ + j] = faces[j] + (edges[j - 1] + edges[j + 1])


def own_kernel(*refs):
    own = Own(refs[:7])
    c1_own, ck_own, it2, inv, c1, ck, pp, qq = refs[7:]
    core = where_am_i()[0]
    lanes = lane_iota()
    first = lanes == 0
    last = lanes == LANES - 1

    xb = core * LOW
    yb = LOW + core * OWN_Y
    xe = core * (PX - 1)
    tables = (own.ie_r, own.io_r, own.ie_i, own.io_i)

    def own_stage(k):
        y = yb + k
        for xx in range(OWN_X):
            x = xb + xx
            at = (y * PX + x) * 2
            for h in range(2):
                it2[xx * OWN_Y + k, h] = 1.2 * own.it1[at + h] + own.update(y, x, h)
        for n, ref in enumerate(tables):
            inv[n, pl.ds(k, 1), :] = ref[y, pl.ds(xe, 1), :]

    own_i = CX - core * CX
    for i in range(CX):
        for j in range(NJ):
            c1[(own_i + i) * NJ + j] = c1_own[i, 4 * core + j]
        for k in range(2):
            ck[k, own_i + i] = ck_own[k, i]
    row_loop(
        own_i, CX, 5, lambda i: coarse_sums(c1, pp, qq, i, 0, first, last)
    )
    row_loop(0, OWN_Y, 2, own_stage)


def cycle_kernel(recv, it2, inv, *refs):
    c1, ck, pp, qq, out, cc, parts, o0, o1 = refs[4:]
    core = where_am_i()[0]
    lanes = lane_iota()
    first = lanes == 0
    last = lanes == LANES - 1
    sgn = sign_rows()
    j0 = 4 * core
    other_i = core * CX

    def spread(row):
        return jnp.broadcast_to(row, (8, LANES))

    for i in range(CX):
        for j in range(NJ):
            c1[(other_i + i) * NJ + j] = recv[i * NJ + j]
        for k in range(2):
            for h in range(2):
                tile = slice(8 * h, 8 * h + 8)
                ck[k, other_i + i, tile, :] = recv[CX * NJ + (k * CX + i) * 2 + h]

    for sweep, (sum_step, relax_step) in enumerate(((5, 4), (4, 3), (3, 4))):
        ref = c1 if sweep == 0 else cc

        def sums(i, ref=ref, sweep=sweep):
            coarse_sums(ref, pp, qq, i, sweep, first, last)

        if sweep:
            row_loop(sweep, NI - 2 * sweep, sum_step, sums)
        else:
            row_loop(other_i, CX, sum_step, sums)

        def relax(i, ref=ref, sweep=sweep):
            for j in range(sweep + 1, NJ - sweep - 1):
                at = i * NJ + j
                n = (pp[at] + (qq[at - NJ] + qq[at + NJ])) * (14.0 / 120.0)
                kr = spread(ck[0, i, pl.ds(j0 + j, 1), :])
                ki = spread(ck[1, i, pl.ds(j0 + j, 1), :])
                cc[at] = (0.2 * ref[at] + c1[at]) + (kr * n + ki * (sgn * turned(n)))

        row_loop(sweep + 1, NI - 2 * sweep - 2, relax_step, relax)

    flags = {0: jnp.where(core == 0, 1.0, 0.0), OWN_X - 1: jnp.where(core == 1, 1.0, 0.0)}
    added = []
    for k in range(OWN_Y):
        pair = []
        for h in range(2):
            n = recv[CX * NJ + 4 * CX + 2 * k + h]
            ir = spread(inv[h, k : k + 1, :])
            ii = spread(inv[2 + h, k : k + 1, :])
            pair.append(ir * n + ii * (sgn * turned(n)))
        added.append(pair)

    rows = lax.broadcasted_iota(jnp.int32, (2 * LANES, 2 * LANES), 0)
    cols = lax.broadcasted_iota(jnp.int32, (2 * LANES, 2 * LANES), 1)
    target = jnp.where(rows < LANES, 2 * rows, 2 * (rows - LANES) + 1)
    perm = jnp.where(cols == target, 1.0, 0.0).astype(jnp.bfloat16)
    count = OWN_X * OWN_Y

    def fine(x, y, value):
        col = x * OWN_Y + y
        even = it2[col, 0] + 0.5 * (value + up(value, first))
        odd = it2[col, 1] + value
        if x in flags:
            even = even + flags[x] * added[y][0]
            odd = odd + flags[x] * added[y][1]
        return even, odd

    size = 2 * OWN_Y * 8
    for i in range(OWN_X // 2):
        for j in range(OWN_Y // 2):
            at = (i + 4) * NJ + j + 4
            here = cc[at]
            left = cc[at - NJ]
            mix = 0.5 * (left + here)
            below = cc[at - 1]
            mix_below = 0.5 * (cc[at - NJ - 1] + below)
            for x in range(2):
                lower, upper = (
                    (0.5 * (mix_below + mix), mix),
                    (0.5 * (below + here), here),
                )[x]
                a = fine(2 * i + x, 2 * j, lower)
                b = fine(2 * i + x, 2 * j + 1, upper)
                for h in range(2):
                    value = jnp.concatenate([a[h], b[h]], axis=0)
                    top = value.astype(jnp.bfloat16)
                    rest = (value - top.astype(F32)).astype(jnp.bfloat16)
                    start = i * 2 * size + (x * OWN_Y + 2 * j) * 8
                    half = slice(h * LANES, h * LANES + LANES)
                    parts[start : start + 16, half] = top
                    parts[start + size : start + size + 16, half] = rest
        mixed = jnp.dot(
            parts[i * 2 * size : (i + 1) * 2 * size, :], perm, preferred_element_type=F32
        )
        for n in range(2 * OWN_Y):
            block = mixed[n * 8 : n * 8 + 8] + mixed[size + n * 8 : size + n * 8 + 8]
            col = i * 2 * OWN_Y + n
            o0[pl.ds(col, 8, stride=count), :] = block[:, :LANES]
            o1[pl.ds(col, 8, stride=count), :] = block[:, LANES:]
    out[:, :LANES] = o0[...]
    out[:, LANES:] = o1[...]


def vmem(*shape):
    return pltpu.VMEM(shape, F32)


SPEC = pl.BlockSpec(memory_space=pltpu.VMEM)
CELLS = PY * PX
SHARED = (vmem(PY, PX, LANES),) * 6 + (vmem(CELLS * 2, 8, LANES),) * 3 + (
    vmem(CELLS, 8, LANES),
) * 3
TABLES = [vmem(PY, PX, LANES)] * 6


def limit(mib):
    return pltpu.CompilerParams(vmem_limit_bytes=mib << 20)


def near_core(*arrays):
    return [pltpu.with_memory_space_constraint(a, pltpu.VMEM) for a in arrays]


def stay_call(labels):
    return pl.pallas_call(
        stay_kernel,
        out_shape=pltpu.VMEM(labels.shape, labels.dtype),
        in_specs=[pl.BlockSpec(memory_space=pltpu.HBM)],
        out_specs=SPEC,
        scratch_shapes=[pltpu.SemaphoreType.DMA(())],
        compiler_params=limit(1),
    )(pltpu.with_memory_space_constraint(labels, pltpu.HBM))


def wave_call(real, imag, angles, picks, after):
    small = pl.BlockSpec(memory_space=pltpu.HBM)
    return pl.pallas_call(
        wave_kernel,
        out_shape=(vmem(CELLS * 2, 8, LANES), vmem(8, LANES)),
        in_specs=[small] * 4 + [SPEC],
        out_specs=(SPEC,) * 2,
        scratch_shapes=[
            pltpu.SMEM(a.shape, a.dtype) for a in (real, imag, angles, picks)
        ]
        + [pltpu.SemaphoreType.DMA((4,))],
        compiler_params=limit(6),
    )(
        *(pltpu.with_memory_space_constraint(a, pltpu.HBM) for a in (real, imag, angles, picks)),
        *near_core(after),
    )


def middle_call(sizes, labels, tab, wave):
    def kernel(*refs):
        middle_kernel(sizes, *refs)

    return pl.pallas_call(
        kernel,
        out_shape=SHARED,
        in_specs=[SPEC] * 3,
        out_specs=(SPEC,) * 12,
        scratch_shapes=TABLES + [vmem(2 * OWN_Y * PX, 2 * LANES)],
        compiler_params=limit(6),
    )(*near_core(labels, tab, wave))


def low_call(sizes, labels, tab, wave, shared):
    def kernel(*refs):
        low_kernel(sizes, *refs)

    return pl.pallas_call(
        kernel,
        out_shape=SHARED,
        in_specs=[SPEC] * 15,
        out_specs=(SPEC,) * 12,
        input_output_aliases={3 + n: n for n in range(12)},
        scratch_shapes=TABLES + [vmem(LOW * PX, 2 * LANES)],
        compiler_params=limit(6),
    )(*near_core(labels, tab, wave), *shared)


def high_call(sizes, labels, tab, wave, shared):
    def kernel(*refs):
        high_kernel(sizes, *refs)

    results = pl.pallas_call(
        kernel,
        out_shape=SHARED
        + (
            vmem(CX, CY, 8, LANES),
            vmem(2, CX, 16, LANES),
            vmem(SEND, 8, LANES),
        ),
        in_specs=[SPEC] * 15,
        out_specs=(SPEC,) * 15,
        input_output_aliases={3 + n: n for n in range(12)},
        scratch_shapes=TABLES + [vmem(LOW * PX, 2 * LANES)],
        compiler_params=limit(6),
    )(*near_core(labels, tab, wave), *shared)
    return results[:12], results[12:]


POINTS = NI * NJ
HALF = (vmem(POINTS, 8, LANES), vmem(2, NI, 16, LANES)) + (vmem(POINTS, 8, LANES),) * 2


def own_call(shared, c1, ck):
    used = shared[:4] + shared[6:9]
    results = pl.pallas_call(
        own_kernel,
        out_shape=(vmem(OWN_X * OWN_Y, 2, 8, LANES), vmem(4, 8, LANES)) + HALF,
        in_specs=[SPEC] * 9,
        out_specs=(SPEC,) * 6,
        compiler_params=limit(6),
    )(*used, c1, ck)
    return results[:2], results[2:]


def cycle_call(recv, block, half):
    rows = OWN_X * OWN_Y * 8
    results = pl.pallas_call(
        cycle_kernel,
        out_shape=HALF + (jax.ShapeDtypeStruct((rows, 2 * LANES), F32),),
        in_specs=[SPEC] * 7,
        out_specs=(SPEC,) * 5,
        input_output_aliases={3 + n: n for n in range(4)},
        scratch_shapes=[vmem(POINTS, 8, LANES)]
        + [pltpu.VMEM((2 * rows, 2 * LANES), jnp.bfloat16)]
        + [vmem(rows, LANES)] * 2,
        compiler_params=limit(8),
    )(*near_core(recv), *block, *half)
    return results[4]


def complex_inverse(real, imag):
    modulus = real * real + imag * imag
    return real / modulus, -imag / modulus


def material_tables(er, ei):
    med_r = WAVE_SQUARED * (er + SHIFT_IMAG * ei)
    med_i = WAVE_SQUARED * (ei - SHIFT_IMAG * er)
    inv_r, inv_i = complex_inverse(128.0 / 30.0 - med_r, -med_i)
    src_r = SOURCE_GAIN * (er - 1.0)
    src_i = SOURCE_GAIN * ei
    ci_r, ci_i = complex_inverse(128.0 / 120.0 - med_r, -med_i)
    scale = 14.0 * DAMPING / 30.0
    return (
        scale * inv_r, scale * inv_i, 1.2 * src_r, 1.2 * src_i,
        DAMPING * ci_r, DAMPING * ci_i,
    )


def body(labels, permittivity_real, permittivity_imag, angles, angle_pick):
    gx_n = lax.axis_size("gx")
    gy_n = lax.axis_size("gy")
    core = lax.axis_index("gy") % 2
    is_low = core == 0

    def along_x(values, by):
        pairs = []
        for j in range(gy_n):
            step = by if j % 2 == 0 else -by
            for i in range(gx_n):
                if 0 <= i + step < gx_n:
                    pairs.append(((i + step) * gy_n + j, i * gy_n + j))
        return lax.ppermute(values, ("gx", "gy"), pairs)

    def along_y(values, by):
        pairs = [(j, j + by) for j in range(gy_n) if 0 <= j + by < gy_n]
        return lax.ppermute(values, "gy", pairs)

    def core_swap(values):
        return lax.ppermute(values, "gy", [(j, j ^ 1) for j in range(gy_n)])

    other = core_swap(labels)
    labels = stay_call(labels)
    both = jnp.where(
        is_low,
        jnp.concatenate([labels, other], axis=1),
        jnp.concatenate([other, labels], axis=1),
    )
    both = with_layout_constraint(both, Layout((0, 1, 2)))
    far = along_x(jnp.where(is_low, both[:4], both[2:]), 2)
    near = along_x(both, 1)
    near = with_layout_constraint(near, Layout((0, 1, 2)))
    far = with_layout_constraint(far, Layout((0, 1, 2)))
    region = jnp.where(
        is_low,
        jnp.concatenate([both, near, far], axis=0),
        jnp.concatenate([far, near, both], axis=0),
    )
    region = jnp.transpose(region, (1, 0, 2))
    low = along_y(region[2 * OWN_Y - LOW :], 2)
    high = along_y(region[: PY - LOW - 2 * OWN_Y], -2)

    wave, table = wave_call(
        permittivity_real, permittivity_imag, angles, angle_pick, both
    )
    sizes = (OWN_X * gx_n, OWN_Y * gy_n)
    shared = middle_call(sizes, region, table, wave)
    shared = low_call(sizes, low, table, wave, shared)
    shared, (c1, ck, send) = high_call(sizes, high, table, wave, shared)
    recv = core_swap(send)
    block, half = own_call(shared, c1, ck)
    out = cycle_call(recv, block, half)
    return out.reshape(2, 4, OWN_X, OWN_Y, 2 * LANES)


def solution(mesh):
    return jax.shard_map(
        body,
        mesh=mesh,
        in_specs=(P("gx", "gy", None), P(), P(), P(), P()),
        out_specs=P(None, None, "gx", "gy", None),
        check_vma=False,
    )
```

```python
import jax
import jax.numpy as jnp
import numpy as np
from jax import lax
from jax.experimental import pallas as pl
from jax.experimental.pallas import tpu as pltpu
from jax.experimental.layout import Layout, with_layout_constraint
from jax.sharding import PartitionSpec as P

MAT = 8
DAMPING = 0.8
WAVE_SQUARED = 0.1
SHIFT_IMAG = 0.5
SOURCE_GAIN = 4.0

OWN_X = 6
OWN_Y = 8
PX = 16
PY = 35
LOW = 10
CX, CY = 5, 15
NI, NJ = 10, 11
LANES = 128
F32 = jnp.float32
OUTSIDE = 8
WAVENUMBER = float(np.sqrt(np.float32(WAVE_SQUARED)))


def lane_iota():
    return lax.broadcasted_iota(jnp.int32, (8, LANES), 1)


def sign_rows():
    rows = lax.broadcasted_iota(jnp.int32, (8, LANES), 0)
    return jnp.where(rows < 4, -1.0, 1.0).astype(F32)


def up(values, first):
    return jnp.where(first, 0.0, pltpu.roll(values, 1, 1))


def down(values, last):
    return jnp.where(last, 0.0, pltpu.roll(values, LANES - 1, 1))


def turned(values):
    return pltpu.roll(values, 4, 0)


def row_of(ref, y, x):
    return jnp.broadcast_to(ref[y, pl.ds(x, 1), :], (8, LANES))


def edge_face(values, near):
    edge = (3.0 / 14.0) * (values + (1.0 / 3.0) * near)
    face = values + (3.0 / 14.0) * near
    return edge, face


def where_am_i():
    gx = lax.axis_index("gx")
    gy = lax.axis_index("gy")
    core = lax.rem(gy, 2)
    x0 = OWN_X * gx - LOW * core
    y0 = OWN_Y * (gy - core) - LOW
    return core, x0, y0


def stay_kernel(labels, held, sem):
    copy = pltpu.make_async_copy(labels, held, sem)
    copy.start()
    copy.wait()


def splat(value):
    return jnp.full((8, LANES), value, F32)


def wave_kernel(
    real_in, imag_in, angles_in, picks_in, after, wave, tab, real, imag, angles, picks, sems
):
    del after
    copies = [
        pltpu.make_async_copy(src, dst, sems.at[n])
        for n, (src, dst) in enumerate(
            (
                (real_in, real),
                (imag_in, imag),
                (angles_in, angles),
                (picks_in, picks),
            )
        )
    ]
    for copy in copies:
        copy.start()
    for copy in copies:
        copy.wait()
    _, x0, y0 = where_am_i()
    lanes = lane_iota()
    rows = lax.broadcasted_iota(jnp.int32, (8, LANES), 0)

    er = jnp.zeros((8, LANES), F32)
    ei = jnp.zeros((8, LANES), F32)
    for m in range(MAT):
        er = jnp.where(lanes == m, splat(real[m]), er)
        ei = jnp.where(lanes == m, splat(imag[m]), ei)
    for n, table in enumerate(material_tables(er, ei)):
        tab[n : n + 1, :] = jnp.where(lanes < MAT, table, 0.0)[0:1]

    incidence = jnp.zeros((8, LANES), F32)
    for c in range(4):
        mine = jnp.bitwise_and(rows, 3) == c
        incidence = jnp.where(mine, splat(angles[picks[c]]), incidence)
    in_x = lanes < PX
    place = jnp.where(in_x, x0 + lanes, y0 + (lanes - PX)).astype(F32)
    slope = jnp.where(in_x, jnp.cos(incidence), jnp.sin(incidence))
    phases = WAVENUMBER * (slope * place)
    cosine = jnp.cos(phases)
    sine = jnp.sin(phases)
    upper = rows < 4
    front = jnp.where(upper, cosine, sine)
    turn = jnp.where(upper, -sine, cosine)

    def along(values, n):
        return jnp.broadcast_to(values[:, n : n + 1], (8, LANES))

    for x in range(PX):
        wave[x * 2] = along(cosine, x)
        wave[x * 2 + 1] = along(sine, x)
    for y in reversed(range(PY)):
        w = along(front, PX + y)
        w_t = along(turn, PX + y)
        for x in range(PX):
            c = wave[x * 2]
            s = wave[x * 2 + 1]
            wave[(y * PX + x) * 2] = c * w + s * w_t
            wave[(y * PX + x) * 2 + 1] = c * w_t - s * w


def row_loop(first, count, step, body):
    def some(n, carry):
        for k in range(step):
            body(first + n * step + k)
        return carry

    lax.fori_loop(0, count // step, some, 0)


class Region:
    def __init__(self, sizes, tab, wave, shared, scratch):
        self.nx, self.ny = sizes
        self.core, self.x0, self.y0 = where_am_i()
        self.tab = tab
        self.wave = wave
        (self.ie_r, self.io_r, self.ie_i, self.io_i, self.kr, self.ki,
         self.it1, self.pp, self.qq, self.va, self.vb, self.sy) = shared
        (self.ge_r, self.go_r, self.ge_i, self.go_i, self.sa_r, self.sa_i,
         self.apart) = scratch
        lanes = lane_iota()
        self.first = lanes == 0
        self.last = lanes == LANES - 1
        self.sgn = sign_rows()
        rows = lax.broadcasted_iota(jnp.int32, (2 * LANES, 2 * LANES), 0)
        cols = lax.broadcasted_iota(jnp.int32, (2 * LANES, 2 * LANES), 1)
        source = jnp.where(cols < LANES, 2 * cols, 2 * (cols - LANES) + 1)
        self.perm = jnp.where(rows == source, 1.0, 0.0).astype(jnp.bfloat16)

    def pick(self, row, index):
        table = jnp.broadcast_to(self.tab[row : row + 1, :], (8, LANES))
        return jnp.take_along_axis(table, index, axis=1, mode="promise_in_bounds")

    def tables(self, labels, first_row, count, step):
        flat = labels[...].reshape(count * PX, 2 * LANES).astype(F32).astype(jnp.bfloat16)
        self.apart[0 : count * PX, :] = jnp.dot(
            flat, self.perm, preferred_element_type=F32
        )
        rows = lax.broadcasted_iota(jnp.int32, (8, LANES), 0)
        inside = []
        for h in range(2):
            xs = self.x0 + 8 * h + rows
            inside.append(jnp.logical_and(xs >= 0, xs < self.nx))

        def some(n, carry):
            for k in range(step):
                y = first_row + n * step + k
                y_in = jnp.logical_and(self.y0 + y >= 0, self.y0 + y < self.ny)
                beyond = jnp.where(y_in, 0, OUTSIDE)
                for h in range(2):
                    start = pl.multiple_of((n * step + k) * PX + 8 * h, 8)
                    part = self.apart[pl.ds(start, 8), :]
                    at = (y, pl.ds(8 * h, 8), slice(None))
                    label = part[:, :LANES].astype(jnp.int32)
                    index = jnp.where(inside[h], label, OUTSIDE) + beyond
                    even = [self.pick(n, index) for n in range(4)]
                    label = part[:, LANES:].astype(jnp.int32)
                    index = jnp.where(inside[h], label, OUTSIDE) + beyond
                    chosen = 4 + 2 * ((first_row + k) % 2)
                    odd = [self.pick(n, index) for n in range(chosen)]
                    halves = (even, odd)
                    for (ir, ii, sr, si), (inv_r, inv_i, g_r, g_i) in (
                        (even, (self.ie_r, self.ie_i, self.ge_r, self.ge_i)),
                        (odd[:4], (self.io_r, self.io_i, self.go_r, self.go_i)),
                    ):
                        inv_r[at] = ir
                        inv_i[at] = ii
                        g_r[at] = (4.0 / 14.0) * (ir * sr - ii * si)
                        g_i[at] = (4.0 / 14.0) * (ir * si + ii * sr)
                    if chosen > 4:
                        self.kr[at] = odd[4]
                        self.ki[at] = odd[5]
                    for c, out in ((0, self.sa_r), (1, self.sa_i)):
                        se = halves[0][2 + c]
                        out[at] = (se + down(se, self.last) + 2.0 * halves[1][2 + c]) * (1.0 / 14.0)
            return carry

        lax.fori_loop(0, count // step, some, 0)

    def first_stage(self, y):
        edges, faces, centres = [[], []], [[], []], [[], []]
        for x in range(PX):
            at = (y * PX + x) * 2
            e = self.wave[at]
            e_t = self.wave[at + 1]
            even = row_of(self.ge_r, y, x) * e + row_of(self.ge_i, y, x) * e_t
            odd = row_of(self.go_r, y, x) * e + row_of(self.go_i, y, x) * e_t
            if 2 <= x <= 12:
                self.sy[y * PX + x] = (
                    row_of(self.sa_r, y, x) * e + row_of(self.sa_i, y, x) * e_t
                )
            self.it1[at] = even
            self.it1[at + 1] = odd
            near_e = odd + up(odd, self.first)
            near_o = even + down(even, self.last)
            for h, (v, near) in enumerate(((even, near_e), (odd, near_o))):
                edge, face = edge_face(v, near)
                edges[h].append(edge)
                faces[h].append(face)
                centres[h].append(near)
        for x in range(PX):
            at = (y * PX + x) * 2
            for h in range(2):
                p = centres[h][x]
                q = faces[h][x]
                if 0 < x < PX - 1:
                    p = p + (faces[h][x - 1] + faces[h][x + 1])
                    q = q + (edges[h][x - 1] + edges[h][x + 1])
                else:
                    beside = x - 1 if x else x + 1
                    p = p + faces[h][beside]
                    q = q + edges[h][beside]
                self.pp[at + h] = p
                self.qq[at + h] = q

    def update(self, y, x, h):
        at = (y * PX + x) * 2 + h
        row = PX * 2
        ir, ii = ((self.ie_r, self.ie_i), (self.io_r, self.io_i))[h]
        n = self.pp[at] + (self.qq[at - row] + self.qq[at + row])
        return row_of(ir, y, x) * n + row_of(ii, y, x) * (self.sgn * turned(n))

    def second_stage(self, y):
        for x in range(1, 14):
            at = (y * PX + x) * 2
            we = self.it1[at] + self.update(y, x, 0)
            wo = self.it1[at + 1] + self.update(y, x, 1)
            p = we + down(we, self.last)
            half = p + wo
            after = jnp.where(self.last, -wo, pltpu.roll(wo, LANES - 1, 1))
            self.va[y * PX + x] = half + wo
            self.vb[y * PX + x] = (up(wo, self.first) + after) + 2.0 * half

    def third_stage(self, j, c1_out, ck_out):
        base = (2 + 2 * j) * PX
        gs, hs = {}, {}
        for x in range(1, 14):

            def combos(ref):
                vm, v0, v1, v2, v3 = (ref[base + (d - 1) * PX + x] for d in range(5))
                half = (v0 + v2) + v1
                return half + v1, (vm + v3) + 2.0 * half

            aa, ba = combos(self.va)
            ab, bb = combos(self.vb)
            u = ba + ab
            if 2 <= x <= 12:
                at = base + x
                gs[x] = (u + (3.0 / 14.0) * bb) + (
                    (self.sy[at] + self.sy[at + 2 * PX]) + 2.0 * self.sy[at + PX]
                )
            hs[x] = aa + ((3.0 / 14.0) * u + (1.0 / 14.0) * bb)
        for i in range(CX):
            b = 2 + 2 * i
            mx = jnp.where(self.x0 + b + 2 == self.nx, 1.0, 2.0).astype(F32)
            raw = (
                (gs[b] + gs[b + 2])
                + 2.0 * (gs[b + 1] + (hs[b] + hs[b + 2]))
                + (hs[b - 1] + hs[b + 3])
                + mx * hs[b + 1]
            ) * (14.0 / 1920.0)
            kr = row_of(self.kr, 3 + 2 * j, b + 1)
            ki = row_of(self.ki, 3 + 2 * j, b + 1)
            c1_out[i, j] = kr * raw + ki * (self.sgn * turned(raw))
            ck_out[0, i, pl.ds(j, 1), :] = self.kr[3 + 2 * j, b + 1 : b + 2, :]
            ck_out[1, i, pl.ds(j, 1), :] = self.ki[3 + 2 * j, b + 1 : b + 2, :]


def middle_kernel(sizes, labels, tab, wave, *refs):
    region = Region(sizes, tab, wave, refs[:12], refs[12:])
    region.tables(labels, LOW, 2 * OWN_Y, 8)
    row_loop(LOW, 2 * OWN_Y, 4, region.first_stage)
    row_loop(LOW + 1, 2 * OWN_Y - 2, 7, region.second_stage)


def low_kernel(sizes, labels, tab, wave, *refs):
    region = Region(sizes, tab, wave, refs[12:24], refs[24:])
    region.tables(labels, 0, LOW, LOW)
    row_loop(0, LOW, 5, region.first_stage)
    row_loop(1, LOW, 5, region.second_stage)


def high_kernel(sizes, labels, tab, wave, *refs):
    region = Region(sizes, tab, wave, refs[12:24], refs[27:])
    c1_out, ck_out, send_out = refs[24:27]
    core, y0, ny = region.core, region.y0, region.ny
    it1 = region.it1
    top = LOW + 2 * OWN_Y
    region.tables(labels, top, PY - top, PY - top)
    row_loop(top, PY - top, 3, region.first_stage)
    row_loop(top - 1, PY - top, 3, region.second_stage)

    @pl.when(y0 + top == ny)
    def _():
        for x in range(1, 14):
            for ref in (region.va, region.vb):
                ref[(top + 1) * PX + x] = -ref[(top - 1) * PX + x]

    for k in range(2):
        for i in range(CX):
            ck_out[k, i, 8:16, :] = jnp.zeros((8, LANES), F32)
    row_loop(0, CY, 1, lambda j: region.third_stage(j, c1_out, ck_out))

    j0 = 4 - 4 * core
    for i in range(CX):
        for j in range(NJ):
            send_out[i * NJ + j] = c1_out[i, j0 + j]
        for k in range(2):
            send_out[CX * NJ + (k * CX + i) * 2] = ck_out[k, i, 0:8, :]
            send_out[CX * NJ + (k * CX + i) * 2 + 1] = ck_out[k, i, 8:16, :]
    plane = 6 + 3 * core
    ys = LOW + OWN_Y - core * OWN_Y
    edges, faces = [], []
    for k in range(OWN_Y + 2):
        at = ((ys - 1 + k) * PX + plane) * 2
        even = it1[at]
        odd = it1[at + 1]
        ee, fe = edge_face(even, odd + up(odd, region.first))
        eo, fo = edge_face(odd, even + down(even, region.last))
        edges.append((ee, eo))
        faces.append((fe, fo))
    for k in range(OWN_Y):
        for h in range(2):
            send_out[CX * NJ + 4 * CX + 2 * k + h] = faces[k + 1][h] + (
                edges[k][h] + edges[k + 2][h]
            )


SEND = CX * NJ + 4 * CX + 2 * OWN_Y


class Own(Region):
    def __init__(self, refs):
        (self.ie_r, self.io_r, self.ie_i, self.io_i, self.it1, self.pp, self.qq) = refs
        self.sgn = sign_rows()


def coarse_sums(ref, pp, qq, i, sweep, first, last):
    edges, faces, centres = {}, {}, {}
    for j in range(sweep, NJ - sweep):
        v = ref[i * NJ + j]
        near = up(v, first) + down(v, last)
        edges[j], faces[j] = edge_face(v, near)
        centres[j] = near
    for j in range(sweep + 1, NJ - sweep - 1):
        pp[i * NJ + j] = centres[j] + (faces[j - 1] + faces[j + 1])
        qq[i * NJ + j] = faces[j] + (edges[j - 1] + edges[j + 1])


def own_kernel(*refs):
    own = Own(refs[:7])
    c1_own, ck_own, it2, inv, c1, ck, pp, qq = refs[7:]
    core = where_am_i()[0]
    lanes = lane_iota()
    first = lanes == 0
    last = lanes == LANES - 1

    xb = core * LOW
    yb = LOW + core * OWN_Y
    xe = core * (PX - 1)
    tables = (own.ie_r, own.io_r, own.ie_i, own.io_i)

    def own_stage(k):
        y = yb + k
        for xx in range(OWN_X):
            x = xb + xx
            at = (y * PX + x) * 2
            for h in range(2):
                it2[xx * OWN_Y + k, h] = 3.0 * own.it1[at + h] + own.update(y, x, h)
        for n, ref in enumerate(tables):
            inv[n, pl.ds(k, 1), :] = ref[y, pl.ds(xe, 1), :]

    own_i = CX - core * CX
    for i in range(CX):
        for j in range(NJ):
            c1[(own_i + i) * NJ + j] = c1_own[i, 4 * core + j]
        for k in range(2):
            ck[k, own_i + i] = ck_own[k, i]
    row_loop(
        own_i, CX, 5, lambda i: coarse_sums(c1, pp, qq, i, 0, first, last)
    )
    row_loop(0, OWN_Y, 2, own_stage)


def cycle_kernel(recv, it2, inv, *refs):
    c1, ck, pp, qq, out, cc, parts, o0, o1, stage, sems = refs[4:]
    core = where_am_i()[0]
    lanes = lane_iota()
    first = lanes == 0
    last = lanes == LANES - 1
    sgn = sign_rows()
    j0 = 4 * core
    other_i = core * CX

    def spread(row):
        return jnp.broadcast_to(row, (8, LANES))

    for i in range(CX):
        for j in range(NJ):
            c1[(other_i + i) * NJ + j] = recv[i * NJ + j]
        for k in range(2):
            for h in range(2):
                tile = slice(8 * h, 8 * h + 8)
                ck[k, other_i + i, tile, :] = recv[CX * NJ + (k * CX + i) * 2 + h]

    for sweep, (sum_step, relax_step) in enumerate(((5, 4), (4, 3), (3, 4))):
        ref = c1 if sweep == 0 else cc

        def sums(i, ref=ref, sweep=sweep):
            coarse_sums(ref, pp, qq, i, sweep, first, last)

        if sweep:
            row_loop(sweep, NI - 2 * sweep, sum_step, sums)
        else:
            row_loop(other_i, CX, sum_step, sums)

        def relax(i, ref=ref, sweep=sweep):
            for j in range(sweep + 1, NJ - sweep - 1):
                at = i * NJ + j
                n = (pp[at] + (qq[at - NJ] + qq[at + NJ])) * (14.0 / 120.0)
                kr = spread(ck[0, i, pl.ds(j0 + j, 1), :])
                ki = spread(ck[1, i, pl.ds(j0 + j, 1), :])
                cc[at] = (0.2 * ref[at] + c1[at]) + (kr * n + ki * (sgn * turned(n)))

        row_loop(sweep + 1, NI - 2 * sweep - 2, relax_step, relax)

    flags = {0: jnp.where(core == 0, 1.0, 0.0), OWN_X - 1: jnp.where(core == 1, 1.0, 0.0)}
    added = []
    for k in range(OWN_Y):
        pair = []
        for h in range(2):
            n = recv[CX * NJ + 4 * CX + 2 * k + h]
            ir = spread(inv[h, k : k + 1, :])
            ii = spread(inv[2 + h, k : k + 1, :])
            pair.append(ir * n + ii * (sgn * turned(n)))
        added.append(pair)

    rows = lax.broadcasted_iota(jnp.int32, (2 * LANES, 2 * LANES), 0)
    cols = lax.broadcasted_iota(jnp.int32, (2 * LANES, 2 * LANES), 1)
    target = jnp.where(rows < LANES, 2 * rows, 2 * (rows - LANES) + 1)
    perm = jnp.where(cols == target, 1.0, 0.0).astype(jnp.bfloat16)

    def fine(x, y, value):
        col = x * OWN_Y + y
        even = it2[col, 0] + 0.5 * (value + up(value, first))
        odd = it2[col, 1] + value
        if x in flags:
            even = even + flags[x] * added[y][0]
            odd = odd + flags[x] * added[y][1]
        return even, odd

    size = 2 * OWN_Y * 8
    copies = []
    for i in range(OWN_X // 2):
        for j in range(OWN_Y // 2):
            at = (i + 4) * NJ + j + 4
            here = cc[at]
            left = cc[at - NJ]
            mix = 0.5 * (left + here)
            below = cc[at - 1]
            mix_below = 0.5 * (cc[at - NJ - 1] + below)
            for x in range(2):
                lower, upper = (
                    (0.5 * (mix_below + mix), mix),
                    (0.5 * (below + here), here),
                )[x]
                a = fine(2 * i + x, 2 * j, lower)
                b = fine(2 * i + x, 2 * j + 1, upper)
                for h in range(2):
                    value = jnp.concatenate([a[h], b[h]], axis=0)
                    top = value.astype(jnp.bfloat16)
                    rest = (value - top.astype(F32)).astype(jnp.bfloat16)
                    start = i * 2 * size + (x * OWN_Y + 2 * j) * 8
                    half = slice(h * LANES, h * LANES + LANES)
                    parts[start : start + 16, half] = top
                    parts[start + size : start + size + 16, half] = rest
        mixed = jnp.dot(
            parts[i * 2 * size : (i + 1) * 2 * size, :], perm, preferred_element_type=F32
        )
        rows_in = 2 * OWN_Y
        for n in range(rows_in):
            block = mixed[n * 8 : n * 8 + 8] + mixed[size + n * 8 : size + n * 8 + 8]
            o0[pl.ds(i * size + n, 8, stride=rows_in), :] = block[:, :LANES]
            o1[pl.ds(i * size + n, 8, stride=rows_in), :] = block[:, LANES:]
        for f in range(8):
            take = slice(i * size + f * rows_in, i * size + (f + 1) * rows_in)
            stage[i, f, :, :LANES] = o0[take]
            stage[i, f, :, LANES:] = o1[take]
        copies.append(
            pltpu.make_async_copy(
                stage.at[i], out.at[:, pl.ds(i * rows_in, rows_in), :], sems.at[i]
            )
        )
        copies[-1].start()
    for copy in copies:
        copy.wait()


def vmem(*shape):
    return pltpu.VMEM(shape, F32)


SPEC = pl.BlockSpec(memory_space=pltpu.VMEM)
CELLS = PY * PX
SHARED = (vmem(PY, PX, LANES),) * 6 + (vmem(CELLS * 2, 8, LANES),) * 3 + (
    vmem(CELLS, 8, LANES),
) * 3
TABLES = [vmem(PY, PX, LANES)] * 6


def limit(mib):
    return pltpu.CompilerParams(vmem_limit_bytes=mib << 20)


def near_core(*arrays):
    return [pltpu.with_memory_space_constraint(a, pltpu.VMEM) for a in arrays]


def stay_call(labels):
    return pl.pallas_call(
        stay_kernel,
        out_shape=pltpu.VMEM(labels.shape, labels.dtype),
        in_specs=[pl.BlockSpec(memory_space=pltpu.HBM)],
        out_specs=SPEC,
        scratch_shapes=[pltpu.SemaphoreType.DMA(())],
        compiler_params=limit(1),
    )(pltpu.with_memory_space_constraint(labels, pltpu.HBM))


def wave_call(real, imag, angles, picks, after):
    small = pl.BlockSpec(memory_space=pltpu.HBM)
    return pl.pallas_call(
        wave_kernel,
        out_shape=(vmem(CELLS * 2, 8, LANES), vmem(8, LANES)),
        in_specs=[small] * 4 + [SPEC],
        out_specs=(SPEC,) * 2,
        scratch_shapes=[
            pltpu.SMEM(a.shape, a.dtype) for a in (real, imag, angles, picks)
        ]
        + [pltpu.SemaphoreType.DMA((4,))],
        compiler_params=limit(6),
    )(
        *(pltpu.with_memory_space_constraint(a, pltpu.HBM) for a in (real, imag, angles, picks)),
        *near_core(after),
    )


def middle_call(sizes, labels, tab, wave):
    def kernel(*refs):
        middle_kernel(sizes, *refs)

    return pl.pallas_call(
        kernel,
        out_shape=SHARED,
        in_specs=[SPEC] * 3,
        out_specs=(SPEC,) * 12,
        scratch_shapes=TABLES + [vmem(2 * OWN_Y * PX, 2 * LANES)],
        compiler_params=limit(6),
    )(*near_core(labels, tab, wave))


def low_call(sizes, labels, tab, wave, shared):
    def kernel(*refs):
        low_kernel(sizes, *refs)

    return pl.pallas_call(
        kernel,
        out_shape=SHARED,
        in_specs=[SPEC] * 15,
        out_specs=(SPEC,) * 12,
        input_output_aliases={3 + n: n for n in range(12)},
        scratch_shapes=TABLES + [vmem(LOW * PX, 2 * LANES)],
        compiler_params=limit(6),
    )(*near_core(labels, tab, wave), *shared)


def high_call(sizes, labels, tab, wave, shared):
    def kernel(*refs):
        high_kernel(sizes, *refs)

    results = pl.pallas_call(
        kernel,
        out_shape=SHARED
        + (
            vmem(CX, CY, 8, LANES),
            vmem(2, CX, 16, LANES),
            vmem(SEND, 8, LANES),
        ),
        in_specs=[SPEC] * 15,
        out_specs=(SPEC,) * 15,
        input_output_aliases={3 + n: n for n in range(12)},
        scratch_shapes=TABLES + [vmem(LOW * PX, 2 * LANES)],
        compiler_params=limit(6),
    )(*near_core(labels, tab, wave), *shared)
    return results[:12], results[12:]


POINTS = NI * NJ
HALF = (vmem(POINTS, 8, LANES), vmem(2, NI, 16, LANES)) + (vmem(POINTS, 8, LANES),) * 2


def own_call(shared, c1, ck):
    used = shared[:4] + shared[6:9]
    results = pl.pallas_call(
        own_kernel,
        out_shape=(vmem(OWN_X * OWN_Y, 2, 8, LANES), vmem(4, 8, LANES)) + HALF,
        in_specs=[SPEC] * 9,
        out_specs=(SPEC,) * 6,
        compiler_params=limit(6),
    )(*used, c1, ck)
    return results[:2], results[2:]


def cycle_call(recv, block, half):
    rows = OWN_X * OWN_Y * 8
    results = pl.pallas_call(
        cycle_kernel,
        out_shape=HALF
        + (jax.ShapeDtypeStruct((8, OWN_X * OWN_Y, 2 * LANES), F32),),
        in_specs=[SPEC] * 7,
        out_specs=(SPEC,) * 4 + (pl.BlockSpec(memory_space=pltpu.HBM),),
        input_output_aliases={3 + n: n for n in range(4)},
        scratch_shapes=[vmem(POINTS, 8, LANES)]
        + [pltpu.VMEM((2 * rows, 2 * LANES), jnp.bfloat16)]
        + [vmem(rows, LANES)] * 2
        + [vmem(OWN_X // 2, 8, 2 * OWN_Y, 2 * LANES), pltpu.SemaphoreType.DMA((3,))],
        compiler_params=limit(8),
    )(*near_core(recv), *block, *half)
    return results[4]


def complex_inverse(real, imag):
    modulus = real * real + imag * imag
    return real / modulus, -imag / modulus


def material_tables(er, ei):
    med_r = WAVE_SQUARED * (er + SHIFT_IMAG * ei)
    med_i = WAVE_SQUARED * (ei - SHIFT_IMAG * er)
    inv_r, inv_i = complex_inverse(128.0 / 30.0 - med_r, -med_i)
    src_r = SOURCE_GAIN * (er - 1.0)
    src_i = SOURCE_GAIN * ei
    ci_r, ci_i = complex_inverse(128.0 / 120.0 - med_r, -med_i)
    scale = 2.5 * 14.0 * DAMPING / 30.0
    return (
        scale * inv_r, scale * inv_i, 1.2 * src_r, 1.2 * src_i,
        DAMPING * ci_r, DAMPING * ci_i,
    )


def body(labels, permittivity_real, permittivity_imag, angles, angle_pick):
    gx_n = lax.axis_size("gx")
    gy_n = lax.axis_size("gy")
    core = lax.axis_index("gy") % 2
    is_low = core == 0

    def along_x(values, by):
        pairs = []
        for j in range(gy_n):
            step = by if j % 2 == 0 else -by
            for i in range(gx_n):
                if 0 <= i + step < gx_n:
                    pairs.append(((i + step) * gy_n + j, i * gy_n + j))
        return lax.ppermute(values, ("gx", "gy"), pairs)

    def along_y(values, by):
        pairs = [(j, j + by) for j in range(gy_n) if 0 <= j + by < gy_n]
        return lax.ppermute(values, "gy", pairs)

    def core_swap(values):
        return lax.ppermute(values, "gy", [(j, j ^ 1) for j in range(gy_n)])

    other = core_swap(labels)
    labels = stay_call(labels)
    both = jnp.where(
        is_low,
        jnp.concatenate([labels, other], axis=1),
        jnp.concatenate([other, labels], axis=1),
    )
    both = with_layout_constraint(both, Layout((0, 1, 2)))
    far = along_x(jnp.where(is_low, both[:4], both[2:]), 2)
    near = along_x(both, 1)
    near = with_layout_constraint(near, Layout((0, 1, 2)))
    far = with_layout_constraint(far, Layout((0, 1, 2)))
    region = jnp.where(
        is_low,
        jnp.concatenate([both, near, far], axis=0),
        jnp.concatenate([far, near, both], axis=0),
    )
    region = jnp.transpose(region, (1, 0, 2))
    low = along_y(region[2 * OWN_Y - LOW :], 2)
    high = along_y(region[: PY - LOW - 2 * OWN_Y], -2)

    wave, table = wave_call(
        permittivity_real, permittivity_imag, angles, angle_pick, both
    )
    sizes = (OWN_X * gx_n, OWN_Y * gy_n)
    shared = middle_call(sizes, region, table, wave)
    shared = low_call(sizes, low, table, wave, shared)
    shared, (c1, ck, send) = high_call(sizes, high, table, wave, shared)
    recv = core_swap(send)
    block, half = own_call(shared, c1, ck)
    out = cycle_call(recv, block, half)
    return out.reshape(2, 4, OWN_X, OWN_Y, 2 * LANES)


def solution(mesh):
    return jax.shard_map(
        body,
        mesh=mesh,
        in_specs=(P("gx", "gy", None), P(), P(), P(), P()),
        out_specs=P(None, None, "gx", "gy", None),
        check_vma=False,
    )
```

```python
import jax
import jax.numpy as jnp
import numpy as np
from jax import lax
from jax.experimental import pallas as pl
from jax.experimental.pallas import tpu as pltpu
from jax.experimental.layout import Layout, with_layout_constraint
from jax.sharding import PartitionSpec as P

MAT = 8
DAMPING = 0.8
WAVE_SQUARED = 0.1
SHIFT_IMAG = 0.5
SOURCE_GAIN = 4.0

OWN_X = 6
OWN_Y = 8
PX = 16
PY = 35
LOW = 10
CX, CY = 5, 15
NI, NJ = 10, 11
LANES = 128
F32 = jnp.float32
OUTSIDE = 8
WAVENUMBER = float(np.sqrt(np.float32(WAVE_SQUARED)))


def lane_iota():
    return lax.broadcasted_iota(jnp.int32, (8, LANES), 1)


def sign_rows():
    rows = lax.broadcasted_iota(jnp.int32, (8, LANES), 0)
    return jnp.where(rows < 4, -1.0, 1.0).astype(F32)


def up(values, first):
    return jnp.where(first, 0.0, pltpu.roll(values, 1, 1))


def down(values, last):
    return jnp.where(last, 0.0, pltpu.roll(values, LANES - 1, 1))


def turned(values):
    return pltpu.roll(values, 4, 0)


def row_of(ref, y, x):
    return jnp.broadcast_to(ref[y, pl.ds(x, 1), :], (8, LANES))


def edge_face(values, near):
    edge = (3.0 / 14.0) * (values + (1.0 / 3.0) * near)
    face = values + (3.0 / 14.0) * near
    return edge, face


UPDATE_SCALE = 2.5 * 14.0 * DAMPING / 30.0


def fine_diagonal(er, ei):
    real = 128.0 / 30.0 - WAVE_SQUARED * (er + SHIFT_IMAG * ei)
    imag = WAVE_SQUARED * (SHIFT_IMAG * er - ei)
    return real, imag


def scaled_inverse(real, imag, scale, keep):
    ratio = jnp.where(keep, scale / (real * real + imag * imag), 0.0)
    return real * ratio, -imag * ratio


def where_am_i():
    gx = lax.axis_index("gx")
    gy = lax.axis_index("gy")
    core = lax.rem(gy, 2)
    x0 = OWN_X * gx - LOW * core
    y0 = OWN_Y * (gy - core) - LOW
    return core, x0, y0


def stay_kernel(labels, held, sem):
    copy = pltpu.make_async_copy(labels, held, sem)
    copy.start()
    copy.wait()


def splat(value):
    return jnp.full((8, LANES), value, F32)


def wave_kernel(
    real_in, imag_in, angles_in, picks_in, after, wave, tab, real, imag, angles, picks, sems
):
    del after
    copies = [
        pltpu.make_async_copy(src, dst, sems.at[n])
        for n, (src, dst) in enumerate(
            (
                (real_in, real),
                (imag_in, imag),
                (angles_in, angles),
                (picks_in, picks),
            )
        )
    ]
    for copy in copies:
        copy.start()
    for copy in copies:
        copy.wait()
    _, x0, y0 = where_am_i()
    lanes = lane_iota()
    rows = lax.broadcasted_iota(jnp.int32, (8, LANES), 0)

    er = jnp.ones((8, LANES), F32)
    ei = jnp.zeros((8, LANES), F32)
    for m in range(MAT):
        er = jnp.where(lanes == m, splat(real[m]), er)
        ei = jnp.where(lanes == m, splat(imag[m]), ei)
    tab[0:1, :] = er[0:1]
    tab[1:2, :] = ei[0:1]

    incidence = jnp.zeros((8, LANES), F32)
    for c in range(4):
        mine = jnp.bitwise_and(rows, 3) == c
        incidence = jnp.where(mine, splat(angles[picks[c]]), incidence)
    in_x = lanes < PX
    place = jnp.where(in_x, x0 + lanes, y0 + (lanes - PX)).astype(F32)
    slope = jnp.where(in_x, jnp.cos(incidence), jnp.sin(incidence))
    phases = WAVENUMBER * (slope * place)
    cosine = jnp.cos(phases)
    sine = jnp.sin(phases)
    upper = rows < 4
    front = jnp.where(upper, cosine, sine)
    turn = jnp.where(upper, -sine, cosine)

    def along(values, n):
        return jnp.broadcast_to(values[:, n : n + 1], (8, LANES))

    for x in range(PX):
        wave[x * 2] = along(cosine, x)
        wave[x * 2 + 1] = along(sine, x)
    for y in reversed(range(PY)):
        w = along(front, PX + y)
        w_t = along(turn, PX + y)
        for x in range(PX):
            c = wave[x * 2]
            s = wave[x * 2 + 1]
            wave[(y * PX + x) * 2] = c * w + s * w_t
            wave[(y * PX + x) * 2 + 1] = c * w_t - s * w


def row_loop(first, count, step, body):
    def some(n, carry):
        for k in range(step):
            body(first + n * step + k)
        return carry

    lax.fori_loop(0, count // step, some, 0)


class Region:
    def __init__(self, sizes, tab, wave, shared, scratch):
        self.nx, self.ny = sizes
        self.core, self.x0, self.y0 = where_am_i()
        self.tab = tab
        self.wave = wave
        (self.ie_r, self.io_r, self.ie_i, self.io_i, self.kr, self.ki,
         self.it1, self.pp, self.qq, self.va, self.vb, self.sy) = shared
        (self.ge_r, self.go_r, self.ge_i, self.go_i, self.sa_r, self.sa_i,
         self.apart) = scratch
        lanes = lane_iota()
        self.first = lanes == 0
        self.last = lanes == LANES - 1
        self.sgn = sign_rows()
        rows = lax.broadcasted_iota(jnp.int32, (2 * LANES, 2 * LANES), 0)
        cols = lax.broadcasted_iota(jnp.int32, (2 * LANES, 2 * LANES), 1)
        source = jnp.where(cols < LANES, 2 * cols, 2 * (cols - LANES) + 1)
        self.perm = jnp.where(rows == source, 1.0, 0.0).astype(jnp.bfloat16)

    def pick(self, row, index):
        table = jnp.broadcast_to(self.tab[row : row + 1, :], (8, LANES))
        return jnp.take_along_axis(table, index, axis=1, mode="promise_in_bounds")

    def tables(self, labels, first_row, count, step):
        flat = labels[...].reshape(count * PX, 2 * LANES).astype(F32).astype(jnp.bfloat16)
        self.apart[0 : count * PX, :] = jnp.dot(
            flat, self.perm, preferred_element_type=F32
        )
        rows = lax.broadcasted_iota(jnp.int32, (8, LANES), 0)
        inside = []
        for h in range(2):
            xs = self.x0 + 8 * h + rows
            inside.append(jnp.logical_and(xs >= 0, xs < self.nx))

        def some(n, carry):
            for k in range(step):
                y = first_row + n * step + k
                y_in = jnp.logical_and(self.y0 + y >= 0, self.y0 + y < self.ny)
                for h in range(2):
                    start = pl.multiple_of((n * step + k) * PX + 8 * h, 8)
                    part = self.apart[pl.ds(start, 8), :]
                    at = (y, pl.ds(8 * h, 8), slice(None))
                    keep = jnp.logical_and(inside[h], y_in)
                    sources = []
                    for odd, (inv_r, inv_i, g_r, g_i) in enumerate(
                        (
                            (self.ie_r, self.ie_i, self.ge_r, self.ge_i),
                            (self.io_r, self.io_i, self.go_r, self.go_i),
                        )
                    ):
                        label = part[:, odd * LANES : (odd + 1) * LANES].astype(jnp.int32)
                        index = jnp.where(keep, label, OUTSIDE)
                        er = self.pick(0, index)
                        ei = self.pick(1, index)
                        real, imag = fine_diagonal(er, ei)
                        ir, ii = scaled_inverse(real, imag, UPDATE_SCALE, keep)
                        sr, si = 1.2 * SOURCE_GAIN * (er - 1.0), 1.2 * SOURCE_GAIN * ei
                        inv_r[at] = ir
                        inv_i[at] = ii
                        g_r[at] = (4.0 / 14.0) * (ir * sr - ii * si)
                        g_i[at] = (4.0 / 14.0) * (ir * si + ii * sr)
                        sources.append((sr, si))
                        if odd and (first_row + k) % 2 == 1:
                            kr, ki = scaled_inverse(
                                real + (128.0 / 120.0 - 128.0 / 30.0), imag, DAMPING, keep
                            )
                            self.kr[at] = kr
                            self.ki[at] = ki
                    for c, out in ((0, self.sa_r), (1, self.sa_i)):
                        se = sources[0][c]
                        out[at] = (se + down(se, self.last) + 2.0 * sources[1][c]) * (1.0 / 14.0)
            return carry

        lax.fori_loop(0, count // step, some, 0)

    def first_stage(self, y):
        edges, faces, centres = [[], []], [[], []], [[], []]
        for x in range(PX):
            at = (y * PX + x) * 2
            e = self.wave[at]
            e_t = self.wave[at + 1]
            even = row_of(self.ge_r, y, x) * e + row_of(self.ge_i, y, x) * e_t
            odd = row_of(self.go_r, y, x) * e + row_of(self.go_i, y, x) * e_t
            if 2 <= x <= 12:
                self.sy[y * PX + x] = (
                    row_of(self.sa_r, y, x) * e + row_of(self.sa_i, y, x) * e_t
                )
            self.it1[at] = even
            self.it1[at + 1] = odd
            near_e = odd + up(odd, self.first)
            near_o = even + down(even, self.last)
            for h, (v, near) in enumerate(((even, near_e), (odd, near_o))):
                edge, face = edge_face(v, near)
                edges[h].append(edge)
                faces[h].append(face)
                centres[h].append(near)
        for x in range(PX):
            at = (y * PX + x) * 2
            for h in range(2):
                p = centres[h][x]
                q = faces[h][x]
                if 0 < x < PX - 1:
                    p = p + (faces[h][x - 1] + faces[h][x + 1])
                    q = q + (edges[h][x - 1] + edges[h][x + 1])
                else:
                    beside = x - 1 if x else x + 1
                    p = p + faces[h][beside]
                    q = q + edges[h][beside]
                self.pp[at + h] = p
                self.qq[at + h] = q

    def update(self, y, x, h):
        at = (y * PX + x) * 2 + h
        row = PX * 2
        ir, ii = ((self.ie_r, self.ie_i), (self.io_r, self.io_i))[h]
        n = self.pp[at] + (self.qq[at - row] + self.qq[at + row])
        return row_of(ir, y, x) * n + row_of(ii, y, x) * (self.sgn * turned(n))

    def second_stage(self, y):
        for x in range(1, 14):
            at = (y * PX + x) * 2
            we = self.it1[at] + self.update(y, x, 0)
            wo = self.it1[at + 1] + self.update(y, x, 1)
            p = we + down(we, self.last)
            half = p + wo
            after = jnp.where(self.last, -wo, pltpu.roll(wo, LANES - 1, 1))
            self.va[y * PX + x] = half + wo
            self.vb[y * PX + x] = (up(wo, self.first) + after) + 2.0 * half

    def third_stage(self, j, c1_out, ck_out):
        base = (2 + 2 * j) * PX
        gs, hs = {}, {}
        for x in range(1, 14):

            def combos(ref):
                vm, v0, v1, v2, v3 = (ref[base + (d - 1) * PX + x] for d in range(5))
                half = (v0 + v2) + v1
                return half + v1, (vm + v3) + 2.0 * half

            aa, ba = combos(self.va)
            ab, bb = combos(self.vb)
            u = ba + ab
            if 2 <= x <= 12:
                at = base + x
                gs[x] = (u + (3.0 / 14.0) * bb) + (
                    (self.sy[at] + self.sy[at + 2 * PX]) + 2.0 * self.sy[at + PX]
                )
            hs[x] = aa + ((3.0 / 14.0) * u + (1.0 / 14.0) * bb)
        for i in range(CX):
            b = 2 + 2 * i
            mx = jnp.where(self.x0 + b + 2 == self.nx, 1.0, 2.0).astype(F32)
            raw = (
                (gs[b] + gs[b + 2])
                + 2.0 * (gs[b + 1] + (hs[b] + hs[b + 2]))
                + (hs[b - 1] + hs[b + 3])
                + mx * hs[b + 1]
            ) * (14.0 / 1920.0)
            kr = row_of(self.kr, 3 + 2 * j, b + 1)
            ki = row_of(self.ki, 3 + 2 * j, b + 1)
            c1_out[i, j] = kr * raw + ki * (self.sgn * turned(raw))
            ck_out[0, i, pl.ds(j, 1), :] = self.kr[3 + 2 * j, b + 1 : b + 2, :]
            ck_out[1, i, pl.ds(j, 1), :] = self.ki[3 + 2 * j, b + 1 : b + 2, :]


def middle_kernel(sizes, labels, tab, wave, *refs):
    region = Region(sizes, tab, wave, refs[:12], refs[12:])
    region.tables(labels, LOW, 2 * OWN_Y, 8)
    row_loop(LOW, 2 * OWN_Y, 4, region.first_stage)
    row_loop(LOW + 1, 2 * OWN_Y - 2, 7, region.second_stage)


def low_kernel(sizes, labels, tab, wave, *refs):
    region = Region(sizes, tab, wave, refs[12:24], refs[24:])
    region.tables(labels, 0, LOW, LOW)
    row_loop(0, LOW, 5, region.first_stage)
    row_loop(1, LOW, 5, region.second_stage)


def high_kernel(sizes, labels, tab, wave, *refs):
    region = Region(sizes, tab, wave, refs[12:24], refs[27:])
    c1_out, ck_out, send_out = refs[24:27]
    core, y0, ny = region.core, region.y0, region.ny
    it1 = region.it1
    top = LOW + 2 * OWN_Y
    region.tables(labels, top, PY - top, PY - top)
    row_loop(top, PY - top, 3, region.first_stage)
    row_loop(top - 1, PY - top, 3, region.second_stage)

    @pl.when(y0 + top == ny)
    def _():
        for x in range(1, 14):
            for ref in (region.va, region.vb):
                ref[(top + 1) * PX + x] = -ref[(top - 1) * PX + x]

    for k in range(2):
        for i in range(CX):
            ck_out[k, i, 8:16, :] = jnp.zeros((8, LANES), F32)
    row_loop(0, CY, 1, lambda j: region.third_stage(j, c1_out, ck_out))

    j0 = 4 - 4 * core
    for i in range(CX):
        for j in range(NJ):
            send_out[i * NJ + j] = c1_out[i, j0 + j]
        for k in range(2):
            send_out[CX * NJ + (k * CX + i) * 2] = ck_out[k, i, 0:8, :]
            send_out[CX * NJ + (k * CX + i) * 2 + 1] = ck_out[k, i, 8:16, :]
    plane = 6 + 3 * core
    ys = LOW + OWN_Y - core * OWN_Y
    edges, faces = [], []
    for k in range(OWN_Y + 2):
        at = ((ys - 1 + k) * PX + plane) * 2
        even = it1[at]
        odd = it1[at + 1]
        ee, fe = edge_face(even, odd + up(odd, region.first))
        eo, fo = edge_face(odd, even + down(even, region.last))
        edges.append((ee, eo))
        faces.append((fe, fo))
    for k in range(OWN_Y):
        for h in range(2):
            send_out[CX * NJ + 4 * CX + 2 * k + h] = faces[k + 1][h] + (
                edges[k][h] + edges[k + 2][h]
            )


SEND = CX * NJ + 4 * CX + 2 * OWN_Y


class Own(Region):
    def __init__(self, refs):
        (self.ie_r, self.io_r, self.ie_i, self.io_i, self.it1, self.pp, self.qq) = refs
        self.sgn = sign_rows()


def coarse_sums(ref, pp, qq, i, sweep, first, last):
    edges, faces, centres = {}, {}, {}
    for j in range(sweep, NJ - sweep):
        v = ref[i * NJ + j]
        near = up(v, first) + down(v, last)
        edges[j], faces[j] = edge_face(v, near)
        centres[j] = near
    for j in range(sweep + 1, NJ - sweep - 1):
        pp[i * NJ + j] = centres[j] + (faces[j - 1] + faces[j + 1])
        qq[i * NJ + j] = faces[j] + (edges[j - 1] + edges[j + 1])


def own_kernel(*refs):
    own = Own(refs[:7])
    c1_own, ck_own, it2, inv, c1, ck, pp, qq = refs[7:]
    core = where_am_i()[0]
    lanes = lane_iota()
    first = lanes == 0
    last = lanes == LANES - 1

    xb = core * LOW
    yb = LOW + core * OWN_Y
    xe = core * (PX - 1)
    tables = (own.ie_r, own.io_r, own.ie_i, own.io_i)

    def own_stage(k):
        y = yb + k
        for xx in range(OWN_X):
            x = xb + xx
            at = (y * PX + x) * 2
            for h in range(2):
                it2[xx * OWN_Y + k, h] = 3.0 * own.it1[at + h] + own.update(y, x, h)
        for n, ref in enumerate(tables):
            inv[n, pl.ds(k, 1), :] = ref[y, pl.ds(xe, 1), :]

    own_i = CX - core * CX
    for i in range(CX):
        for j in range(NJ):
            c1[(own_i + i) * NJ + j] = c1_own[i, 4 * core + j]
        for k in range(2):
            ck[k, own_i + i] = ck_own[k, i]
    row_loop(
        own_i, CX, 5, lambda i: coarse_sums(c1, pp, qq, i, 0, first, last)
    )
    row_loop(0, OWN_Y, 2, own_stage)


def cycle_kernel(recv, it2, inv, *refs):
    c1, ck, pp, qq, out, cc, parts, o0, o1, stage, sems = refs[4:]
    core = where_am_i()[0]
    lanes = lane_iota()
    first = lanes == 0
    last = lanes == LANES - 1
    sgn = sign_rows()
    j0 = 4 * core
    other_i = core * CX

    def spread(row):
        return jnp.broadcast_to(row, (8, LANES))

    for i in range(CX):
        for j in range(NJ):
            c1[(other_i + i) * NJ + j] = recv[i * NJ + j]
        for k in range(2):
            for h in range(2):
                tile = slice(8 * h, 8 * h + 8)
                ck[k, other_i + i, tile, :] = recv[CX * NJ + (k * CX + i) * 2 + h]

    for sweep, (sum_step, relax_step) in enumerate(((5, 4), (4, 3), (3, 4))):
        ref = c1 if sweep == 0 else cc

        def sums(i, ref=ref, sweep=sweep):
            coarse_sums(ref, pp, qq, i, sweep, first, last)

        if sweep:
            row_loop(sweep, NI - 2 * sweep, sum_step, sums)
        else:
            row_loop(other_i, CX, sum_step, sums)

        def relax(i, ref=ref, sweep=sweep):
            for j in range(sweep + 1, NJ - sweep - 1):
                at = i * NJ + j
                n = (pp[at] + (qq[at - NJ] + qq[at + NJ])) * (14.0 / 120.0)
                kr = spread(ck[0, i, pl.ds(j0 + j, 1), :])
                ki = spread(ck[1, i, pl.ds(j0 + j, 1), :])
                cc[at] = (0.2 * ref[at] + c1[at]) + (kr * n + ki * (sgn * turned(n)))

        row_loop(sweep + 1, NI - 2 * sweep - 2, relax_step, relax)

    flags = {0: jnp.where(core == 0, 1.0, 0.0), OWN_X - 1: jnp.where(core == 1, 1.0, 0.0)}
    added = []
    for k in range(OWN_Y):
        pair = []
        for h in range(2):
            n = recv[CX * NJ + 4 * CX + 2 * k + h]
            ir = spread(inv[h, k : k + 1, :])
            ii = spread(inv[2 + h, k : k + 1, :])
            pair.append(ir * n + ii * (sgn * turned(n)))
        added.append(pair)

    rows = lax.broadcasted_iota(jnp.int32, (2 * LANES, 2 * LANES), 0)
    cols = lax.broadcasted_iota(jnp.int32, (2 * LANES, 2 * LANES), 1)
    target = jnp.where(rows < LANES, 2 * rows, 2 * (rows - LANES) + 1)
    perm = jnp.where(cols == target, 1.0, 0.0).astype(jnp.bfloat16)

    def fine(x, y, value):
        col = x * OWN_Y + y
        even = it2[col, 0] + 0.5 * (value + up(value, first))
        odd = it2[col, 1] + value
        if x in flags:
            even = even + flags[x] * added[y][0]
            odd = odd + flags[x] * added[y][1]
        return even, odd

    size = 2 * OWN_Y * 8
    copies = []
    for i in range(OWN_X // 2):
        for j in range(OWN_Y // 2):
            at = (i + 4) * NJ + j + 4
            here = cc[at]
            left = cc[at - NJ]
            mix = 0.5 * (left + here)
            below = cc[at - 1]
            mix_below = 0.5 * (cc[at - NJ - 1] + below)
            for x in range(2):
                lower, upper = (
                    (0.5 * (mix_below + mix), mix),
                    (0.5 * (below + here), here),
                )[x]
                a = fine(2 * i + x, 2 * j, lower)
                b = fine(2 * i + x, 2 * j + 1, upper)
                for h in range(2):
                    value = jnp.concatenate([a[h], b[h]], axis=0)
                    top = value.astype(jnp.bfloat16)
                    rest = (value - top.astype(F32)).astype(jnp.bfloat16)
                    start = i * 2 * size + (x * OWN_Y + 2 * j) * 8
                    half = slice(h * LANES, h * LANES + LANES)
                    parts[start : start + 16, half] = top
                    parts[start + size : start + size + 16, half] = rest
        mixed = jnp.dot(
            parts[i * 2 * size : (i + 1) * 2 * size, :], perm, preferred_element_type=F32
        )
        rows_in = 2 * OWN_Y
        for n in range(rows_in):
            block = mixed[n * 8 : n * 8 + 8] + mixed[size + n * 8 : size + n * 8 + 8]
            o0[pl.ds(i * size + n, 8, stride=rows_in), :] = block[:, :LANES]
            o1[pl.ds(i * size + n, 8, stride=rows_in), :] = block[:, LANES:]
        for f in range(8):
            take = slice(i * size + f * rows_in, i * size + (f + 1) * rows_in)
            stage[i, f, :, :LANES] = o0[take]
            stage[i, f, :, LANES:] = o1[take]
        copies.append(
            pltpu.make_async_copy(
                stage.at[i], out.at[:, pl.ds(i * rows_in, rows_in), :], sems.at[i]
            )
        )
        copies[-1].start()
    for copy in copies:
        copy.wait()


def vmem(*shape):
    return pltpu.VMEM(shape, F32)


SPEC = pl.BlockSpec(memory_space=pltpu.VMEM)
CELLS = PY * PX
SHARED = (vmem(PY, PX, LANES),) * 6 + (vmem(CELLS * 2, 8, LANES),) * 3 + (
    vmem(CELLS, 8, LANES),
) * 3
TABLES = [vmem(PY, PX, LANES)] * 6


def limit(mib):
    return pltpu.CompilerParams(vmem_limit_bytes=mib << 20)


def near_core(*arrays):
    return [pltpu.with_memory_space_constraint(a, pltpu.VMEM) for a in arrays]


def stay_call(labels):
    return pl.pallas_call(
        stay_kernel,
        out_shape=pltpu.VMEM(labels.shape, labels.dtype),
        in_specs=[pl.BlockSpec(memory_space=pltpu.HBM)],
        out_specs=SPEC,
        scratch_shapes=[pltpu.SemaphoreType.DMA(())],
        compiler_params=limit(1),
    )(pltpu.with_memory_space_constraint(labels, pltpu.HBM))


def wave_call(real, imag, angles, picks, after):
    small = pl.BlockSpec(memory_space=pltpu.HBM)
    return pl.pallas_call(
        wave_kernel,
        out_shape=(vmem(CELLS * 2, 8, LANES), vmem(8, LANES)),
        in_specs=[small] * 4 + [SPEC],
        out_specs=(SPEC,) * 2,
        scratch_shapes=[
            pltpu.SMEM(a.shape, a.dtype) for a in (real, imag, angles, picks)
        ]
        + [pltpu.SemaphoreType.DMA((4,))],
        compiler_params=limit(6),
    )(
        *(pltpu.with_memory_space_constraint(a, pltpu.HBM) for a in (real, imag, angles, picks)),
        *near_core(after),
    )


def middle_call(sizes, labels, tab, wave):
    def kernel(*refs):
        middle_kernel(sizes, *refs)

    return pl.pallas_call(
        kernel,
        out_shape=SHARED,
        in_specs=[SPEC] * 3,
        out_specs=(SPEC,) * 12,
        scratch_shapes=TABLES + [vmem(2 * OWN_Y * PX, 2 * LANES)],
        compiler_params=limit(6),
    )(*near_core(labels, tab, wave))


def low_call(sizes, labels, tab, wave, shared):
    def kernel(*refs):
        low_kernel(sizes, *refs)

    return pl.pallas_call(
        kernel,
        out_shape=SHARED,
        in_specs=[SPEC] * 15,
        out_specs=(SPEC,) * 12,
        input_output_aliases={3 + n: n for n in range(12)},
        scratch_shapes=TABLES + [vmem(LOW * PX, 2 * LANES)],
        compiler_params=limit(6),
    )(*near_core(labels, tab, wave), *shared)


def high_call(sizes, labels, tab, wave, shared):
    def kernel(*refs):
        high_kernel(sizes, *refs)

    results = pl.pallas_call(
        kernel,
        out_shape=SHARED
        + (
            vmem(CX, CY, 8, LANES),
            vmem(2, CX, 16, LANES),
            vmem(SEND, 8, LANES),
        ),
        in_specs=[SPEC] * 15,
        out_specs=(SPEC,) * 15,
        input_output_aliases={3 + n: n for n in range(12)},
        scratch_shapes=TABLES + [vmem(LOW * PX, 2 * LANES)],
        compiler_params=limit(6),
    )(*near_core(labels, tab, wave), *shared)
    return results[:12], results[12:]


POINTS = NI * NJ
HALF = (vmem(POINTS, 8, LANES), vmem(2, NI, 16, LANES)) + (vmem(POINTS, 8, LANES),) * 2


def own_call(shared, c1, ck):
    used = shared[:4] + shared[6:9]
    results = pl.pallas_call(
        own_kernel,
        out_shape=(vmem(OWN_X * OWN_Y, 2, 8, LANES), vmem(4, 8, LANES)) + HALF,
        in_specs=[SPEC] * 9,
        out_specs=(SPEC,) * 6,
        compiler_params=limit(6),
    )(*used, c1, ck)
    return results[:2], results[2:]


def cycle_call(recv, block, half):
    rows = OWN_X * OWN_Y * 8
    results = pl.pallas_call(
        cycle_kernel,
        out_shape=HALF
        + (jax.ShapeDtypeStruct((8, OWN_X * OWN_Y, 2 * LANES), F32),),
        in_specs=[SPEC] * 7,
        out_specs=(SPEC,) * 4 + (pl.BlockSpec(memory_space=pltpu.HBM),),
        input_output_aliases={3 + n: n for n in range(4)},
        scratch_shapes=[vmem(POINTS, 8, LANES)]
        + [pltpu.VMEM((2 * rows, 2 * LANES), jnp.bfloat16)]
        + [vmem(rows, LANES)] * 2
        + [vmem(OWN_X // 2, 8, 2 * OWN_Y, 2 * LANES), pltpu.SemaphoreType.DMA((3,))],
        compiler_params=limit(8),
    )(*near_core(recv), *block, *half)
    return results[4]


def body(labels, permittivity_real, permittivity_imag, angles, angle_pick):
    gx_n = lax.axis_size("gx")
    gy_n = lax.axis_size("gy")
    core = lax.axis_index("gy") % 2
    is_low = core == 0

    def along_x(values, by):
        pairs = []
        for j in range(gy_n):
            step = by if j % 2 == 0 else -by
            for i in range(gx_n):
                if 0 <= i + step < gx_n:
                    pairs.append(((i + step) * gy_n + j, i * gy_n + j))
        return lax.ppermute(values, ("gx", "gy"), pairs)

    def along_y(values, by):
        pairs = [(j, j + by) for j in range(gy_n) if 0 <= j + by < gy_n]
        return lax.ppermute(values, "gy", pairs)

    def core_swap(values):
        return lax.ppermute(values, "gy", [(j, j ^ 1) for j in range(gy_n)])

    other = core_swap(labels)
    labels = stay_call(labels)
    both = jnp.where(
        is_low,
        jnp.concatenate([labels, other], axis=1),
        jnp.concatenate([other, labels], axis=1),
    )
    both = with_layout_constraint(both, Layout((0, 1, 2)))
    far = along_x(jnp.where(is_low, both[:4], both[2:]), 2)
    near = along_x(both, 1)
    near = with_layout_constraint(near, Layout((0, 1, 2)))
    far = with_layout_constraint(far, Layout((0, 1, 2)))
    region = jnp.where(
        is_low,
        jnp.concatenate([both, near, far], axis=0),
        jnp.concatenate([far, near, both], axis=0),
    )
    region = jnp.transpose(region, (1, 0, 2))
    low = along_y(region[2 * OWN_Y - LOW :], 2)
    high = along_y(region[: PY - LOW - 2 * OWN_Y], -2)

    wave, table = wave_call(
        permittivity_real, permittivity_imag, angles, angle_pick, both
    )
    sizes = (OWN_X * gx_n, OWN_Y * gy_n)
    shared = middle_call(sizes, region, table, wave)
    shared = low_call(sizes, low, table, wave, shared)
    shared, (c1, ck, send) = high_call(sizes, high, table, wave, shared)
    recv = core_swap(send)
    block, half = own_call(shared, c1, ck)
    out = cycle_call(recv, block, half)
    return out.reshape(2, 4, OWN_X, OWN_Y, 2 * LANES)


def solution(mesh):
    return jax.shard_map(
        body,
        mesh=mesh,
        in_specs=(P("gx", "gy", None), P(), P(), P(), P()),
        out_specs=P(None, None, "gx", "gy", None),
        check_vma=False,
    )
```

```python
import jax
import jax.numpy as jnp
import numpy as np
from jax import lax
from jax.experimental import pallas as pl
from jax.experimental.pallas import tpu as pltpu
from jax.experimental.layout import Layout, with_layout_constraint
from jax.sharding import PartitionSpec as P

MAT = 8
DAMPING = 0.8
WAVE_SQUARED = 0.1
SHIFT_IMAG = 0.5
SOURCE_GAIN = 4.0

OWN_X = 6
OWN_Y = 8
PX = 16
PY = 35
LOW = 10
CX, CY = 5, 15
EARLY = 10
NI, NJ = 10, 11
LANES = 128
F32 = jnp.float32
OUTSIDE = 8
WAVENUMBER = float(np.sqrt(np.float32(WAVE_SQUARED)))


def lane_iota():
    return lax.broadcasted_iota(jnp.int32, (8, LANES), 1)


def sign_rows():
    rows = lax.broadcasted_iota(jnp.int32, (8, LANES), 0)
    return jnp.where(rows < 4, -1.0, 1.0).astype(F32)


def up(values, first):
    return jnp.where(first, 0.0, pltpu.roll(values, 1, 1))


def down(values, last):
    return jnp.where(last, 0.0, pltpu.roll(values, LANES - 1, 1))


def turned(values):
    return pltpu.roll(values, 4, 0)


def row_of(ref, y, x):
    return jnp.broadcast_to(ref[y, pl.ds(x, 1), :], (8, LANES))


def edge_face(values, near):
    edge = (3.0 / 14.0) * (values + (1.0 / 3.0) * near)
    face = values + (3.0 / 14.0) * near
    return edge, face


UPDATE_SCALE = 2.5 * 14.0 * DAMPING / 30.0


def fine_diagonal(er, ei):
    real = 128.0 / 30.0 - WAVE_SQUARED * (er + SHIFT_IMAG * ei)
    imag = WAVE_SQUARED * (SHIFT_IMAG * er - ei)
    return real, imag


def scaled_inverse(real, imag, scale, keep):
    ratio = jnp.where(keep, scale / (real * real + imag * imag), 0.0)
    return real * ratio, -imag * ratio


def where_am_i():
    gx = lax.axis_index("gx")
    gy = lax.axis_index("gy")
    core = lax.rem(gy, 2)
    x0 = OWN_X * gx - LOW * core
    y0 = OWN_Y * (gy - core) - LOW
    return core, x0, y0


def stay_kernel(labels, held, sem):
    copy = pltpu.make_async_copy(labels, held, sem)
    copy.start()
    copy.wait()


def splat(value):
    return jnp.full((8, LANES), value, F32)


def wave_kernel(
    real_in, imag_in, angles_in, picks_in, after, wave, tab, real, imag, angles, picks, sems
):
    del after
    copies = [
        pltpu.make_async_copy(src, dst, sems.at[n])
        for n, (src, dst) in enumerate(
            (
                (real_in, real),
                (imag_in, imag),
                (angles_in, angles),
                (picks_in, picks),
            )
        )
    ]
    for copy in copies:
        copy.start()
    for copy in copies:
        copy.wait()
    _, x0, y0 = where_am_i()
    lanes = lane_iota()
    rows = lax.broadcasted_iota(jnp.int32, (8, LANES), 0)

    er = jnp.ones((8, LANES), F32)
    ei = jnp.zeros((8, LANES), F32)
    for m in range(MAT):
        er = jnp.where(lanes == m, splat(real[m]), er)
        ei = jnp.where(lanes == m, splat(imag[m]), ei)
    tab[0:1, :] = er[0:1]
    tab[1:2, :] = ei[0:1]

    incidence = jnp.zeros((8, LANES), F32)
    for c in range(4):
        mine = jnp.bitwise_and(rows, 3) == c
        incidence = jnp.where(mine, splat(angles[picks[c]]), incidence)
    in_x = lanes < PX
    place = jnp.where(in_x, x0 + lanes, y0 + (lanes - PX)).astype(F32)
    slope = jnp.where(in_x, jnp.cos(incidence), jnp.sin(incidence))
    phases = WAVENUMBER * (slope * place)
    cosine = jnp.cos(phases)
    sine = jnp.sin(phases)
    upper = rows < 4
    front = jnp.where(upper, cosine, sine)
    turn = jnp.where(upper, -sine, cosine)

    def along(values, n):
        return jnp.broadcast_to(values[:, n : n + 1], (8, LANES))

    for x in range(PX):
        wave[x * 2] = along(cosine, x)
        wave[x * 2 + 1] = along(sine, x)
    for y in reversed(range(PY)):
        w = along(front, PX + y)
        w_t = along(turn, PX + y)
        for x in range(PX):
            c = wave[x * 2]
            s = wave[x * 2 + 1]
            wave[(y * PX + x) * 2] = c * w + s * w_t
            wave[(y * PX + x) * 2 + 1] = c * w_t - s * w


def row_loop(first, count, step, body):
    def some(n, carry):
        for k in range(step):
            body(first + n * step + k)
        return carry

    lax.fori_loop(0, count // step, some, 0)


class Region:
    def __init__(self, sizes, tab, wave, shared, scratch):
        self.nx, self.ny = sizes
        self.core, self.x0, self.y0 = where_am_i()
        self.tab = tab
        self.wave = wave
        (self.ie_r, self.io_r, self.ie_i, self.io_i, self.kr, self.ki,
         self.it1, self.pp, self.qq, self.va, self.vb, self.sy) = shared
        (self.ge_r, self.go_r, self.ge_i, self.go_i, self.sa_r, self.sa_i,
         self.apart) = scratch
        lanes = lane_iota()
        self.first = lanes == 0
        self.last = lanes == LANES - 1
        self.sgn = sign_rows()
        rows = lax.broadcasted_iota(jnp.int32, (2 * LANES, 2 * LANES), 0)
        cols = lax.broadcasted_iota(jnp.int32, (2 * LANES, 2 * LANES), 1)
        source = jnp.where(cols < LANES, 2 * cols, 2 * (cols - LANES) + 1)
        self.perm = jnp.where(rows == source, 1.0, 0.0).astype(jnp.bfloat16)

    def pick(self, row, index):
        table = jnp.broadcast_to(self.tab[row : row + 1, :], (8, LANES))
        return jnp.take_along_axis(table, index, axis=1, mode="promise_in_bounds")

    def tables(self, labels, first_row, count, step):
        flat = labels[...].reshape(count * PX, 2 * LANES).astype(F32).astype(jnp.bfloat16)
        self.apart[0 : count * PX, :] = jnp.dot(
            flat, self.perm, preferred_element_type=F32
        )
        rows = lax.broadcasted_iota(jnp.int32, (8, LANES), 0)
        inside = []
        for h in range(2):
            xs = self.x0 + 8 * h + rows
            inside.append(jnp.logical_and(xs >= 0, xs < self.nx))

        def some(n, carry):
            for k in range(step):
                y = first_row + n * step + k
                y_in = jnp.logical_and(self.y0 + y >= 0, self.y0 + y < self.ny)
                for h in range(2):
                    start = pl.multiple_of((n * step + k) * PX + 8 * h, 8)
                    part = self.apart[pl.ds(start, 8), :]
                    at = (y, pl.ds(8 * h, 8), slice(None))
                    keep = jnp.logical_and(inside[h], y_in)
                    sources = []
                    for odd, (inv_r, inv_i, g_r, g_i) in enumerate(
                        (
                            (self.ie_r, self.ie_i, self.ge_r, self.ge_i),
                            (self.io_r, self.io_i, self.go_r, self.go_i),
                        )
                    ):
                        label = part[:, odd * LANES : (odd + 1) * LANES].astype(jnp.int32)
                        index = jnp.where(keep, label, OUTSIDE)
                        er = self.pick(0, index)
                        ei = self.pick(1, index)
                        real, imag = fine_diagonal(er, ei)
                        ir, ii = scaled_inverse(real, imag, UPDATE_SCALE, keep)
                        sr, si = 1.2 * SOURCE_GAIN * (er - 1.0), 1.2 * SOURCE_GAIN * ei
                        inv_r[at] = ir
                        inv_i[at] = ii
                        g_r[at] = (4.0 / 14.0) * (ir * sr - ii * si)
                        g_i[at] = (4.0 / 14.0) * (ir * si + ii * sr)
                        sources.append((sr, si))
                        if odd and (first_row + k) % 2 == 1:
                            kr, ki = scaled_inverse(
                                real + (128.0 / 120.0 - 128.0 / 30.0), imag, DAMPING, keep
                            )
                            self.kr[at] = kr
                            self.ki[at] = ki
                    for c, out in ((0, self.sa_r), (1, self.sa_i)):
                        se = sources[0][c]
                        out[at] = (se + down(se, self.last) + 2.0 * sources[1][c]) * (1.0 / 14.0)
            return carry

        lax.fori_loop(0, count // step, some, 0)

    def first_stage(self, y):
        edges, faces, centres = [[], []], [[], []], [[], []]
        for x in range(PX):
            at = (y * PX + x) * 2
            e = self.wave[at]
            e_t = self.wave[at + 1]
            even = row_of(self.ge_r, y, x) * e + row_of(self.ge_i, y, x) * e_t
            odd = row_of(self.go_r, y, x) * e + row_of(self.go_i, y, x) * e_t
            if 2 <= x <= 12:
                self.sy[y * PX + x] = (
                    row_of(self.sa_r, y, x) * e + row_of(self.sa_i, y, x) * e_t
                )
            self.it1[at] = even
            self.it1[at + 1] = odd
            near_e = odd + up(odd, self.first)
            near_o = even + down(even, self.last)
            for h, (v, near) in enumerate(((even, near_e), (odd, near_o))):
                edge, face = edge_face(v, near)
                edges[h].append(edge)
                faces[h].append(face)
                centres[h].append(near)
        for x in range(PX):
            at = (y * PX + x) * 2
            for h in range(2):
                p = centres[h][x]
                q = faces[h][x]
                if 0 < x < PX - 1:
                    p = p + (faces[h][x - 1] + faces[h][x + 1])
                    q = q + (edges[h][x - 1] + edges[h][x + 1])
                else:
                    beside = x - 1 if x else x + 1
                    p = p + faces[h][beside]
                    q = q + edges[h][beside]
                self.pp[at + h] = p
                self.qq[at + h] = q

    def update(self, y, x, h):
        at = (y * PX + x) * 2 + h
        row = PX * 2
        ir, ii = ((self.ie_r, self.ie_i), (self.io_r, self.io_i))[h]
        n = self.pp[at] + (self.qq[at - row] + self.qq[at + row])
        return row_of(ir, y, x) * n + row_of(ii, y, x) * (self.sgn * turned(n))

    def second_stage(self, y):
        for x in range(1, 14):
            at = (y * PX + x) * 2
            we = self.it1[at] + self.update(y, x, 0)
            wo = self.it1[at + 1] + self.update(y, x, 1)
            p = we + down(we, self.last)
            half = p + wo
            after = jnp.where(self.last, -wo, pltpu.roll(wo, LANES - 1, 1))
            self.va[y * PX + x] = half + wo
            self.vb[y * PX + x] = (up(wo, self.first) + after) + 2.0 * half

    def third_stage(self, j, c1_out, ck_out):
        base = (2 + 2 * j) * PX
        gs, hs = {}, {}
        for x in range(1, 14):

            def combos(ref):
                vm, v0, v1, v2, v3 = (ref[base + (d - 1) * PX + x] for d in range(5))
                half = (v0 + v2) + v1
                return half + v1, (vm + v3) + 2.0 * half

            aa, ba = combos(self.va)
            ab, bb = combos(self.vb)
            u = ba + ab
            if 2 <= x <= 12:
                at = base + x
                gs[x] = (u + (3.0 / 14.0) * bb) + (
                    (self.sy[at] + self.sy[at + 2 * PX]) + 2.0 * self.sy[at + PX]
                )
            hs[x] = aa + ((3.0 / 14.0) * u + (1.0 / 14.0) * bb)
        for i in range(CX):
            b = 2 + 2 * i
            mx = jnp.where(self.x0 + b + 2 == self.nx, 1.0, 2.0).astype(F32)
            raw = (
                (gs[b] + gs[b + 2])
                + 2.0 * (gs[b + 1] + (hs[b] + hs[b + 2]))
                + (hs[b - 1] + hs[b + 3])
                + mx * hs[b + 1]
            ) * (14.0 / 1920.0)
            kr = row_of(self.kr, 3 + 2 * j, b + 1)
            ki = row_of(self.ki, 3 + 2 * j, b + 1)
            c1_out[i, j] = kr * raw + ki * (self.sgn * turned(raw))
            ck_out[0, i, pl.ds(j, 1), :] = self.kr[3 + 2 * j, b + 1 : b + 2, :]
            ck_out[1, i, pl.ds(j, 1), :] = self.ki[3 + 2 * j, b + 1 : b + 2, :]


def middle_kernel(sizes, labels, tab, wave, *refs):
    region = Region(sizes, tab, wave, refs[:12], refs[12:])
    region.tables(labels, LOW, 2 * OWN_Y, 8)
    row_loop(LOW, 2 * OWN_Y, 4, region.first_stage)
    row_loop(LOW + 1, 2 * OWN_Y - 2, 7, region.second_stage)


def low_kernel(sizes, labels, tab, wave, *refs):
    region = Region(sizes, tab, wave, refs[12:24], refs[26:])
    c1_out, ck_out = refs[24:26]
    region.tables(labels, 0, LOW, LOW)
    row_loop(0, LOW, 5, region.first_stage)
    row_loop(1, LOW, 5, region.second_stage)
    for k in range(2):
        for i in range(CX):
            ck_out[k, i, 8:16, :] = jnp.zeros((8, LANES), F32)
    row_loop(0, EARLY, 1, lambda j: region.third_stage(j, c1_out, ck_out))


def high_kernel(sizes, labels, tab, wave, *refs):
    region = Region(sizes, tab, wave, refs[14:26], refs[29:])
    c1_out, ck_out, send_out = refs[26:29]
    core, y0, ny = region.core, region.y0, region.ny
    it1 = region.it1
    top = LOW + 2 * OWN_Y
    region.tables(labels, top, PY - top, PY - top)
    row_loop(top, PY - top, 3, region.first_stage)
    row_loop(top - 1, PY - top, 3, region.second_stage)

    @pl.when(y0 + top == ny)
    def _():
        for x in range(1, 14):
            for ref in (region.va, region.vb):
                ref[(top + 1) * PX + x] = -ref[(top - 1) * PX + x]

    row_loop(EARLY, CY - EARLY, 1, lambda j: region.third_stage(j, c1_out, ck_out))

    j0 = 4 - 4 * core
    for i in range(CX):
        for j in range(NJ):
            send_out[i * NJ + j] = c1_out[i, j0 + j]
        for k in range(2):
            send_out[CX * NJ + (k * CX + i) * 2] = ck_out[k, i, 0:8, :]
            send_out[CX * NJ + (k * CX + i) * 2 + 1] = ck_out[k, i, 8:16, :]
    plane = 6 + 3 * core
    ys = LOW + OWN_Y - core * OWN_Y
    edges, faces = [], []
    for k in range(OWN_Y + 2):
        at = ((ys - 1 + k) * PX + plane) * 2
        even = it1[at]
        odd = it1[at + 1]
        ee, fe = edge_face(even, odd + up(odd, region.first))
        eo, fo = edge_face(odd, even + down(even, region.last))
        edges.append((ee, eo))
        faces.append((fe, fo))
    for k in range(OWN_Y):
        for h in range(2):
            send_out[CX * NJ + 4 * CX + 2 * k + h] = faces[k + 1][h] + (
                edges[k][h] + edges[k + 2][h]
            )


SEND = CX * NJ + 4 * CX + 2 * OWN_Y


class Own(Region):
    def __init__(self, refs):
        (self.ie_r, self.io_r, self.ie_i, self.io_i, self.it1, self.pp, self.qq) = refs
        self.sgn = sign_rows()


def coarse_sums(ref, pp, qq, i, sweep, first, last):
    edges, faces, centres = {}, {}, {}
    for j in range(sweep, NJ - sweep):
        v = ref[i * NJ + j]
        near = up(v, first) + down(v, last)
        edges[j], faces[j] = edge_face(v, near)
        centres[j] = near
    for j in range(sweep + 1, NJ - sweep - 1):
        pp[i * NJ + j] = centres[j] + (faces[j - 1] + faces[j + 1])
        qq[i * NJ + j] = faces[j] + (edges[j - 1] + edges[j + 1])


def own_kernel(*refs):
    own = Own(refs[:7])
    c1_own, ck_own, it2, inv, c1, ck, pp, qq = refs[7:]
    core = where_am_i()[0]
    lanes = lane_iota()
    first = lanes == 0
    last = lanes == LANES - 1

    xb = core * LOW
    yb = LOW + core * OWN_Y
    xe = core * (PX - 1)
    tables = (own.ie_r, own.io_r, own.ie_i, own.io_i)

    def own_stage(k):
        y = yb + k
        for xx in range(OWN_X):
            x = xb + xx
            at = (y * PX + x) * 2
            for h in range(2):
                it2[xx * OWN_Y + k, h] = 3.0 * own.it1[at + h] + own.update(y, x, h)
        for n, ref in enumerate(tables):
            inv[n, pl.ds(k, 1), :] = ref[y, pl.ds(xe, 1), :]

    own_i = CX - core * CX
    for i in range(CX):
        for j in range(NJ):
            c1[(own_i + i) * NJ + j] = c1_own[i, 4 * core + j]
        for k in range(2):
            ck[k, own_i + i] = ck_own[k, i]
    row_loop(
        own_i, CX, 5, lambda i: coarse_sums(c1, pp, qq, i, 0, first, last)
    )
    row_loop(0, OWN_Y, 2, own_stage)


def cycle_kernel(recv, it2, inv, *refs):
    c1, ck, pp, qq, out, cc, parts, o0, o1, stage, sems = refs[4:]
    core = where_am_i()[0]
    lanes = lane_iota()
    first = lanes == 0
    last = lanes == LANES - 1
    sgn = sign_rows()
    j0 = 4 * core
    other_i = core * CX

    def spread(row):
        return jnp.broadcast_to(row, (8, LANES))

    for i in range(CX):
        for j in range(NJ):
            c1[(other_i + i) * NJ + j] = recv[i * NJ + j]
        for k in range(2):
            for h in range(2):
                tile = slice(8 * h, 8 * h + 8)
                ck[k, other_i + i, tile, :] = recv[CX * NJ + (k * CX + i) * 2 + h]

    for sweep, (sum_step, relax_step) in enumerate(((5, 4), (4, 3), (3, 4))):
        ref = c1 if sweep == 0 else cc

        def sums(i, ref=ref, sweep=sweep):
            coarse_sums(ref, pp, qq, i, sweep, first, last)

        if sweep:
            row_loop(sweep, NI - 2 * sweep, sum_step, sums)
        else:
            row_loop(other_i, CX, sum_step, sums)

        def relax(i, ref=ref, sweep=sweep):
            for j in range(sweep + 1, NJ - sweep - 1):
                at = i * NJ + j
                n = (pp[at] + (qq[at - NJ] + qq[at + NJ])) * (14.0 / 120.0)
                kr = spread(ck[0, i, pl.ds(j0 + j, 1), :])
                ki = spread(ck[1, i, pl.ds(j0 + j, 1), :])
                cc[at] = (0.2 * ref[at] + c1[at]) + (kr * n + ki * (sgn * turned(n)))

        row_loop(sweep + 1, NI - 2 * sweep - 2, relax_step, relax)

    flags = {0: jnp.where(core == 0, 1.0, 0.0), OWN_X - 1: jnp.where(core == 1, 1.0, 0.0)}
    added = []
    for k in range(OWN_Y):
        pair = []
        for h in range(2):
            n = recv[CX * NJ + 4 * CX + 2 * k + h]
            ir = spread(inv[h, k : k + 1, :])
            ii = spread(inv[2 + h, k : k + 1, :])
            pair.append(ir * n + ii * (sgn * turned(n)))
        added.append(pair)

    rows = lax.broadcasted_iota(jnp.int32, (2 * LANES, 2 * LANES), 0)
    cols = lax.broadcasted_iota(jnp.int32, (2 * LANES, 2 * LANES), 1)
    target = jnp.where(rows < LANES, 2 * rows, 2 * (rows - LANES) + 1)
    perm = jnp.where(cols == target, 1.0, 0.0).astype(jnp.bfloat16)

    def fine(x, y, value):
        col = x * OWN_Y + y
        even = it2[col, 0] + 0.5 * (value + up(value, first))
        odd = it2[col, 1] + value
        if x in flags:
            even = even + flags[x] * added[y][0]
            odd = odd + flags[x] * added[y][1]
        return even, odd

    size = 2 * OWN_Y * 8
    copies = []
    for i in range(OWN_X // 2):
        for j in range(OWN_Y // 2):
            at = (i + 4) * NJ + j + 4
            here = cc[at]
            left = cc[at - NJ]
            mix = 0.5 * (left + here)
            below = cc[at - 1]
            mix_below = 0.5 * (cc[at - NJ - 1] + below)
            for x in range(2):
                lower, upper = (
                    (0.5 * (mix_below + mix), mix),
                    (0.5 * (below + here), here),
                )[x]
                a = fine(2 * i + x, 2 * j, lower)
                b = fine(2 * i + x, 2 * j + 1, upper)
                for h in range(2):
                    value = jnp.concatenate([a[h], b[h]], axis=0)
                    top = value.astype(jnp.bfloat16)
                    rest = (value - top.astype(F32)).astype(jnp.bfloat16)
                    start = i * 2 * size + (x * OWN_Y + 2 * j) * 8
                    half = slice(h * LANES, h * LANES + LANES)
                    parts[start : start + 16, half] = top
                    parts[start + size : start + size + 16, half] = rest
        mixed = jnp.dot(
            parts[i * 2 * size : (i + 1) * 2 * size, :], perm, preferred_element_type=F32
        )
        rows_in = 2 * OWN_Y
        for n in range(rows_in):
            block = mixed[n * 8 : n * 8 + 8] + mixed[size + n * 8 : size + n * 8 + 8]
            o0[pl.ds(i * size + n, 8, stride=rows_in), :] = block[:, :LANES]
            o1[pl.ds(i * size + n, 8, stride=rows_in), :] = block[:, LANES:]
        for f in range(8):
            take = slice(i * size + f * rows_in, i * size + (f + 1) * rows_in)
            stage[i, f, :, :LANES] = o0[take]
            stage[i, f, :, LANES:] = o1[take]
        copies.append(
            pltpu.make_async_copy(
                stage.at[i], out.at[:, pl.ds(i * rows_in, rows_in), :], sems.at[i]
            )
        )
        copies[-1].start()
    for copy in copies:
        copy.wait()


def vmem(*shape):
    return pltpu.VMEM(shape, F32)


SPEC = pl.BlockSpec(memory_space=pltpu.VMEM)
CELLS = PY * PX
SHARED = (vmem(PY, PX, LANES),) * 6 + (vmem(CELLS * 2, 8, LANES),) * 3 + (
    vmem(CELLS, 8, LANES),
) * 3
COARSE = (vmem(CX, CY, 8, LANES), vmem(2, CX, 16, LANES))
TABLES = [vmem(PY, PX, LANES)] * 6


def limit(mib):
    return pltpu.CompilerParams(vmem_limit_bytes=mib << 20)


def near_core(*arrays):
    return [pltpu.with_memory_space_constraint(a, pltpu.VMEM) for a in arrays]


def stay_call(labels):
    return pl.pallas_call(
        stay_kernel,
        out_shape=pltpu.VMEM(labels.shape, labels.dtype),
        in_specs=[pl.BlockSpec(memory_space=pltpu.HBM)],
        out_specs=SPEC,
        scratch_shapes=[pltpu.SemaphoreType.DMA(())],
        compiler_params=limit(1),
    )(pltpu.with_memory_space_constraint(labels, pltpu.HBM))


def wave_call(real, imag, angles, picks, after):
    small = pl.BlockSpec(memory_space=pltpu.HBM)
    return pl.pallas_call(
        wave_kernel,
        out_shape=(vmem(CELLS * 2, 8, LANES), vmem(8, LANES)),
        in_specs=[small] * 4 + [SPEC],
        out_specs=(SPEC,) * 2,
        scratch_shapes=[
            pltpu.SMEM(a.shape, a.dtype) for a in (real, imag, angles, picks)
        ]
        + [pltpu.SemaphoreType.DMA((4,))],
        compiler_params=limit(6),
    )(
        *(pltpu.with_memory_space_constraint(a, pltpu.HBM) for a in (real, imag, angles, picks)),
        *near_core(after),
    )


def middle_call(sizes, labels, tab, wave):
    def kernel(*refs):
        middle_kernel(sizes, *refs)

    return pl.pallas_call(
        kernel,
        out_shape=SHARED,
        in_specs=[SPEC] * 3,
        out_specs=(SPEC,) * 12,
        scratch_shapes=TABLES + [vmem(2 * OWN_Y * PX, 2 * LANES)],
        compiler_params=limit(6),
    )(*near_core(labels, tab, wave))


def low_call(sizes, labels, tab, wave, shared):
    def kernel(*refs):
        low_kernel(sizes, *refs)

    return pl.pallas_call(
        kernel,
        out_shape=SHARED + COARSE,
        in_specs=[SPEC] * 15,
        out_specs=(SPEC,) * 14,
        input_output_aliases={3 + n: n for n in range(12)},
        scratch_shapes=TABLES + [vmem(LOW * PX, 2 * LANES)],
        compiler_params=limit(6),
    )(*near_core(labels, tab, wave), *shared)


def high_call(sizes, labels, tab, wave, shared):
    def kernel(*refs):
        high_kernel(sizes, *refs)

    results = pl.pallas_call(
        kernel,
        out_shape=SHARED + COARSE + (vmem(SEND, 8, LANES),),
        in_specs=[SPEC] * 17,
        out_specs=(SPEC,) * 15,
        input_output_aliases={3 + n: n for n in range(14)},
        scratch_shapes=TABLES + [vmem(LOW * PX, 2 * LANES)],
        compiler_params=limit(6),
    )(*near_core(labels, tab, wave), *shared)
    return results[:12], results[12:]


POINTS = NI * NJ
HALF = (vmem(POINTS, 8, LANES), vmem(2, NI, 16, LANES)) + (vmem(POINTS, 8, LANES),) * 2


def own_call(shared, c1, ck):
    used = shared[:4] + shared[6:9]
    results = pl.pallas_call(
        own_kernel,
        out_shape=(vmem(OWN_X * OWN_Y, 2, 8, LANES), vmem(4, 8, LANES)) + HALF,
        in_specs=[SPEC] * 9,
        out_specs=(SPEC,) * 6,
        compiler_params=limit(6),
    )(*used, c1, ck)
    return results[:2], results[2:]


def cycle_call(recv, block, half):
    rows = OWN_X * OWN_Y * 8
    results = pl.pallas_call(
        cycle_kernel,
        out_shape=HALF
        + (jax.ShapeDtypeStruct((8, OWN_X * OWN_Y, 2 * LANES), F32),),
        in_specs=[SPEC] * 7,
        out_specs=(SPEC,) * 4 + (pl.BlockSpec(memory_space=pltpu.HBM),),
        input_output_aliases={3 + n: n for n in range(4)},
        scratch_shapes=[vmem(POINTS, 8, LANES)]
        + [pltpu.VMEM((2 * rows, 2 * LANES), jnp.bfloat16)]
        + [vmem(rows, LANES)] * 2
        + [vmem(OWN_X // 2, 8, 2 * OWN_Y, 2 * LANES), pltpu.SemaphoreType.DMA((3,))],
        compiler_params=limit(8),
    )(*near_core(recv), *block, *half)
    return results[4]


def body(labels, permittivity_real, permittivity_imag, angles, angle_pick):
    gx_n = lax.axis_size("gx")
    gy_n = lax.axis_size("gy")
    core = lax.axis_index("gy") % 2
    is_low = core == 0

    def along_x(values, by):
        pairs = []
        for j in range(gy_n):
            step = by if j % 2 == 0 else -by
            for i in range(gx_n):
                if 0 <= i + step < gx_n:
                    pairs.append(((i + step) * gy_n + j, i * gy_n + j))
        return lax.ppermute(values, ("gx", "gy"), pairs)

    def along_y(values, by):
        pairs = [(j, j + by) for j in range(gy_n) if 0 <= j + by < gy_n]
        return lax.ppermute(values, "gy", pairs)

    def core_swap(values):
        return lax.ppermute(values, "gy", [(j, j ^ 1) for j in range(gy_n)])

    other = core_swap(labels)
    labels = stay_call(labels)
    both = jnp.where(
        is_low,
        jnp.concatenate([labels, other], axis=1),
        jnp.concatenate([other, labels], axis=1),
    )
    both = with_layout_constraint(both, Layout((0, 1, 2)))
    far = along_x(jnp.where(is_low, both[:4], both[2:]), 2)
    near = along_x(both, 1)
    near = with_layout_constraint(near, Layout((0, 1, 2)))
    far = with_layout_constraint(far, Layout((0, 1, 2)))
    region = jnp.where(
        is_low,
        jnp.concatenate([both, near, far], axis=0),
        jnp.concatenate([far, near, both], axis=0),
    )
    region = jnp.transpose(region, (1, 0, 2))
    low = along_y(region[2 * OWN_Y - LOW :], 2)
    high = along_y(region[: PY - LOW - 2 * OWN_Y], -2)

    wave, table = wave_call(
        permittivity_real, permittivity_imag, angles, angle_pick, both
    )
    sizes = (OWN_X * gx_n, OWN_Y * gy_n)
    shared = middle_call(sizes, region, table, wave)
    shared = low_call(sizes, low, table, wave, shared)
    shared, (c1, ck, send) = high_call(sizes, high, table, wave, shared)
    recv = core_swap(send)
    block, half = own_call(shared, c1, ck)
    out = cycle_call(recv, block, half)
    return out.reshape(2, 4, OWN_X, OWN_Y, 2 * LANES)


def solution(mesh):
    return jax.shard_map(
        body,
        mesh=mesh,
        in_specs=(P("gx", "gy", None), P(), P(), P(), P()),
        out_specs=P(None, None, "gx", "gy", None),
        check_vma=False,
    )
```

```python
import jax
import jax.numpy as jnp
import numpy as np
from jax import lax
from jax.experimental import pallas as pl
from jax.experimental.pallas import tpu as pltpu
from jax.experimental.layout import Layout, with_layout_constraint
from jax.sharding import PartitionSpec as P

MAT = 8
DAMPING = 0.8
WAVE_SQUARED = 0.1
SHIFT_IMAG = 0.5
SOURCE_GAIN = 4.0

OWN_X = 6
OWN_Y = 8
PX = 16
PY = 35
LOW = 10
CX, CY = 5, 15
EARLY = 10
NI, NJ = 10, 11
LANES = 128
F32 = jnp.float32
OUTSIDE = 8
WAVENUMBER = float(np.sqrt(np.float32(WAVE_SQUARED)))


def lane_iota():
    return lax.broadcasted_iota(jnp.int32, (8, LANES), 1)


def sign_rows():
    rows = lax.broadcasted_iota(jnp.int32, (8, LANES), 0)
    return jnp.where(rows < 4, -1.0, 1.0).astype(F32)


def up(values, first):
    return jnp.where(first, 0.0, pltpu.roll(values, 1, 1))


def down(values, last):
    return jnp.where(last, 0.0, pltpu.roll(values, LANES - 1, 1))


def turned(values):
    return pltpu.roll(values, 4, 0)


def row_of(ref, y, x):
    return jnp.broadcast_to(ref[y, pl.ds(x, 1), :], (8, LANES))


def edge_face(values, near):
    edge = (3.0 / 14.0) * (values + (1.0 / 3.0) * near)
    face = values + (3.0 / 14.0) * near
    return edge, face


UPDATE_SCALE = 2.5 * 14.0 * DAMPING / 30.0


def fine_diagonal(er, ei):
    real = 128.0 / 30.0 - WAVE_SQUARED * (er + SHIFT_IMAG * ei)
    imag = WAVE_SQUARED * (SHIFT_IMAG * er - ei)
    return real, imag


def scaled_inverse(real, imag, scale, keep):
    ratio = jnp.where(keep, scale / (real * real + imag * imag), 0.0)
    return real * ratio, -imag * ratio


def where_am_i():
    gx = lax.axis_index("gx")
    gy = lax.axis_index("gy")
    core = lax.rem(gy, 2)
    x0 = OWN_X * gx - LOW * core
    y0 = OWN_Y * (gy - core) - LOW
    return core, x0, y0


def stay_kernel(labels, held, sem):
    copy = pltpu.make_async_copy(labels, held, sem)
    copy.start()
    copy.wait()


def splat(value):
    return jnp.full((8, LANES), value, F32)


def wave_kernel(
    real_in, imag_in, angles_in, picks_in, after, wave, tab, real, imag, angles, picks, sems
):
    del after
    copies = [
        pltpu.make_async_copy(src, dst, sems.at[n])
        for n, (src, dst) in enumerate(
            (
                (real_in, real),
                (imag_in, imag),
                (angles_in, angles),
                (picks_in, picks),
            )
        )
    ]
    for copy in copies:
        copy.start()
    for copy in copies:
        copy.wait()
    _, x0, y0 = where_am_i()
    lanes = lane_iota()
    rows = lax.broadcasted_iota(jnp.int32, (8, LANES), 0)

    er = jnp.ones((8, LANES), F32)
    ei = jnp.zeros((8, LANES), F32)
    for m in range(MAT):
        er = jnp.where(lanes == m, splat(real[m]), er)
        ei = jnp.where(lanes == m, splat(imag[m]), ei)
    tab[0:1, :] = er[0:1]
    tab[1:2, :] = ei[0:1]

    incidence = jnp.zeros((8, LANES), F32)
    for c in range(4):
        mine = jnp.bitwise_and(rows, 3) == c
        incidence = jnp.where(mine, splat(angles[picks[c]]), incidence)
    in_x = lanes < PX
    place = jnp.where(in_x, x0 + lanes, y0 + (lanes - PX)).astype(F32)
    slope = jnp.where(in_x, jnp.cos(incidence), jnp.sin(incidence))
    phases = WAVENUMBER * (slope * place)
    cosine = jnp.cos(phases)
    sine = jnp.sin(phases)
    upper = rows < 4
    front = jnp.where(upper, cosine, sine)
    turn = jnp.where(upper, -sine, cosine)

    def along(values, n):
        return jnp.broadcast_to(values[:, n : n + 1], (8, LANES))

    for x in range(PX):
        wave[x * 2] = along(cosine, x)
        wave[x * 2 + 1] = along(sine, x)
    for y in reversed(range(PY)):
        w = along(front, PX + y)
        w_t = along(turn, PX + y)
        for x in range(PX):
            c = wave[x * 2]
            s = wave[x * 2 + 1]
            wave[(y * PX + x) * 2] = c * w + s * w_t
            wave[(y * PX + x) * 2 + 1] = c * w_t - s * w


def row_loop(first, count, step, body):
    def some(n, carry):
        for k in range(step):
            body(first + n * step + k)
        return carry

    lax.fori_loop(0, count // step, some, 0)


class Region:
    def __init__(self, sizes, tab, wave, shared, scratch):
        self.nx, self.ny = sizes
        self.core, self.x0, self.y0 = where_am_i()
        self.tab = tab
        self.wave = wave
        (self.ie_r, self.io_r, self.ie_i, self.io_i, self.kr, self.ki,
         self.it1, self.pp, self.qq, self.va, self.vb, self.sy) = shared
        (self.ge_r, self.go_r, self.ge_i, self.go_i, self.sa_r, self.sa_i,
         self.apart) = scratch
        lanes = lane_iota()
        self.first = lanes == 0
        self.last = lanes == LANES - 1
        self.sgn = sign_rows()
        rows = lax.broadcasted_iota(jnp.int32, (2 * LANES, 2 * LANES), 0)
        cols = lax.broadcasted_iota(jnp.int32, (2 * LANES, 2 * LANES), 1)
        source = jnp.where(cols < LANES, 2 * cols, 2 * (cols - LANES) + 1)
        self.perm = jnp.where(rows == source, 1.0, 0.0).astype(jnp.bfloat16)

    def pick(self, row, index):
        table = jnp.broadcast_to(self.tab[row : row + 1, :], (8, LANES))
        return jnp.take_along_axis(table, index, axis=1, mode="promise_in_bounds")

    def tables(self, labels, first_row, count, step):
        flat = labels[...].reshape(count * PX, 2 * LANES).astype(F32).astype(jnp.bfloat16)
        self.apart[0 : count * PX, :] = jnp.dot(
            flat, self.perm, preferred_element_type=F32
        )
        rows = lax.broadcasted_iota(jnp.int32, (8, LANES), 0)
        inside = []
        for h in range(2):
            xs = self.x0 + 8 * h + rows
            inside.append(jnp.logical_and(xs >= 0, xs < self.nx))

        def some(n, carry):
            for k in range(step):
                y = first_row + n * step + k
                y_in = jnp.logical_and(self.y0 + y >= 0, self.y0 + y < self.ny)
                for h in range(2):
                    start = pl.multiple_of((n * step + k) * PX + 8 * h, 8)
                    part = self.apart[pl.ds(start, 8), :]
                    at = (y, pl.ds(8 * h, 8), slice(None))
                    keep = jnp.logical_and(inside[h], y_in)
                    sources = []
                    for odd, (inv_r, inv_i, g_r, g_i) in enumerate(
                        (
                            (self.ie_r, self.ie_i, self.ge_r, self.ge_i),
                            (self.io_r, self.io_i, self.go_r, self.go_i),
                        )
                    ):
                        label = part[:, odd * LANES : (odd + 1) * LANES].astype(jnp.int32)
                        index = jnp.where(keep, label, OUTSIDE)
                        er = self.pick(0, index)
                        ei = self.pick(1, index)
                        real, imag = fine_diagonal(er, ei)
                        ir, ii = scaled_inverse(real, imag, UPDATE_SCALE, keep)
                        sr, si = 1.2 * SOURCE_GAIN * (er - 1.0), 1.2 * SOURCE_GAIN * ei
                        inv_r[at] = ir
                        inv_i[at] = ii
                        g_r[at] = (4.0 / 14.0) * (ir * sr - ii * si)
                        g_i[at] = (4.0 / 14.0) * (ir * si + ii * sr)
                        sources.append((sr, si))
                        if odd and (first_row + k) % 2 == 1:
                            kr, ki = scaled_inverse(
                                real + (128.0 / 120.0 - 128.0 / 30.0), imag, DAMPING, keep
                            )
                            self.kr[at] = kr
                            self.ki[at] = ki
                    for c, out in ((0, self.sa_r), (1, self.sa_i)):
                        se = sources[0][c]
                        out[at] = (se + down(se, self.last) + 2.0 * sources[1][c]) * (1.0 / 14.0)
            return carry

        lax.fori_loop(0, count // step, some, 0)

    def first_stage(self, y):
        edges, faces, centres = [[], []], [[], []], [[], []]
        for x in range(PX):
            at = (y * PX + x) * 2
            e = self.wave[at]
            e_t = self.wave[at + 1]
            even = row_of(self.ge_r, y, x) * e + row_of(self.ge_i, y, x) * e_t
            odd = row_of(self.go_r, y, x) * e + row_of(self.go_i, y, x) * e_t
            if 2 <= x <= 12:
                self.sy[y * PX + x] = (
                    row_of(self.sa_r, y, x) * e + row_of(self.sa_i, y, x) * e_t
                )
            self.it1[at] = even
            self.it1[at + 1] = odd
            near_e = odd + up(odd, self.first)
            near_o = even + down(even, self.last)
            for h, (v, near) in enumerate(((even, near_e), (odd, near_o))):
                edge, face = edge_face(v, near)
                edges[h].append(edge)
                faces[h].append(face)
                centres[h].append(near)
        for x in range(PX):
            at = (y * PX + x) * 2
            for h in range(2):
                p = centres[h][x]
                q = faces[h][x]
                if 0 < x < PX - 1:
                    p = p + (faces[h][x - 1] + faces[h][x + 1])
                    q = q + (edges[h][x - 1] + edges[h][x + 1])
                else:
                    beside = x - 1 if x else x + 1
                    p = p + faces[h][beside]
                    q = q + edges[h][beside]
                self.pp[at + h] = p
                self.qq[at + h] = q

    def update(self, y, x, h):
        at = (y * PX + x) * 2 + h
        row = PX * 2
        ir, ii = ((self.ie_r, self.ie_i), (self.io_r, self.io_i))[h]
        n = self.pp[at] + (self.qq[at - row] + self.qq[at + row])
        return row_of(ir, y, x) * n + row_of(ii, y, x) * (self.sgn * turned(n))

    def second_stage(self, y):
        for x in range(1, 14):
            at = (y * PX + x) * 2
            we = self.it1[at] + self.update(y, x, 0)
            wo = self.it1[at + 1] + self.update(y, x, 1)
            p = we + down(we, self.last)
            half = p + wo
            after = jnp.where(self.last, -wo, pltpu.roll(wo, LANES - 1, 1))
            self.va[y * PX + x] = half + wo
            self.vb[y * PX + x] = (up(wo, self.first) + after) + 2.0 * half

    def third_stage(self, j, c1_out, ck_out):
        base = (2 + 2 * j) * PX
        gs, hs = {}, {}
        for x in range(1, 14):

            def combos(ref):
                vm, v0, v1, v2, v3 = (ref[base + (d - 1) * PX + x] for d in range(5))
                half = (v0 + v2) + v1
                return half + v1, (vm + v3) + 2.0 * half

            aa, ba = combos(self.va)
            ab, bb = combos(self.vb)
            u = ba + ab
            if 2 <= x <= 12:
                at = base + x
                gs[x] = (u + (3.0 / 14.0) * bb) + (
                    (self.sy[at] + self.sy[at + 2 * PX]) + 2.0 * self.sy[at + PX]
                )
            hs[x] = aa + ((3.0 / 14.0) * u + (1.0 / 14.0) * bb)
        for i in range(CX):
            b = 2 + 2 * i
            mx = jnp.where(self.x0 + b + 2 == self.nx, 1.0, 2.0).astype(F32)
            raw = (
                (gs[b] + gs[b + 2])
                + 2.0 * (gs[b + 1] + (hs[b] + hs[b + 2]))
                + (hs[b - 1] + hs[b + 3])
                + mx * hs[b + 1]
            ) * (14.0 / 1920.0)
            kr = row_of(self.kr, 3 + 2 * j, b + 1)
            ki = row_of(self.ki, 3 + 2 * j, b + 1)
            c1_out[i, j] = kr * raw + ki * (self.sgn * turned(raw))
            ck_out[0, i, pl.ds(j, 1), :] = self.kr[3 + 2 * j, b + 1 : b + 2, :]
            ck_out[1, i, pl.ds(j, 1), :] = self.ki[3 + 2 * j, b + 1 : b + 2, :]


def middle_kernel(sizes, labels, tab, wave, *refs):
    region = Region(sizes, tab, wave, refs[:12], refs[12:])
    region.tables(labels, LOW, 2 * OWN_Y, 8)
    row_loop(LOW, 2 * OWN_Y, 4, region.first_stage)
    row_loop(LOW + 1, 2 * OWN_Y - 2, 7, region.second_stage)


def low_kernel(sizes, labels, tab, wave, *refs):
    region = Region(sizes, tab, wave, refs[12:24], refs[26:])
    c1_out, ck_out = refs[24:26]
    region.tables(labels, 0, LOW, LOW)
    row_loop(0, LOW, 5, region.first_stage)
    row_loop(1, LOW, 5, region.second_stage)
    for k in range(2):
        for i in range(CX):
            ck_out[k, i, 8:16, :] = jnp.zeros((8, LANES), F32)
    row_loop(0, EARLY, 1, lambda j: region.third_stage(j, c1_out, ck_out))


def high_kernel(sizes, labels, tab, wave, *refs):
    region = Region(sizes, tab, wave, refs[14:26], refs[29:])
    c1_out, ck_out, send_out = refs[26:29]
    core, y0, ny = region.core, region.y0, region.ny
    it1 = region.it1
    top = LOW + 2 * OWN_Y
    region.tables(labels, top, PY - top, PY - top)
    row_loop(top, PY - top, 3, region.first_stage)
    row_loop(top - 1, PY - top, 3, region.second_stage)

    @pl.when(y0 + top == ny)
    def _():
        for x in range(1, 14):
            for ref in (region.va, region.vb):
                ref[(top + 1) * PX + x] = -ref[(top - 1) * PX + x]

    row_loop(EARLY, CY - EARLY, 1, lambda j: region.third_stage(j, c1_out, ck_out))

    j0 = 4 - 4 * core
    for i in range(CX):
        for j in range(NJ):
            send_out[i * NJ + j] = c1_out[i, j0 + j]
        for k in range(2):
            send_out[CX * NJ + (k * CX + i) * 2] = ck_out[k, i, 0:8, :]
            send_out[CX * NJ + (k * CX + i) * 2 + 1] = ck_out[k, i, 8:16, :]
    plane = 6 + 3 * core
    ys = LOW + OWN_Y - core * OWN_Y
    edges, faces = [], []
    for k in range(OWN_Y + 2):
        at = ((ys - 1 + k) * PX + plane) * 2
        even = it1[at]
        odd = it1[at + 1]
        ee, fe = edge_face(even, odd + up(odd, region.first))
        eo, fo = edge_face(odd, even + down(even, region.last))
        edges.append((ee, eo))
        faces.append((fe, fo))
    for k in range(OWN_Y):
        for h in range(2):
            send_out[CX * NJ + 4 * CX + 2 * k + h] = faces[k + 1][h] + (
                edges[k][h] + edges[k + 2][h]
            )


SEND = CX * NJ + 4 * CX + 2 * OWN_Y


class Own(Region):
    def __init__(self, refs):
        (self.ie_r, self.io_r, self.ie_i, self.io_i, self.it1, self.pp, self.qq) = refs
        self.sgn = sign_rows()


def coarse_sums(ref, pp, qq, i, sweep, first, last):
    edges, faces, centres = {}, {}, {}
    for j in range(sweep, NJ - sweep):
        v = ref[i * NJ + j]
        near = up(v, first) + down(v, last)
        edges[j], faces[j] = edge_face(v, near)
        centres[j] = near
    for j in range(sweep + 1, NJ - sweep - 1):
        pp[i * NJ + j] = centres[j] + (faces[j - 1] + faces[j + 1])
        qq[i * NJ + j] = faces[j] + (edges[j - 1] + edges[j + 1])


def own_kernel(*refs):
    own = Own(refs[:7])
    c1_own, ck_own, it2, inv, c1, ck, pp, qq = refs[7:]
    core = where_am_i()[0]
    lanes = lane_iota()
    first = lanes == 0
    last = lanes == LANES - 1

    xb = core * LOW
    yb = LOW + core * OWN_Y
    xe = core * (PX - 1)
    tables = (own.ie_r, own.io_r, own.ie_i, own.io_i)

    def own_stage(k):
        y = yb + k
        for xx in range(OWN_X):
            x = xb + xx
            at = (y * PX + x) * 2
            for h in range(2):
                it2[xx * OWN_Y + k, h] = 3.0 * own.it1[at + h] + own.update(y, x, h)
        for n, ref in enumerate(tables):
            inv[n, pl.ds(k, 1), :] = ref[y, pl.ds(xe, 1), :]

    own_i = CX - core * CX
    for i in range(CX):
        for j in range(NJ):
            c1[(own_i + i) * NJ + j] = c1_own[i, 4 * core + j]
        for k in range(2):
            ck[k, own_i + i] = ck_own[k, i]
    row_loop(
        own_i, CX, 5, lambda i: coarse_sums(c1, pp, qq, i, 0, first, last)
    )
    row_loop(0, OWN_Y, 2, own_stage)


def cycle_kernel(recv, it2, inv, *refs):
    c1, ck, pp, qq, out, cc, parts, o0, o1, stage, sems = refs[4:]
    core = where_am_i()[0]
    lanes = lane_iota()
    first = lanes == 0
    last = lanes == LANES - 1
    sgn = sign_rows()
    j0 = 4 * core
    other_i = core * CX

    def spread(row):
        return jnp.broadcast_to(row, (8, LANES))

    for i in range(CX):
        for j in range(NJ):
            c1[(other_i + i) * NJ + j] = recv[i * NJ + j]
        for k in range(2):
            for h in range(2):
                tile = slice(8 * h, 8 * h + 8)
                ck[k, other_i + i, tile, :] = recv[CX * NJ + (k * CX + i) * 2 + h]

    for sweep, (sum_step, relax_step) in enumerate(((5, 4), (4, 3), (3, 4))):
        ref = c1 if sweep == 0 else cc

        def sums(i, ref=ref, sweep=sweep):
            coarse_sums(ref, pp, qq, i, sweep, first, last)

        if sweep:
            row_loop(sweep, NI - 2 * sweep, sum_step, sums)
        else:
            row_loop(other_i, CX, sum_step, sums)

        def relax(i, ref=ref, sweep=sweep):
            for j in range(sweep + 1, NJ - sweep - 1):
                at = i * NJ + j
                n = (pp[at] + (qq[at - NJ] + qq[at + NJ])) * (14.0 / 120.0)
                kr = spread(ck[0, i, pl.ds(j0 + j, 1), :])
                ki = spread(ck[1, i, pl.ds(j0 + j, 1), :])
                cc[at] = (0.2 * ref[at] + c1[at]) + (kr * n + ki * (sgn * turned(n)))

        row_loop(sweep + 1, NI - 2 * sweep - 2, relax_step, relax)

    flags = {0: jnp.where(core == 0, 1.0, 0.0), OWN_X - 1: jnp.where(core == 1, 1.0, 0.0)}
    added = []
    for k in range(OWN_Y):
        pair = []
        for h in range(2):
            n = recv[CX * NJ + 4 * CX + 2 * k + h]
            ir = spread(inv[h, k : k + 1, :])
            ii = spread(inv[2 + h, k : k + 1, :])
            pair.append(ir * n + ii * (sgn * turned(n)))
        added.append(pair)

    rows = lax.broadcasted_iota(jnp.int32, (2 * LANES, 2 * LANES), 0)
    cols = lax.broadcasted_iota(jnp.int32, (2 * LANES, 2 * LANES), 1)
    target = jnp.where(rows < LANES, 2 * rows, 2 * (rows - LANES) + 1)
    perm = jnp.where(cols == target, 1.0, 0.0).astype(jnp.bfloat16)

    def fine(x, y, value):
        col = x * OWN_Y + y
        even = it2[col, 0] + 0.5 * (value + up(value, first))
        odd = it2[col, 1] + value
        if x in flags:
            even = even + flags[x] * added[y][0]
            odd = odd + flags[x] * added[y][1]
        return even, odd

    size = 2 * OWN_Y * 8
    copies = []
    for i in range(OWN_X // 2):
        for j in range(OWN_Y // 2):
            at = (i + 4) * NJ + j + 4
            here = cc[at]
            left = cc[at - NJ]
            mix = 0.5 * (left + here)
            below = cc[at - 1]
            mix_below = 0.5 * (cc[at - NJ - 1] + below)
            for x in range(2):
                lower, upper = (
                    (0.5 * (mix_below + mix), mix),
                    (0.5 * (below + here), here),
                )[x]
                a = fine(2 * i + x, 2 * j, lower)
                b = fine(2 * i + x, 2 * j + 1, upper)
                for h in range(2):
                    value = jnp.concatenate([a[h], b[h]], axis=0)
                    top = value.astype(jnp.bfloat16)
                    rest = (value - top.astype(F32)).astype(jnp.bfloat16)
                    start = i * 2 * size + (x * OWN_Y + 2 * j) * 8
                    half = slice(h * LANES, h * LANES + LANES)
                    parts[start : start + 16, half] = top
                    parts[start + size : start + size + 16, half] = rest
        mixed = jnp.dot(
            parts[i * 2 * size : (i + 1) * 2 * size, :], perm, preferred_element_type=F32
        )
        rows_in = 2 * OWN_Y
        for n in range(rows_in):
            block = mixed[n * 8 : n * 8 + 8] + mixed[size + n * 8 : size + n * 8 + 8]
            o0[pl.ds(i * size + n, 8, stride=rows_in), :] = block[:, :LANES]
            o1[pl.ds(i * size + n, 8, stride=rows_in), :] = block[:, LANES:]
        for f in range(8):
            take = slice(i * size + f * rows_in, i * size + (f + 1) * rows_in)
            stage[i, f, :, :LANES] = o0[take]
            stage[i, f, :, LANES:] = o1[take]
        copies.append(
            pltpu.make_async_copy(
                stage.at[i], out.at[:, pl.ds(i * rows_in, rows_in), :], sems.at[i]
            )
        )
        copies[-1].start()
    for copy in copies:
        copy.wait()


def vmem(*shape):
    return pltpu.VMEM(shape, F32)


SPEC = pl.BlockSpec(memory_space=pltpu.VMEM)
CELLS = PY * PX
SHARED = (vmem(PY, PX, LANES),) * 6 + (vmem(CELLS * 2, 8, LANES),) * 3 + (
    vmem(CELLS, 8, LANES),
) * 3
COARSE = (vmem(CX, CY, 8, LANES), vmem(2, CX, 16, LANES))
TABLES = [vmem(PY, PX, LANES)] * 6


def limit(mib):
    return pltpu.CompilerParams(vmem_limit_bytes=mib << 20)


def near_core(*arrays):
    return [pltpu.with_memory_space_constraint(a, pltpu.VMEM) for a in arrays]


def stay_call(labels):
    return pl.pallas_call(
        stay_kernel,
        out_shape=pltpu.VMEM(labels.shape, labels.dtype),
        in_specs=[pl.BlockSpec(memory_space=pltpu.HBM)],
        out_specs=SPEC,
        scratch_shapes=[pltpu.SemaphoreType.DMA(())],
        compiler_params=limit(1),
    )(pltpu.with_memory_space_constraint(labels, pltpu.HBM))


def wave_call(real, imag, angles, picks, after):
    small = pl.BlockSpec(memory_space=pltpu.HBM)
    return pl.pallas_call(
        wave_kernel,
        out_shape=(vmem(CELLS * 2, 8, LANES), vmem(8, LANES)),
        in_specs=[small] * 4 + [SPEC],
        out_specs=(SPEC,) * 2,
        scratch_shapes=[
            pltpu.SMEM(a.shape, a.dtype) for a in (real, imag, angles, picks)
        ]
        + [pltpu.SemaphoreType.DMA((4,))],
        compiler_params=limit(6),
    )(
        *(pltpu.with_memory_space_constraint(a, pltpu.HBM) for a in (real, imag, angles, picks)),
        *near_core(after),
    )


def middle_call(sizes, labels, tab, wave):
    def kernel(*refs):
        middle_kernel(sizes, *refs)

    return pl.pallas_call(
        kernel,
        out_shape=SHARED,
        in_specs=[SPEC] * 3,
        out_specs=(SPEC,) * 12,
        scratch_shapes=TABLES + [vmem(2 * OWN_Y * PX, 2 * LANES)],
        compiler_params=limit(6),
    )(*near_core(labels, tab, wave))


def low_call(sizes, labels, tab, wave, shared):
    def kernel(*refs):
        low_kernel(sizes, *refs)

    return pl.pallas_call(
        kernel,
        out_shape=SHARED + COARSE,
        in_specs=[SPEC] * 15,
        out_specs=(SPEC,) * 14,
        input_output_aliases={3 + n: n for n in range(12)},
        scratch_shapes=TABLES + [vmem(LOW * PX, 2 * LANES)],
        compiler_params=limit(6),
    )(*near_core(labels, tab, wave), *shared)


def high_call(sizes, labels, tab, wave, shared):
    def kernel(*refs):
        high_kernel(sizes, *refs)

    results = pl.pallas_call(
        kernel,
        out_shape=SHARED + COARSE + (vmem(SEND, 8, LANES),),
        in_specs=[SPEC] * 17,
        out_specs=(SPEC,) * 15,
        input_output_aliases={3 + n: n for n in range(14)},
        scratch_shapes=TABLES + [vmem(LOW * PX, 2 * LANES)],
        compiler_params=limit(6),
    )(*near_core(labels, tab, wave), *shared)
    return results[:12], results[12:]


POINTS = NI * NJ
HALF = (vmem(POINTS, 8, LANES), vmem(2, NI, 16, LANES)) + (vmem(POINTS, 8, LANES),) * 2


def own_call(shared, c1, ck):
    used = shared[:4] + shared[6:9]
    results = pl.pallas_call(
        own_kernel,
        out_shape=(vmem(OWN_X * OWN_Y, 2, 8, LANES), vmem(4, 8, LANES)) + HALF,
        in_specs=[SPEC] * 9,
        out_specs=(SPEC,) * 6,
        compiler_params=limit(6),
    )(*used, c1, ck)
    return results[:2], results[2:]


def cycle_call(recv, block, half):
    rows = OWN_X * OWN_Y * 8
    results = pl.pallas_call(
        cycle_kernel,
        out_shape=HALF
        + (jax.ShapeDtypeStruct((8, OWN_X * OWN_Y, 2 * LANES), F32),),
        in_specs=[SPEC] * 7,
        out_specs=(SPEC,) * 4 + (pl.BlockSpec(memory_space=pltpu.HBM),),
        input_output_aliases={3 + n: n for n in range(4)},
        scratch_shapes=[vmem(POINTS, 8, LANES)]
        + [pltpu.VMEM((2 * rows, 2 * LANES), jnp.bfloat16)]
        + [vmem(rows, LANES)] * 2
        + [vmem(OWN_X // 2, 8, 2 * OWN_Y, 2 * LANES), pltpu.SemaphoreType.DMA((3,))],
        compiler_params=limit(8),
    )(*near_core(recv), *block, *half)
    return results[4]


def body(labels, permittivity_real, permittivity_imag, angles, angle_pick):
    gx_n = lax.axis_size("gx")
    gy_n = lax.axis_size("gy")
    core = lax.axis_index("gy") % 2
    is_low = core == 0

    def along_x(values, by):
        pairs = []
        for j in range(0, gy_n, 2):
            for i in range(gx_n - by):
                here, there = i * gy_n + j, (i + by) * gy_n + j + 1
                pairs += [(here, there), (there, here)]
        return lax.ppermute(values, ("gx", "gy"), pairs)

    def along_y(values, by):
        pairs = [(j, j + by) for j in range(gy_n) if 0 <= j + by < gy_n]
        return lax.ppermute(values, "gy", pairs)

    def core_swap(values):
        return lax.ppermute(values, "gy", [(j, j ^ 1) for j in range(gy_n)])

    other = core_swap(labels)
    labels = stay_call(labels)
    both = jnp.where(
        is_low,
        jnp.concatenate([labels, other], axis=1),
        jnp.concatenate([other, labels], axis=1),
    )
    both = with_layout_constraint(both, Layout((0, 1, 2)))
    far = along_x(jnp.where(is_low, both[2:], both[:4]), 2)
    near = along_x(both, 1)
    near = with_layout_constraint(near, Layout((0, 1, 2)))
    far = with_layout_constraint(far, Layout((0, 1, 2)))
    region = jnp.where(
        is_low,
        jnp.concatenate([both, near, far], axis=0),
        jnp.concatenate([far, near, both], axis=0),
    )
    region = jnp.transpose(region, (1, 0, 2))
    low = along_y(region[2 * OWN_Y - LOW :], 2)
    high = along_y(region[: PY - LOW - 2 * OWN_Y], -2)

    wave, table = wave_call(
        permittivity_real, permittivity_imag, angles, angle_pick, both
    )
    sizes = (OWN_X * gx_n, OWN_Y * gy_n)
    shared = middle_call(sizes, region, table, wave)
    shared = low_call(sizes, low, table, wave, shared)
    shared, (c1, ck, send) = high_call(sizes, high, table, wave, shared)
    recv = core_swap(send)
    block, half = own_call(shared, c1, ck)
    out = cycle_call(recv, block, half)
    return out.reshape(2, 4, OWN_X, OWN_Y, 2 * LANES)


def solution(mesh):
    return jax.shard_map(
        body,
        mesh=mesh,
        in_specs=(P("gx", "gy", None), P(), P(), P(), P()),
        out_specs=P(None, None, "gx", "gy", None),
        check_vma=False,
    )
```

```python
import jax
import jax.numpy as jnp
import numpy as np
from jax import lax
from jax.experimental import pallas as pl
from jax.experimental.pallas import tpu as pltpu
from jax.experimental.layout import Layout, with_layout_constraint
from jax.sharding import PartitionSpec as P

MAT = 8
DAMPING = 0.8
WAVE_SQUARED = 0.1
SHIFT_IMAG = 0.5
SOURCE_GAIN = 4.0

OWN_X = 6
OWN_Y = 8
PX = 16
PY = 35
LOW = 10
CX, CY = 5, 15
EARLY = 10
NI, NJ = 10, 11
LANES = 128
F32 = jnp.float32
OUTSIDE = 8
WAVENUMBER = float(np.sqrt(np.float32(WAVE_SQUARED)))


def lane_iota():
    return lax.broadcasted_iota(jnp.int32, (8, LANES), 1)


def sign_rows():
    rows = lax.broadcasted_iota(jnp.int32, (8, LANES), 0)
    return jnp.where(rows < 4, -1.0, 1.0).astype(F32)


def up(values, first):
    return jnp.where(first, 0.0, pltpu.roll(values, 1, 1))


def down(values, last):
    return jnp.where(last, 0.0, pltpu.roll(values, LANES - 1, 1))


def turned(values):
    return pltpu.roll(values, 4, 0)


def row_of(ref, y, x):
    return jnp.broadcast_to(ref[y, pl.ds(x, 1), :], (8, LANES))


def edge_face(values, near):
    edge = (3.0 / 14.0) * (values + (1.0 / 3.0) * near)
    face = values + (3.0 / 14.0) * near
    return edge, face


UPDATE_SCALE = 2.5 * 14.0 * DAMPING / 30.0


def fine_diagonal(er, ei):
    real = 128.0 / 30.0 - WAVE_SQUARED * (er + SHIFT_IMAG * ei)
    imag = WAVE_SQUARED * (SHIFT_IMAG * er - ei)
    return real, imag


def scaled_inverse(real, imag, scale, keep):
    ratio = jnp.where(keep, scale / (real * real + imag * imag), 0.0)
    return real * ratio, -imag * ratio


def side_of(core):
    return 1 - core


def where_am_i():
    gx = lax.axis_index("gx")
    gy = lax.axis_index("gy")
    core = lax.rem(gy, 2)
    x0 = OWN_X * gx - LOW * side_of(core)
    y0 = OWN_Y * (gy - core) - LOW
    return core, x0, y0


def stay_kernel(labels, held, sem):
    copy = pltpu.make_async_copy(labels, held, sem)
    copy.start()
    copy.wait()


def splat(value):
    return jnp.full((8, LANES), value, F32)


def wave_kernel(
    real_in, imag_in, angles_in, picks_in, after, wave, tab, real, imag, angles, picks, sems
):
    del after
    copies = [
        pltpu.make_async_copy(src, dst, sems.at[n])
        for n, (src, dst) in enumerate(
            (
                (real_in, real),
                (imag_in, imag),
                (angles_in, angles),
                (picks_in, picks),
            )
        )
    ]
    for copy in copies:
        copy.start()
    for copy in copies:
        copy.wait()
    _, x0, y0 = where_am_i()
    lanes = lane_iota()
    rows = lax.broadcasted_iota(jnp.int32, (8, LANES), 0)

    er = jnp.ones((8, LANES), F32)
    ei = jnp.zeros((8, LANES), F32)
    for m in range(MAT):
        er = jnp.where(lanes == m, splat(real[m]), er)
        ei = jnp.where(lanes == m, splat(imag[m]), ei)
    tab[0:1, :] = er[0:1]
    tab[1:2, :] = ei[0:1]

    incidence = jnp.zeros((8, LANES), F32)
    for c in range(4):
        mine = jnp.bitwise_and(rows, 3) == c
        incidence = jnp.where(mine, splat(angles[picks[c]]), incidence)
    in_x = lanes < PX
    place = jnp.where(in_x, x0 + lanes, y0 + (lanes - PX)).astype(F32)
    slope = jnp.where(in_x, jnp.cos(incidence), jnp.sin(incidence))
    phases = WAVENUMBER * (slope * place)
    cosine = jnp.cos(phases)
    sine = jnp.sin(phases)
    upper = rows < 4
    front = jnp.where(upper, cosine, sine)
    turn = jnp.where(upper, -sine, cosine)

    def along(values, n):
        return jnp.broadcast_to(values[:, n : n + 1], (8, LANES))

    for x in range(PX):
        wave[x * 2] = along(cosine, x)
        wave[x * 2 + 1] = along(sine, x)
    for y in reversed(range(PY)):
        w = along(front, PX + y)
        w_t = along(turn, PX + y)
        for x in range(PX):
            c = wave[x * 2]
            s = wave[x * 2 + 1]
            wave[(y * PX + x) * 2] = c * w + s * w_t
            wave[(y * PX + x) * 2 + 1] = c * w_t - s * w


def row_loop(first, count, step, body):
    def some(n, carry):
        for k in range(step):
            body(first + n * step + k)
        return carry

    lax.fori_loop(0, count // step, some, 0)


class Region:
    def __init__(self, sizes, tab, wave, shared, scratch):
        self.nx, self.ny = sizes
        self.core, self.x0, self.y0 = where_am_i()
        self.tab = tab
        self.wave = wave
        (self.ie_r, self.io_r, self.ie_i, self.io_i, self.kr, self.ki,
         self.it1, self.pp, self.qq, self.va, self.vb, self.sy) = shared
        (self.ge_r, self.go_r, self.ge_i, self.go_i, self.sa_r, self.sa_i,
         self.apart) = scratch
        lanes = lane_iota()
        self.first = lanes == 0
        self.last = lanes == LANES - 1
        self.sgn = sign_rows()
        rows = lax.broadcasted_iota(jnp.int32, (2 * LANES, 2 * LANES), 0)
        cols = lax.broadcasted_iota(jnp.int32, (2 * LANES, 2 * LANES), 1)
        source = jnp.where(cols < LANES, 2 * cols, 2 * (cols - LANES) + 1)
        self.perm = jnp.where(rows == source, 1.0, 0.0).astype(jnp.bfloat16)

    def pick(self, row, index):
        table = jnp.broadcast_to(self.tab[row : row + 1, :], (8, LANES))
        return jnp.take_along_axis(table, index, axis=1, mode="promise_in_bounds")

    def tables(self, labels, first_row, count, step):
        flat = labels[...].reshape(count * PX, 2 * LANES).astype(F32).astype(jnp.bfloat16)
        self.apart[0 : count * PX, :] = jnp.dot(
            flat, self.perm, preferred_element_type=F32
        )
        rows = lax.broadcasted_iota(jnp.int32, (8, LANES), 0)
        inside = []
        for h in range(2):
            xs = self.x0 + 8 * h + rows
            inside.append(jnp.logical_and(xs >= 0, xs < self.nx))

        def some(n, carry):
            for k in range(step):
                y = first_row + n * step + k
                y_in = jnp.logical_and(self.y0 + y >= 0, self.y0 + y < self.ny)
                for h in range(2):
                    start = pl.multiple_of((n * step + k) * PX + 8 * h, 8)
                    part = self.apart[pl.ds(start, 8), :]
                    at = (y, pl.ds(8 * h, 8), slice(None))
                    keep = jnp.logical_and(inside[h], y_in)
                    sources = []
                    for odd, (inv_r, inv_i, g_r, g_i) in enumerate(
                        (
                            (self.ie_r, self.ie_i, self.ge_r, self.ge_i),
                            (self.io_r, self.io_i, self.go_r, self.go_i),
                        )
                    ):
                        label = part[:, odd * LANES : (odd + 1) * LANES].astype(jnp.int32)
                        index = jnp.where(keep, label, OUTSIDE)
                        er = self.pick(0, index)
                        ei = self.pick(1, index)
                        real, imag = fine_diagonal(er, ei)
                        ir, ii = scaled_inverse(real, imag, UPDATE_SCALE, keep)
                        sr, si = 1.2 * SOURCE_GAIN * (er - 1.0), 1.2 * SOURCE_GAIN * ei
                        inv_r[at] = ir
                        inv_i[at] = ii
                        g_r[at] = (4.0 / 14.0) * (ir * sr - ii * si)
                        g_i[at] = (4.0 / 14.0) * (ir * si + ii * sr)
                        sources.append((sr, si))
                        if odd and (first_row + k) % 2 == 1:
                            kr, ki = scaled_inverse(
                                real + (128.0 / 120.0 - 128.0 / 30.0), imag, DAMPING, keep
                            )
                            self.kr[at] = kr
                            self.ki[at] = ki
                    for c, out in ((0, self.sa_r), (1, self.sa_i)):
                        se = sources[0][c]
                        out[at] = (se + down(se, self.last) + 2.0 * sources[1][c]) * (1.0 / 14.0)
            return carry

        lax.fori_loop(0, count // step, some, 0)

    def first_stage(self, y, full=True):
        planes = PX if full else PX - 1
        edges, faces, centres = [[], []], [[], []], [[], []]
        for x in range(planes):
            at = (y * PX + x) * 2
            e = self.wave[at]
            e_t = self.wave[at + 1]
            even = row_of(self.ge_r, y, x) * e + row_of(self.ge_i, y, x) * e_t
            odd = row_of(self.go_r, y, x) * e + row_of(self.go_i, y, x) * e_t
            if 2 <= x <= 12:
                self.sy[y * PX + x] = (
                    row_of(self.sa_r, y, x) * e + row_of(self.sa_i, y, x) * e_t
                )
            self.it1[at] = even
            self.it1[at + 1] = odd
            near_e = odd + up(odd, self.first)
            near_o = even + down(even, self.last)
            for h, (v, near) in enumerate(((even, near_e), (odd, near_o))):
                edge, face = edge_face(v, near)
                edges[h].append(edge)
                faces[h].append(face)
                centres[h].append(near)
        for x in range(PX) if full else range(1, 14):
            at = (y * PX + x) * 2
            for h in range(2):
                p = centres[h][x]
                q = faces[h][x]
                if 0 < x < PX - 1:
                    p = p + (faces[h][x - 1] + faces[h][x + 1])
                    q = q + (edges[h][x - 1] + edges[h][x + 1])
                else:
                    beside = x - 1 if x else x + 1
                    p = p + faces[h][beside]
                    q = q + edges[h][beside]
                self.pp[at + h] = p
                self.qq[at + h] = q

    def update(self, y, x, h):
        at = (y * PX + x) * 2 + h
        row = PX * 2
        ir, ii = ((self.ie_r, self.ie_i), (self.io_r, self.io_i))[h]
        n = self.pp[at] + (self.qq[at - row] + self.qq[at + row])
        return row_of(ir, y, x) * n + row_of(ii, y, x) * (self.sgn * turned(n))

    def second_stage(self, y):
        for x in range(1, 14):
            at = (y * PX + x) * 2
            we = self.it1[at] + self.update(y, x, 0)
            wo = self.it1[at + 1] + self.update(y, x, 1)
            p = we + down(we, self.last)
            half = p + wo
            after = jnp.where(self.last, -wo, pltpu.roll(wo, LANES - 1, 1))
            self.va[y * PX + x] = half + wo
            self.vb[y * PX + x] = (up(wo, self.first) + after) + 2.0 * half

    def third_stage(self, j, c1_out, ck_out):
        base = (2 + 2 * j) * PX
        gs, hs = {}, {}
        for x in range(1, 14):

            def combos(ref):
                vm, v0, v1, v2, v3 = (ref[base + (d - 1) * PX + x] for d in range(5))
                half = (v0 + v2) + v1
                return half + v1, (vm + v3) + 2.0 * half

            aa, ba = combos(self.va)
            ab, bb = combos(self.vb)
            u = ba + ab
            if 2 <= x <= 12:
                at = base + x
                gs[x] = (u + (3.0 / 14.0) * bb) + (
                    (self.sy[at] + self.sy[at + 2 * PX]) + 2.0 * self.sy[at + PX]
                )
            hs[x] = aa + ((3.0 / 14.0) * u + (1.0 / 14.0) * bb)
        for i in range(CX):
            b = 2 + 2 * i
            mx = jnp.where(self.x0 + b + 2 == self.nx, 1.0, 2.0).astype(F32)
            raw = (
                (gs[b] + gs[b + 2])
                + 2.0 * (gs[b + 1] + (hs[b] + hs[b + 2]))
                + (hs[b - 1] + hs[b + 3])
                + mx * hs[b + 1]
            ) * (14.0 / 1920.0)
            kr = row_of(self.kr, 3 + 2 * j, b + 1)
            ki = row_of(self.ki, 3 + 2 * j, b + 1)
            c1_out[i, j] = kr * raw + ki * (self.sgn * turned(raw))
            ck_out[0, i, pl.ds(j, 1), :] = self.kr[3 + 2 * j, b + 1 : b + 2, :]
            ck_out[1, i, pl.ds(j, 1), :] = self.ki[3 + 2 * j, b + 1 : b + 2, :]


def middle_kernel(sizes, labels, tab, wave, *refs):
    region = Region(sizes, tab, wave, refs[:12], refs[12:])
    region.tables(labels, LOW, 2 * OWN_Y, 8)
    row_loop(LOW, 2 * OWN_Y, 4, region.first_stage)
    row_loop(LOW + 1, 2 * OWN_Y - 2, 7, region.second_stage)


def low_kernel(sizes, labels, tab, wave, *refs):
    region = Region(sizes, tab, wave, refs[12:24], refs[26:])
    c1_out, ck_out = refs[24:26]
    region.tables(labels, 0, LOW, LOW)
    row_loop(0, LOW - 1, 3, lambda y: region.first_stage(y, False))
    region.first_stage(LOW - 1)
    row_loop(1, LOW, 5, region.second_stage)
    for k in range(2):
        for i in range(CX):
            ck_out[k, i, 8:16, :] = jnp.zeros((8, LANES), F32)
    row_loop(0, EARLY, 1, lambda j: region.third_stage(j, c1_out, ck_out))


def high_kernel(sizes, labels, tab, wave, *refs):
    region = Region(sizes, tab, wave, refs[14:26], refs[29:])
    c1_out, ck_out, send_out = refs[26:29]
    core, y0, ny = region.core, region.y0, region.ny
    it1 = region.it1
    top = LOW + 2 * OWN_Y
    region.tables(labels, top, PY - top, PY - top)
    region.first_stage(top)
    row_loop(top + 1, PY - top - 1, 4, lambda y: region.first_stage(y, False))
    row_loop(top - 1, PY - top, 3, region.second_stage)

    @pl.when(y0 + top == ny)
    def _():
        for x in range(1, 14):
            for ref in (region.va, region.vb):
                ref[(top + 1) * PX + x] = -ref[(top - 1) * PX + x]

    row_loop(EARLY, CY - EARLY, 1, lambda j: region.third_stage(j, c1_out, ck_out))

    j0 = 4 - 4 * core
    for i in range(CX):
        for j in range(NJ):
            send_out[i * NJ + j] = c1_out[i, j0 + j]
        for k in range(2):
            send_out[CX * NJ + (k * CX + i) * 2] = ck_out[k, i, 0:8, :]
            send_out[CX * NJ + (k * CX + i) * 2 + 1] = ck_out[k, i, 8:16, :]
    plane = 6 + 3 * side_of(core)
    ys = LOW + OWN_Y - core * OWN_Y
    edges, faces = [], []
    for k in range(OWN_Y + 2):
        at = ((ys - 1 + k) * PX + plane) * 2
        even = it1[at]
        odd = it1[at + 1]
        ee, fe = edge_face(even, odd + up(odd, region.first))
        eo, fo = edge_face(odd, even + down(even, region.last))
        edges.append((ee, eo))
        faces.append((fe, fo))
    for k in range(OWN_Y):
        for h in range(2):
            send_out[CX * NJ + 4 * CX + 2 * k + h] = faces[k + 1][h] + (
                edges[k][h] + edges[k + 2][h]
            )


SEND = CX * NJ + 4 * CX + 2 * OWN_Y


class Own(Region):
    def __init__(self, refs):
        (self.ie_r, self.io_r, self.ie_i, self.io_i, self.it1, self.pp, self.qq) = refs
        self.sgn = sign_rows()


def coarse_sums(ref, pp, qq, i, sweep, first, last):
    edges, faces, centres = {}, {}, {}
    for j in range(sweep, NJ - sweep):
        v = ref[i * NJ + j]
        near = up(v, first) + down(v, last)
        edges[j], faces[j] = edge_face(v, near)
        centres[j] = near
    for j in range(sweep + 1, NJ - sweep - 1):
        pp[i * NJ + j] = centres[j] + (faces[j - 1] + faces[j + 1])
        qq[i * NJ + j] = faces[j] + (edges[j - 1] + edges[j + 1])


def own_kernel(*refs):
    own = Own(refs[:7])
    c1_own, ck_own, it2, inv, c1, ck, pp, qq = refs[7:]
    core = where_am_i()[0]
    lanes = lane_iota()
    first = lanes == 0
    last = lanes == LANES - 1

    xb = side_of(core) * LOW
    yb = LOW + core * OWN_Y
    xe = side_of(core) * (PX - 1)
    tables = (own.ie_r, own.io_r, own.ie_i, own.io_i)

    def own_stage(k):
        y = yb + k
        for xx in range(OWN_X):
            x = xb + xx
            at = (y * PX + x) * 2
            for h in range(2):
                it2[xx * OWN_Y + k, h] = 3.0 * own.it1[at + h] + own.update(y, x, h)
        for n, ref in enumerate(tables):
            inv[n, pl.ds(k, 1), :] = ref[y, pl.ds(xe, 1), :]

    own_i = CX - side_of(core) * CX
    for i in range(CX):
        for j in range(NJ):
            c1[(own_i + i) * NJ + j] = c1_own[i, 4 * core + j]
        for k in range(2):
            ck[k, own_i + i] = ck_own[k, i]
    row_loop(
        own_i, CX, 5, lambda i: coarse_sums(c1, pp, qq, i, 0, first, last)
    )
    row_loop(0, OWN_Y, 2, own_stage)


def cycle_kernel(recv, it2, inv, *refs):
    c1, ck, pp, qq, out, cc, parts, o0, o1, stage, sems = refs[4:]
    core = where_am_i()[0]
    lanes = lane_iota()
    first = lanes == 0
    last = lanes == LANES - 1
    sgn = sign_rows()
    j0 = 4 * core
    other_i = side_of(core) * CX

    def spread(row):
        return jnp.broadcast_to(row, (8, LANES))

    for i in range(CX):
        for j in range(NJ):
            c1[(other_i + i) * NJ + j] = recv[i * NJ + j]
        for k in range(2):
            for h in range(2):
                tile = slice(8 * h, 8 * h + 8)
                ck[k, other_i + i, tile, :] = recv[CX * NJ + (k * CX + i) * 2 + h]

    for sweep, (sum_step, relax_step) in enumerate(((5, 4), (4, 3), (3, 4))):
        ref = c1 if sweep == 0 else cc

        def sums(i, ref=ref, sweep=sweep):
            coarse_sums(ref, pp, qq, i, sweep, first, last)

        if sweep:
            row_loop(sweep, NI - 2 * sweep, sum_step, sums)
        else:
            row_loop(other_i, CX, sum_step, sums)

        def relax(i, ref=ref, sweep=sweep):
            for j in range(sweep + 1, NJ - sweep - 1):
                at = i * NJ + j
                n = (pp[at] + (qq[at - NJ] + qq[at + NJ])) * (14.0 / 120.0)
                kr = spread(ck[0, i, pl.ds(j0 + j, 1), :])
                ki = spread(ck[1, i, pl.ds(j0 + j, 1), :])
                cc[at] = (0.2 * ref[at] + c1[at]) + (kr * n + ki * (sgn * turned(n)))

        row_loop(sweep + 1, NI - 2 * sweep - 2, relax_step, relax)

    flags = {0: jnp.where(core == 1, 1.0, 0.0), OWN_X - 1: jnp.where(core == 0, 1.0, 0.0)}
    added = []
    for k in range(OWN_Y):
        pair = []
        for h in range(2):
            n = recv[CX * NJ + 4 * CX + 2 * k + h]
            ir = spread(inv[h, k : k + 1, :])
            ii = spread(inv[2 + h, k : k + 1, :])
            pair.append(ir * n + ii * (sgn * turned(n)))
        added.append(pair)

    rows = lax.broadcasted_iota(jnp.int32, (2 * LANES, 2 * LANES), 0)
    cols = lax.broadcasted_iota(jnp.int32, (2 * LANES, 2 * LANES), 1)
    target = jnp.where(rows < LANES, 2 * rows, 2 * (rows - LANES) + 1)
    perm = jnp.where(cols == target, 1.0, 0.0).astype(jnp.bfloat16)

    def fine(x, y, value):
        col = x * OWN_Y + y
        even = it2[col, 0] + 0.5 * (value + up(value, first))
        odd = it2[col, 1] + value
        if x in flags:
            even = even + flags[x] * added[y][0]
            odd = odd + flags[x] * added[y][1]
        return even, odd

    size = 2 * OWN_Y * 8
    copies = []
    for i in range(OWN_X // 2):
        for j in range(OWN_Y // 2):
            at = (i + 4) * NJ + j + 4
            here = cc[at]
            left = cc[at - NJ]
            mix = 0.5 * (left + here)
            below = cc[at - 1]
            mix_below = 0.5 * (cc[at - NJ - 1] + below)
            for x in range(2):
                lower, upper = (
                    (0.5 * (mix_below + mix), mix),
                    (0.5 * (below + here), here),
                )[x]
                a = fine(2 * i + x, 2 * j, lower)
                b = fine(2 * i + x, 2 * j + 1, upper)
                for h in range(2):
                    value = jnp.concatenate([a[h], b[h]], axis=0)
                    top = value.astype(jnp.bfloat16)
                    rest = (value - top.astype(F32)).astype(jnp.bfloat16)
                    start = i * 2 * size + (x * OWN_Y + 2 * j) * 8
                    half = slice(h * LANES, h * LANES + LANES)
                    parts[start : start + 16, half] = top
                    parts[start + size : start + size + 16, half] = rest
        mixed = jnp.dot(
            parts[i * 2 * size : (i + 1) * 2 * size, :], perm, preferred_element_type=F32
        )
        rows_in = 2 * OWN_Y
        for n in range(rows_in):
            block = mixed[n * 8 : n * 8 + 8] + mixed[size + n * 8 : size + n * 8 + 8]
            o0[pl.ds(i * size + n, 8, stride=rows_in), :] = block[:, :LANES]
            o1[pl.ds(i * size + n, 8, stride=rows_in), :] = block[:, LANES:]
        for f in range(8):
            take = slice(i * size + f * rows_in, i * size + (f + 1) * rows_in)
            stage[i, f, :, :LANES] = o0[take]
            stage[i, f, :, LANES:] = o1[take]
        copies.append(
            pltpu.make_async_copy(
                stage.at[i], out.at[:, pl.ds(i * rows_in, rows_in), :], sems.at[i]
            )
        )
        copies[-1].start()
    for copy in copies:
        copy.wait()


def vmem(*shape):
    return pltpu.VMEM(shape, F32)


SPEC = pl.BlockSpec(memory_space=pltpu.VMEM)
CELLS = PY * PX
SHARED = (vmem(PY, PX, LANES),) * 6 + (vmem(CELLS * 2, 8, LANES),) * 3 + (
    vmem(CELLS, 8, LANES),
) * 3
COARSE = (vmem(CX, CY, 8, LANES), vmem(2, CX, 16, LANES))
TABLES = [vmem(PY, PX, LANES)] * 6


def limit(mib):
    return pltpu.CompilerParams(vmem_limit_bytes=mib << 20)


def near_core(*arrays):
    return [pltpu.with_memory_space_constraint(a, pltpu.VMEM) for a in arrays]


def stay_call(labels):
    return pl.pallas_call(
        stay_kernel,
        out_shape=pltpu.VMEM(labels.shape, labels.dtype),
        in_specs=[pl.BlockSpec(memory_space=pltpu.HBM)],
        out_specs=SPEC,
        scratch_shapes=[pltpu.SemaphoreType.DMA(())],
        compiler_params=limit(1),
    )(pltpu.with_memory_space_constraint(labels, pltpu.HBM))


def wave_call(real, imag, angles, picks, after):
    small = pl.BlockSpec(memory_space=pltpu.HBM)
    return pl.pallas_call(
        wave_kernel,
        out_shape=(vmem(CELLS * 2, 8, LANES), vmem(8, LANES)),
        in_specs=[small] * 4 + [SPEC],
        out_specs=(SPEC,) * 2,
        scratch_shapes=[
            pltpu.SMEM(a.shape, a.dtype) for a in (real, imag, angles, picks)
        ]
        + [pltpu.SemaphoreType.DMA((4,))],
        compiler_params=limit(6),
    )(
        *(pltpu.with_memory_space_constraint(a, pltpu.HBM) for a in (real, imag, angles, picks)),
        *near_core(after),
    )


def middle_call(sizes, labels, tab, wave):
    def kernel(*refs):
        middle_kernel(sizes, *refs)

    return pl.pallas_call(
        kernel,
        out_shape=SHARED,
        in_specs=[SPEC] * 3,
        out_specs=(SPEC,) * 12,
        scratch_shapes=TABLES + [vmem(2 * OWN_Y * PX, 2 * LANES)],
        compiler_params=limit(6),
    )(*near_core(labels, tab, wave))


def low_call(sizes, labels, tab, wave, shared):
    def kernel(*refs):
        low_kernel(sizes, *refs)

    return pl.pallas_call(
        kernel,
        out_shape=SHARED + COARSE,
        in_specs=[SPEC] * 15,
        out_specs=(SPEC,) * 14,
        input_output_aliases={3 + n: n for n in range(12)},
        scratch_shapes=TABLES + [vmem(LOW * PX, 2 * LANES)],
        compiler_params=limit(6),
    )(*near_core(labels, tab, wave), *shared)


def high_call(sizes, labels, tab, wave, shared):
    def kernel(*refs):
        high_kernel(sizes, *refs)

    results = pl.pallas_call(
        kernel,
        out_shape=SHARED + COARSE + (vmem(SEND, 8, LANES),),
        in_specs=[SPEC] * 17,
        out_specs=(SPEC,) * 15,
        input_output_aliases={3 + n: n for n in range(14)},
        scratch_shapes=TABLES + [vmem(LOW * PX, 2 * LANES)],
        compiler_params=limit(6),
    )(*near_core(labels, tab, wave), *shared)
    return results[:12], results[12:]


POINTS = NI * NJ
HALF = (vmem(POINTS, 8, LANES), vmem(2, NI, 16, LANES)) + (vmem(POINTS, 8, LANES),) * 2


def own_call(shared, c1, ck):
    used = shared[:4] + shared[6:9]
    results = pl.pallas_call(
        own_kernel,
        out_shape=(vmem(OWN_X * OWN_Y, 2, 8, LANES), vmem(4, 8, LANES)) + HALF,
        in_specs=[SPEC] * 9,
        out_specs=(SPEC,) * 6,
        compiler_params=limit(6),
    )(*used, c1, ck)
    return results[:2], results[2:]


def cycle_call(recv, block, half):
    rows = OWN_X * OWN_Y * 8
    results = pl.pallas_call(
        cycle_kernel,
        out_shape=HALF
        + (jax.ShapeDtypeStruct((8, OWN_X * OWN_Y, 2 * LANES), F32),),
        in_specs=[SPEC] * 7,
        out_specs=(SPEC,) * 4 + (pl.BlockSpec(memory_space=pltpu.HBM),),
        input_output_aliases={3 + n: n for n in range(4)},
        scratch_shapes=[vmem(POINTS, 8, LANES)]
        + [pltpu.VMEM((2 * rows, 2 * LANES), jnp.bfloat16)]
        + [vmem(rows, LANES)] * 2
        + [vmem(OWN_X // 2, 8, 2 * OWN_Y, 2 * LANES), pltpu.SemaphoreType.DMA((3,))],
        compiler_params=limit(8),
    )(*near_core(recv), *block, *half)
    return results[4]


def body(labels, permittivity_real, permittivity_imag, angles, angle_pick):
    gx_n = lax.axis_size("gx")
    gy_n = lax.axis_size("gy")
    core = lax.axis_index("gy") % 2
    is_low = core == 0

    def along_x(values, by):
        pairs = []
        for j in range(gy_n):
            step = by if j % 2 == 1 else -by
            for i in range(gx_n):
                if 0 <= i + step < gx_n:
                    pairs.append(((i + step) * gy_n + j, i * gy_n + j))
        return lax.ppermute(values, ("gx", "gy"), pairs)

    def along_y(values, by):
        pairs = [(j, j + by) for j in range(gy_n) if 0 <= j + by < gy_n]
        return lax.ppermute(values, "gy", pairs)

    def core_swap(values):
        return lax.ppermute(values, "gy", [(j, j ^ 1) for j in range(gy_n)])

    other = core_swap(labels)
    labels = stay_call(labels)
    both = jnp.where(
        is_low,
        jnp.concatenate([labels, other], axis=1),
        jnp.concatenate([other, labels], axis=1),
    )
    both = with_layout_constraint(both, Layout((0, 1, 2)))
    far = along_x(jnp.where(is_low, both[2:], both[:4]), 2)
    near = along_x(both, 1)
    near = with_layout_constraint(near, Layout((0, 1, 2)))
    far = with_layout_constraint(far, Layout((0, 1, 2)))
    region = jnp.where(
        is_low,
        jnp.concatenate([far, near, both], axis=0),
        jnp.concatenate([both, near, far], axis=0),
    )
    region = jnp.transpose(region, (1, 0, 2))
    low = along_y(region[2 * OWN_Y - LOW :], 2)
    high = along_y(region[: PY - LOW - 2 * OWN_Y], -2)

    wave, table = wave_call(
        permittivity_real, permittivity_imag, angles, angle_pick, both
    )
    sizes = (OWN_X * gx_n, OWN_Y * gy_n)
    shared = middle_call(sizes, region, table, wave)
    shared = low_call(sizes, low, table, wave, shared)
    shared, (c1, ck, send) = high_call(sizes, high, table, wave, shared)
    recv = core_swap(send)
    block, half = own_call(shared, c1, ck)
    out = cycle_call(recv, block, half)
    return out.reshape(2, 4, OWN_X, OWN_Y, 2 * LANES)


def solution(mesh):
    return jax.shard_map(
        body,
        mesh=mesh,
        in_specs=(P("gx", "gy", None), P(), P(), P(), P()),
        out_specs=P(None, None, "gx", "gy", None),
        check_vma=False,
    )
```

```python
import jax
import jax.numpy as jnp
import numpy as np
from jax import lax
from jax.experimental import pallas as pl
from jax.experimental.pallas import tpu as pltpu
from jax.experimental.layout import Layout, with_layout_constraint
from jax.sharding import PartitionSpec as P

MAT = 8
DAMPING = 0.8
WAVE_SQUARED = 0.1
SHIFT_IMAG = 0.5
SOURCE_GAIN = 4.0

OWN_X = 6
OWN_Y = 8
PX = 16
PY = 35
LOW = 10
CX, CY = 5, 15
EARLY = 10
NI, NJ = 10, 11
LANES = 128
F32 = jnp.float32
OUTSIDE = 8
WAVENUMBER = float(np.sqrt(np.float32(WAVE_SQUARED)))


def lane_iota():
    return lax.broadcasted_iota(jnp.int32, (8, LANES), 1)


def sign_rows():
    rows = lax.broadcasted_iota(jnp.int32, (8, LANES), 0)
    return jnp.where(rows < 4, -1.0, 1.0).astype(F32)


def up(values, first):
    return jnp.where(first, 0.0, pltpu.roll(values, 1, 1))


def down(values, last):
    return jnp.where(last, 0.0, pltpu.roll(values, LANES - 1, 1))


def turned(values):
    return pltpu.roll(values, 4, 0)


def row_of(ref, y, x):
    return jnp.broadcast_to(ref[y, pl.ds(x, 1), :], (8, LANES))


def edge_face(values, near):
    edge = (3.0 / 14.0) * (values + (1.0 / 3.0) * near)
    face = values + (3.0 / 14.0) * near
    return edge, face


UPDATE_SCALE = 2.5 * 14.0 * DAMPING / 30.0


def fine_diagonal(er, ei):
    real = 128.0 / 30.0 - WAVE_SQUARED * (er + SHIFT_IMAG * ei)
    imag = WAVE_SQUARED * (SHIFT_IMAG * er - ei)
    return real, imag


def scaled_inverse(real, imag, scale, keep):
    ratio = jnp.where(keep, scale / (real * real + imag * imag), 0.0)
    return real * ratio, -imag * ratio


def side_of(core):
    return 1 - core


def where_am_i():
    gx = lax.axis_index("gx")
    gy = lax.axis_index("gy")
    core = lax.rem(gy, 2)
    x0 = OWN_X * gx - LOW * side_of(core)
    y0 = OWN_Y * (gy - core) - LOW
    return core, x0, y0


def stay_kernel(labels, held, sem):
    copy = pltpu.make_async_copy(labels, held, sem)
    copy.start()
    copy.wait()


def splat(value):
    return jnp.full((8, LANES), value, F32)


def wave_kernel(
    real_in, imag_in, angles_in, picks_in, after, wave, tab, real, imag, angles, picks, sems
):
    del after
    copies = [
        pltpu.make_async_copy(src, dst, sems.at[n])
        for n, (src, dst) in enumerate(
            (
                (real_in, real),
                (imag_in, imag),
                (angles_in, angles),
                (picks_in, picks),
            )
        )
    ]
    for copy in copies:
        copy.start()
    for copy in copies:
        copy.wait()
    _, x0, y0 = where_am_i()
    lanes = lane_iota()
    rows = lax.broadcasted_iota(jnp.int32, (8, LANES), 0)

    er = jnp.ones((8, LANES), F32)
    ei = jnp.zeros((8, LANES), F32)
    for m in range(MAT):
        er = jnp.where(lanes == m, splat(real[m]), er)
        ei = jnp.where(lanes == m, splat(imag[m]), ei)
    tab[0:1, :] = er[0:1]
    tab[1:2, :] = ei[0:1]

    incidence = jnp.zeros((8, LANES), F32)
    for c in range(4):
        mine = jnp.bitwise_and(rows, 3) == c
        incidence = jnp.where(mine, splat(angles[picks[c]]), incidence)
    in_x = lanes < PX
    place = jnp.where(in_x, x0 + lanes, y0 + (lanes - PX)).astype(F32)
    slope = jnp.where(in_x, jnp.cos(incidence), jnp.sin(incidence))
    phases = WAVENUMBER * (slope * place)
    cosine = jnp.cos(phases)
    sine = jnp.sin(phases)
    upper = rows < 4
    front = jnp.where(upper, cosine, sine)
    turn = jnp.where(upper, -sine, cosine)

    def along(values, n):
        return jnp.broadcast_to(values[:, n : n + 1], (8, LANES))

    for x in range(PX):
        wave[x * 2] = along(cosine, x)
        wave[x * 2 + 1] = along(sine, x)
    for y in reversed(range(PY)):
        w = along(front, PX + y)
        w_t = along(turn, PX + y)
        for x in range(PX):
            c = wave[x * 2]
            s = wave[x * 2 + 1]
            wave[(y * PX + x) * 2] = c * w + s * w_t
            wave[(y * PX + x) * 2 + 1] = c * w_t - s * w


def row_loop(first, count, step, body):
    def some(n, carry):
        for k in range(step):
            body(first + n * step + k)
        return carry

    lax.fori_loop(0, count // step, some, 0)


class Region:
    def __init__(self, sizes, tab, wave, shared, scratch):
        self.nx, self.ny = sizes
        self.core, self.x0, self.y0 = where_am_i()
        self.tab = tab
        self.wave = wave
        (self.ie_r, self.io_r, self.ie_i, self.io_i, self.kr, self.ki,
         self.it1, self.pp, self.qq, self.va, self.vb, self.sy) = shared
        (self.ge_r, self.go_r, self.ge_i, self.go_i, self.sa_r, self.sa_i,
         self.apart) = scratch
        lanes = lane_iota()
        self.first = lanes == 0
        self.last = lanes == LANES - 1
        self.sgn = sign_rows()
        rows = lax.broadcasted_iota(jnp.int32, (2 * LANES, 2 * LANES), 0)
        cols = lax.broadcasted_iota(jnp.int32, (2 * LANES, 2 * LANES), 1)
        source = jnp.where(cols < LANES, 2 * cols, 2 * (cols - LANES) + 1)
        self.perm = jnp.where(rows == source, 1.0, 0.0).astype(jnp.bfloat16)

    def pick(self, row, index):
        table = jnp.broadcast_to(self.tab[row : row + 1, :], (8, LANES))
        return jnp.take_along_axis(table, index, axis=1, mode="promise_in_bounds")

    def tables(self, labels, first_row, count, step):
        flat = labels[...].reshape(count * PX, 2 * LANES).astype(F32).astype(jnp.bfloat16)
        self.apart[0 : count * PX, :] = jnp.dot(
            flat, self.perm, preferred_element_type=F32
        )
        rows = lax.broadcasted_iota(jnp.int32, (8, LANES), 0)
        inside = []
        for h in range(2):
            xs = self.x0 + 8 * h + rows
            inside.append(jnp.logical_and(xs >= 0, xs < self.nx))

        def some(n, carry):
            for k in range(step):
                y = first_row + n * step + k
                y_in = jnp.logical_and(self.y0 + y >= 0, self.y0 + y < self.ny)
                for h in range(2):
                    start = pl.multiple_of((n * step + k) * PX + 8 * h, 8)
                    part = self.apart[pl.ds(start, 8), :]
                    at = (y, pl.ds(8 * h, 8), slice(None))
                    keep = jnp.logical_and(inside[h], y_in)
                    sources = []
                    for odd, (inv_r, inv_i, g_r, g_i) in enumerate(
                        (
                            (self.ie_r, self.ie_i, self.ge_r, self.ge_i),
                            (self.io_r, self.io_i, self.go_r, self.go_i),
                        )
                    ):
                        label = part[:, odd * LANES : (odd + 1) * LANES].astype(jnp.int32)
                        index = jnp.where(keep, label, OUTSIDE)
                        er = self.pick(0, index)
                        ei = self.pick(1, index)
                        real, imag = fine_diagonal(er, ei)
                        ir, ii = scaled_inverse(real, imag, UPDATE_SCALE, keep)
                        sr, si = 1.2 * SOURCE_GAIN * (er - 1.0), 1.2 * SOURCE_GAIN * ei
                        inv_r[at] = ir
                        inv_i[at] = ii
                        g_r[at] = (4.0 / 14.0) * (ir * sr - ii * si)
                        g_i[at] = (4.0 / 14.0) * (ir * si + ii * sr)
                        sources.append((sr, si))
                        if odd and (first_row + k) % 2 == 1:
                            kr, ki = scaled_inverse(
                                real + (128.0 / 120.0 - 128.0 / 30.0), imag, DAMPING, keep
                            )
                            self.kr[at] = kr
                            self.ki[at] = ki
                    for c, out in ((0, self.sa_r), (1, self.sa_i)):
                        se = sources[0][c]
                        out[at] = (se + down(se, self.last) + 2.0 * sources[1][c]) * (1.0 / 14.0)
            return carry

        lax.fori_loop(0, count // step, some, 0)

    def first_stage(self, y, full=True):
        planes = PX if full else PX - 1
        edges, faces, centres = [[], []], [[], []], [[], []]
        for x in range(planes):
            at = (y * PX + x) * 2
            e = self.wave[at]
            e_t = self.wave[at + 1]
            even = row_of(self.ge_r, y, x) * e + row_of(self.ge_i, y, x) * e_t
            odd = row_of(self.go_r, y, x) * e + row_of(self.go_i, y, x) * e_t
            if 2 <= x <= 12:
                self.sy[y * PX + x] = (
                    row_of(self.sa_r, y, x) * e + row_of(self.sa_i, y, x) * e_t
                )
            self.it1[at] = even
            self.it1[at + 1] = odd
            near_e = odd + up(odd, self.first)
            near_o = even + down(even, self.last)
            for h, (v, near) in enumerate(((even, near_e), (odd, near_o))):
                edge, face = edge_face(v, near)
                edges[h].append(edge)
                faces[h].append(face)
                centres[h].append(near)
        for x in range(PX) if full else range(1, 14):
            at = (y * PX + x) * 2
            for h in range(2):
                p = centres[h][x]
                q = faces[h][x]
                if 0 < x < PX - 1:
                    p = p + (faces[h][x - 1] + faces[h][x + 1])
                    q = q + (edges[h][x - 1] + edges[h][x + 1])
                else:
                    beside = x - 1 if x else x + 1
                    p = p + faces[h][beside]
                    q = q + edges[h][beside]
                self.pp[at + h] = p
                self.qq[at + h] = q

    def update(self, y, x, h):
        at = (y * PX + x) * 2 + h
        row = PX * 2
        ir, ii = ((self.ie_r, self.ie_i), (self.io_r, self.io_i))[h]
        n = self.pp[at] + (self.qq[at - row] + self.qq[at + row])
        return row_of(ir, y, x) * n + row_of(ii, y, x) * (self.sgn * turned(n))

    def second_stage(self, y):
        for x in range(1, 14):
            at = (y * PX + x) * 2
            we = self.it1[at] + self.update(y, x, 0)
            wo = self.it1[at + 1] + self.update(y, x, 1)
            p = we + down(we, self.last)
            half = p + wo
            after = jnp.where(self.last, -wo, pltpu.roll(wo, LANES - 1, 1))
            self.va[y * PX + x] = half + wo
            self.vb[y * PX + x] = (up(wo, self.first) + after) + 2.0 * half

    def third_stage(self, j, c1_out, ck_out):
        base = (2 + 2 * j) * PX
        gs, hs = {}, {}
        for x in range(1, 14):

            def combos(ref):
                vm, v0, v1, v2, v3 = (ref[base + (d - 1) * PX + x] for d in range(5))
                half = (v0 + v2) + v1
                return half + v1, (vm + v3) + 2.0 * half

            aa, ba = combos(self.va)
            ab, bb = combos(self.vb)
            u = ba + ab
            if 2 <= x <= 12:
                at = base + x
                gs[x] = (u + (3.0 / 14.0) * bb) + (
                    (self.sy[at] + self.sy[at + 2 * PX]) + 2.0 * self.sy[at + PX]
                )
            hs[x] = aa + ((3.0 / 14.0) * u + (1.0 / 14.0) * bb)
        for i in range(CX):
            b = 2 + 2 * i
            mx = jnp.where(self.x0 + b + 2 == self.nx, 1.0, 2.0).astype(F32)
            raw = (
                (gs[b] + gs[b + 2])
                + 2.0 * (gs[b + 1] + (hs[b] + hs[b + 2]))
                + (hs[b - 1] + hs[b + 3])
                + mx * hs[b + 1]
            ) * (14.0 / 1920.0)
            kr = row_of(self.kr, 3 + 2 * j, b + 1)
            ki = row_of(self.ki, 3 + 2 * j, b + 1)
            c1_out[i, j] = kr * raw + ki * (self.sgn * turned(raw))
            ck_out[0, i, pl.ds(j, 1), :] = self.kr[3 + 2 * j, b + 1 : b + 2, :]
            ck_out[1, i, pl.ds(j, 1), :] = self.ki[3 + 2 * j, b + 1 : b + 2, :]


def middle_kernel(sizes, labels, tab, wave, *refs):
    region = Region(sizes, tab, wave, refs[:12], refs[12:])
    region.tables(labels, LOW, 2 * OWN_Y, 8)
    row_loop(LOW, 2 * OWN_Y, 4, region.first_stage)
    row_loop(LOW + 1, 2 * OWN_Y - 2, 7, region.second_stage)


def low_kernel(sizes, labels, tab, wave, *refs):
    region = Region(sizes, tab, wave, refs[12:24], refs[27:])
    c1_out, ck_out, send_out = refs[24:27]
    region.tables(labels, 0, LOW, LOW)
    row_loop(0, LOW - 1, 3, lambda y: region.first_stage(y, False))
    region.first_stage(LOW - 1)
    row_loop(1, LOW, 5, region.second_stage)
    for k in range(2):
        for i in range(CX):
            ck_out[k, i, 8:16, :] = jnp.zeros((8, LANES), F32)
    row_loop(0, EARLY, 1, lambda j: region.third_stage(j, c1_out, ck_out))
    j0 = 4 - 4 * region.core
    for i in range(CX):
        for j in range(EARLY - 4):
            send_out[i * NJ + j] = c1_out[i, j0 + j]
        for k in range(2):
            send_out[CX * NJ + (k * CX + i) * 2] = ck_out[k, i, 0:8, :]


def high_kernel(sizes, labels, tab, wave, *refs):
    region = Region(sizes, tab, wave, refs[15:27], refs[30:])
    c1_out, ck_out, send_out = refs[27:30]
    core, y0, ny = region.core, region.y0, region.ny
    it1 = region.it1
    top = LOW + 2 * OWN_Y
    region.tables(labels, top, PY - top, PY - top)
    region.first_stage(top)
    row_loop(top + 1, PY - top - 1, 4, lambda y: region.first_stage(y, False))
    row_loop(top - 1, PY - top, 3, region.second_stage)

    @pl.when(y0 + top == ny)
    def _():
        for x in range(1, 14):
            for ref in (region.va, region.vb):
                ref[(top + 1) * PX + x] = -ref[(top - 1) * PX + x]

    row_loop(EARLY, CY - EARLY, 1, lambda j: region.third_stage(j, c1_out, ck_out))

    j0 = 4 - 4 * core
    for i in range(CX):
        for j in range(EARLY - 4, NJ):
            send_out[i * NJ + j] = c1_out[i, j0 + j]
        for k in range(2):
            send_out[CX * NJ + (k * CX + i) * 2 + 1] = ck_out[k, i, 8:16, :]
    plane = 6 + 3 * side_of(core)
    ys = LOW + OWN_Y - core * OWN_Y
    edges, faces = [], []
    for k in range(OWN_Y + 2):
        at = ((ys - 1 + k) * PX + plane) * 2
        even = it1[at]
        odd = it1[at + 1]
        ee, fe = edge_face(even, odd + up(odd, region.first))
        eo, fo = edge_face(odd, even + down(even, region.last))
        edges.append((ee, eo))
        faces.append((fe, fo))
    for k in range(OWN_Y):
        for h in range(2):
            send_out[CX * NJ + 4 * CX + 2 * k + h] = faces[k + 1][h] + (
                edges[k][h] + edges[k + 2][h]
            )


SEND = CX * NJ + 4 * CX + 2 * OWN_Y


class Own(Region):
    def __init__(self, refs):
        (self.ie_r, self.io_r, self.ie_i, self.io_i, self.it1, self.pp, self.qq) = refs
        self.sgn = sign_rows()


def coarse_sums(ref, pp, qq, i, sweep, first, last):
    edges, faces, centres = {}, {}, {}
    for j in range(sweep, NJ - sweep):
        v = ref[i * NJ + j]
        near = up(v, first) + down(v, last)
        edges[j], faces[j] = edge_face(v, near)
        centres[j] = near
    for j in range(sweep + 1, NJ - sweep - 1):
        pp[i * NJ + j] = centres[j] + (faces[j - 1] + faces[j + 1])
        qq[i * NJ + j] = faces[j] + (edges[j - 1] + edges[j + 1])


def own_kernel(*refs):
    own = Own(refs[:7])
    c1_own, ck_own, it2, inv, c1, ck, pp, qq = refs[7:]
    core = where_am_i()[0]
    lanes = lane_iota()
    first = lanes == 0
    last = lanes == LANES - 1

    xb = side_of(core) * LOW
    yb = LOW + core * OWN_Y
    xe = side_of(core) * (PX - 1)
    tables = (own.ie_r, own.io_r, own.ie_i, own.io_i)

    def own_stage(k):
        y = yb + k
        for xx in range(OWN_X):
            x = xb + xx
            at = (y * PX + x) * 2
            for h in range(2):
                it2[xx * OWN_Y + k, h] = 3.0 * own.it1[at + h] + own.update(y, x, h)
        for n, ref in enumerate(tables):
            inv[n, pl.ds(k, 1), :] = ref[y, pl.ds(xe, 1), :]

    own_i = CX - side_of(core) * CX
    for i in range(CX):
        for j in range(NJ):
            c1[(own_i + i) * NJ + j] = c1_own[i, 4 * core + j]
        for k in range(2):
            ck[k, own_i + i] = ck_own[k, i]
    row_loop(
        own_i, CX, 5, lambda i: coarse_sums(c1, pp, qq, i, 0, first, last)
    )
    row_loop(0, OWN_Y, 2, own_stage)


def cycle_kernel(recv, it2, inv, *refs):
    c1, ck, pp, qq, out, cc, parts, o0, o1, stage, sems = refs[4:]
    core = where_am_i()[0]
    lanes = lane_iota()
    first = lanes == 0
    last = lanes == LANES - 1
    sgn = sign_rows()
    j0 = 4 * core
    other_i = side_of(core) * CX

    def spread(row):
        return jnp.broadcast_to(row, (8, LANES))

    for i in range(CX):
        for j in range(NJ):
            c1[(other_i + i) * NJ + j] = recv[i * NJ + j]
        for k in range(2):
            for h in range(2):
                tile = slice(8 * h, 8 * h + 8)
                ck[k, other_i + i, tile, :] = recv[CX * NJ + (k * CX + i) * 2 + h]

    for sweep, (sum_step, relax_step) in enumerate(((5, 4), (4, 3), (3, 4))):
        ref = c1 if sweep == 0 else cc

        def sums(i, ref=ref, sweep=sweep):
            coarse_sums(ref, pp, qq, i, sweep, first, last)

        if sweep:
            row_loop(sweep, NI - 2 * sweep, sum_step, sums)
        else:
            row_loop(other_i, CX, sum_step, sums)

        def relax(i, ref=ref, sweep=sweep):
            for j in range(sweep + 1, NJ - sweep - 1):
                at = i * NJ + j
                n = (pp[at] + (qq[at - NJ] + qq[at + NJ])) * (14.0 / 120.0)
                kr = spread(ck[0, i, pl.ds(j0 + j, 1), :])
                ki = spread(ck[1, i, pl.ds(j0 + j, 1), :])
                cc[at] = (0.2 * ref[at] + c1[at]) + (kr * n + ki * (sgn * turned(n)))

        row_loop(sweep + 1, NI - 2 * sweep - 2, relax_step, relax)

    flags = {0: jnp.where(core == 1, 1.0, 0.0), OWN_X - 1: jnp.where(core == 0, 1.0, 0.0)}
    added = []
    for k in range(OWN_Y):
        pair = []
        for h in range(2):
            n = recv[CX * NJ + 4 * CX + 2 * k + h]
            ir = spread(inv[h, k : k + 1, :])
            ii = spread(inv[2 + h, k : k + 1, :])
            pair.append(ir * n + ii * (sgn * turned(n)))
        added.append(pair)

    rows = lax.broadcasted_iota(jnp.int32, (2 * LANES, 2 * LANES), 0)
    cols = lax.broadcasted_iota(jnp.int32, (2 * LANES, 2 * LANES), 1)
    target = jnp.where(rows < LANES, 2 * rows, 2 * (rows - LANES) + 1)
    perm = jnp.where(cols == target, 1.0, 0.0).astype(jnp.bfloat16)

    def fine(x, y, value):
        col = x * OWN_Y + y
        even = it2[col, 0] + 0.5 * (value + up(value, first))
        odd = it2[col, 1] + value
        if x in flags:
            even = even + flags[x] * added[y][0]
            odd = odd + flags[x] * added[y][1]
        return even, odd

    size = 2 * OWN_Y * 8
    copies = []
    for i in range(OWN_X // 2):
        for j in range(OWN_Y // 2):
            at = (i + 4) * NJ + j + 4
            here = cc[at]
            left = cc[at - NJ]
            mix = 0.5 * (left + here)
            below = cc[at - 1]
            mix_below = 0.5 * (cc[at - NJ - 1] + below)
            for x in range(2):
                lower, upper = (
                    (0.5 * (mix_below + mix), mix),
                    (0.5 * (below + here), here),
                )[x]
                a = fine(2 * i + x, 2 * j, lower)
                b = fine(2 * i + x, 2 * j + 1, upper)
                for h in range(2):
                    value = jnp.concatenate([a[h], b[h]], axis=0)
                    top = value.astype(jnp.bfloat16)
                    rest = (value - top.astype(F32)).astype(jnp.bfloat16)
                    start = i * 2 * size + (x * OWN_Y + 2 * j) * 8
                    half = slice(h * LANES, h * LANES + LANES)
                    parts[start : start + 16, half] = top
                    parts[start + size : start + size + 16, half] = rest
        mixed = jnp.dot(
            parts[i * 2 * size : (i + 1) * 2 * size, :], perm, preferred_element_type=F32
        )
        rows_in = 2 * OWN_Y
        for n in range(rows_in):
            block = mixed[n * 8 : n * 8 + 8] + mixed[size + n * 8 : size + n * 8 + 8]
            o0[pl.ds(i * size + n, 8, stride=rows_in), :] = block[:, :LANES]
            o1[pl.ds(i * size + n, 8, stride=rows_in), :] = block[:, LANES:]
        for f in range(8):
            take = slice(i * size + f * rows_in, i * size + (f + 1) * rows_in)
            stage[i, f, :, :LANES] = o0[take]
            stage[i, f, :, LANES:] = o1[take]
        copies.append(
            pltpu.make_async_copy(
                stage.at[i], out.at[:, pl.ds(i * rows_in, rows_in), :], sems.at[i]
            )
        )
        copies[-1].start()
    for copy in copies:
        copy.wait()


def vmem(*shape):
    return pltpu.VMEM(shape, F32)


SPEC = pl.BlockSpec(memory_space=pltpu.VMEM)
CELLS = PY * PX
SHARED = (vmem(PY, PX, LANES),) * 6 + (vmem(CELLS * 2, 8, LANES),) * 3 + (
    vmem(CELLS, 8, LANES),
) * 3
COARSE = (vmem(CX, CY, 8, LANES), vmem(2, CX, 16, LANES))
TABLES = [vmem(PY, PX, LANES)] * 6


def limit(mib):
    return pltpu.CompilerParams(vmem_limit_bytes=mib << 20)


def near_core(*arrays):
    return [pltpu.with_memory_space_constraint(a, pltpu.VMEM) for a in arrays]


def stay_call(labels):
    return pl.pallas_call(
        stay_kernel,
        out_shape=pltpu.VMEM(labels.shape, labels.dtype),
        in_specs=[pl.BlockSpec(memory_space=pltpu.HBM)],
        out_specs=SPEC,
        scratch_shapes=[pltpu.SemaphoreType.DMA(())],
        compiler_params=limit(1),
    )(pltpu.with_memory_space_constraint(labels, pltpu.HBM))


def wave_call(real, imag, angles, picks, after):
    small = pl.BlockSpec(memory_space=pltpu.HBM)
    return pl.pallas_call(
        wave_kernel,
        out_shape=(vmem(CELLS * 2, 8, LANES), vmem(8, LANES)),
        in_specs=[small] * 4 + [SPEC],
        out_specs=(SPEC,) * 2,
        scratch_shapes=[
            pltpu.SMEM(a.shape, a.dtype) for a in (real, imag, angles, picks)
        ]
        + [pltpu.SemaphoreType.DMA((4,))],
        compiler_params=limit(6),
    )(
        *(pltpu.with_memory_space_constraint(a, pltpu.HBM) for a in (real, imag, angles, picks)),
        *near_core(after),
    )


def middle_call(sizes, labels, tab, wave):
    def kernel(*refs):
        middle_kernel(sizes, *refs)

    return pl.pallas_call(
        kernel,
        out_shape=SHARED,
        in_specs=[SPEC] * 3,
        out_specs=(SPEC,) * 12,
        scratch_shapes=TABLES + [vmem(2 * OWN_Y * PX, 2 * LANES)],
        compiler_params=limit(6),
    )(*near_core(labels, tab, wave))


def low_call(sizes, labels, tab, wave, shared):
    def kernel(*refs):
        low_kernel(sizes, *refs)

    return pl.pallas_call(
        kernel,
        out_shape=SHARED + COARSE + (vmem(SEND, 8, LANES),),
        in_specs=[SPEC] * 15,
        out_specs=(SPEC,) * 15,
        input_output_aliases={3 + n: n for n in range(12)},
        scratch_shapes=TABLES + [vmem(LOW * PX, 2 * LANES)],
        compiler_params=limit(6),
    )(*near_core(labels, tab, wave), *shared)


def high_call(sizes, labels, tab, wave, shared):
    def kernel(*refs):
        high_kernel(sizes, *refs)

    results = pl.pallas_call(
        kernel,
        out_shape=SHARED + COARSE + (vmem(SEND, 8, LANES),),
        in_specs=[SPEC] * 18,
        out_specs=(SPEC,) * 15,
        input_output_aliases={3 + n: n for n in range(15)},
        scratch_shapes=TABLES + [vmem(LOW * PX, 2 * LANES)],
        compiler_params=limit(6),
    )(*near_core(labels, tab, wave), *shared)
    return results[:12], results[12:]


POINTS = NI * NJ
HALF = (vmem(POINTS, 8, LANES), vmem(2, NI, 16, LANES)) + (vmem(POINTS, 8, LANES),) * 2


def own_call(shared, c1, ck):
    used = shared[:4] + shared[6:9]
    results = pl.pallas_call(
        own_kernel,
        out_shape=(vmem(OWN_X * OWN_Y, 2, 8, LANES), vmem(4, 8, LANES)) + HALF,
        in_specs=[SPEC] * 9,
        out_specs=(SPEC,) * 6,
        compiler_params=limit(6),
    )(*used, c1, ck)
    return results[:2], results[2:]


def cycle_call(recv, block, half):
    rows = OWN_X * OWN_Y * 8
    results = pl.pallas_call(
        cycle_kernel,
        out_shape=HALF
        + (jax.ShapeDtypeStruct((8, OWN_X * OWN_Y, 2 * LANES), F32),),
        in_specs=[SPEC] * 7,
        out_specs=(SPEC,) * 4 + (pl.BlockSpec(memory_space=pltpu.HBM),),
        input_output_aliases={3 + n: n for n in range(4)},
        scratch_shapes=[vmem(POINTS, 8, LANES)]
        + [pltpu.VMEM((2 * rows, 2 * LANES), jnp.bfloat16)]
        + [vmem(rows, LANES)] * 2
        + [vmem(OWN_X // 2, 8, 2 * OWN_Y, 2 * LANES), pltpu.SemaphoreType.DMA((3,))],
        compiler_params=limit(8),
    )(*near_core(recv), *block, *half)
    return results[4]


def body(labels, permittivity_real, permittivity_imag, angles, angle_pick):
    gx_n = lax.axis_size("gx")
    gy_n = lax.axis_size("gy")
    core = lax.axis_index("gy") % 2
    is_low = core == 0

    def along_x(values, by):
        pairs = []
        for j in range(gy_n):
            step = by if j % 2 == 1 else -by
            for i in range(gx_n):
                if 0 <= i + step < gx_n:
                    pairs.append(((i + step) * gy_n + j, i * gy_n + j))
        return lax.ppermute(values, ("gx", "gy"), pairs)

    def along_y(values, by):
        pairs = [(j, j + by) for j in range(gy_n) if 0 <= j + by < gy_n]
        return lax.ppermute(values, "gy", pairs)

    def core_swap(values):
        return lax.ppermute(values, "gy", [(j, j ^ 1) for j in range(gy_n)])

    other = core_swap(labels)
    labels = stay_call(labels)
    both = jnp.where(
        is_low,
        jnp.concatenate([labels, other], axis=1),
        jnp.concatenate([other, labels], axis=1),
    )
    both = with_layout_constraint(both, Layout((0, 1, 2)))
    far = along_x(jnp.where(is_low, both[2:], both[:4]), 2)
    near = along_x(both, 1)
    near = with_layout_constraint(near, Layout((0, 1, 2)))
    far = with_layout_constraint(far, Layout((0, 1, 2)))
    region = jnp.where(
        is_low,
        jnp.concatenate([far, near, both], axis=0),
        jnp.concatenate([both, near, far], axis=0),
    )
    region = jnp.transpose(region, (1, 0, 2))
    low = along_y(region[2 * OWN_Y - LOW :], 2)
    high = along_y(region[: PY - LOW - 2 * OWN_Y], -2)

    wave, table = wave_call(
        permittivity_real, permittivity_imag, angles, angle_pick, both
    )
    sizes = (OWN_X * gx_n, OWN_Y * gy_n)
    shared = middle_call(sizes, region, table, wave)
    shared = low_call(sizes, low, table, wave, shared)
    shared, (c1, ck, send) = high_call(sizes, high, table, wave, shared)
    recv = core_swap(send)
    block, half = own_call(shared, c1, ck)
    out = cycle_call(recv, block, half)
    return out.reshape(2, 4, OWN_X, OWN_Y, 2 * LANES)


def solution(mesh):
    return jax.shard_map(
        body,
        mesh=mesh,
        in_specs=(P("gx", "gy", None), P(), P(), P(), P()),
        out_specs=P(None, None, "gx", "gy", None),
        check_vma=False,
    )
```
